32 devices in a mesh: clip: 8 (over z, y), frame: 4 (over x, core).
Axes of the slice: x: 2, y: 2, z: 4, core: 2. Of those that a mesh axis runs over, the one named last changes fastest.
Arguments:
- video_tokens: bfloat16 [8, 8, 196, 768], P('clip', 'frame'), may hold values from -6 to 6
- time_gain: bfloat16 [768], P(('clip', 'frame')), may hold values from 0.25 to 1.75
- time_shift: bfloat16 [768], P(('clip', 'frame')), may hold values from -3 to 3
- time_inproj: bfloat16 [768, 2304], P(('clip', 'frame')), may hold values from -0.21875 to 0.21875
- time_inbias: bfloat16 [1536], P(('clip', 'frame')), may hold values from -3 to 3
- time_outproj: bfloat16 [768, 768], P(('clip', 'frame')), may hold values from -0.4375 to 0.4375
- time_outbias: bfloat16 [768], P(('clip', 'frame')), may hold values from -3 to 3
- time_linear: bfloat16 [768, 768], P(('clip', 'frame')), may hold values from -0.21875 to 0.21875
- time_linbias: bfloat16 [768], P(('clip', 'frame')), may hold values from -3 to 3
- space_gain: bfloat16 [768], P(('clip', 'frame')), may hold values from 0.25 to 1.75
- space_shift: bfloat16 [768], P(('clip', 'frame')), may hold values from -3 to 3
- space_inproj: bfloat16 [768, 2304], P(('clip', 'frame')), may hold values from -0.21875 to 0.21875
- space_inbias: bfloat16 [1536], P(('clip', 'frame')), may hold values from -3 to 3
- space_outproj: bfloat16 [768, 768], P(('clip', 'frame')), may hold values from -1.75 to 1.75
- space_outbias: bfloat16 [768], P(('clip', 'frame')), may hold values from -3 to 3
- feed_gain: bfloat16 [768], P(('clip', 'frame')), may hold values from 0.25 to 1.75
- feed_shift: bfloat16 [768], P(('clip', 'frame')), may hold values from -3 to 3
- expand_weight: bfloat16 [768, 3072], P(('clip', 'frame')), may hold values from -0.21875 to 0.21875
- expand_bias: bfloat16 [3072], P(('clip', 'frame')), may hold values from -3 to 3
- reduce_weight: bfloat16 [3072, 768], P(('clip', 'frame')), may hold values from -0.109375 to 0.109375
- reduce_bias: bfloat16 [768], P(('clip', 'frame')), may hold values from -3 to 3
- cotangent: bfloat16 [8, 8, 196, 768], P('clip', 'frame'), may hold values from -6 to 6
Outputs:
- layer_out: bfloat16 [8, 8, 196, 768], P('clip', 'frame')
- input_grad: float32 [8, 8, 196, 768], P('clip', 'frame')
- grad_time_gain: float32 [768], P(('clip', 'frame'))
- grad_time_shift: float32 [768], P(('clip', 'frame'))
- grad_time_inproj: float32 [768, 2304], P(('clip', 'frame'))
- grad_time_inbias: float32 [1536], P(('clip', 'frame'))
- grad_time_outproj: float32 [768, 768], P(('clip', 'frame'))
- grad_time_outbias: float32 [768], P(('clip', 'frame'))
- grad_time_linear: float32 [768, 768], P(('clip', 'frame'))
- grad_time_linbias: float32 [768], P(('clip', 'frame'))
- grad_space_gain: float32 [768], P(('clip', 'frame'))
- grad_space_shift: float32 [768], P(('clip', 'frame'))
- grad_space_inproj: float32 [768, 2304], P(('clip', 'frame'))
- grad_space_inbias: float32 [1536], P(('clip', 'frame'))
- grad_space_outproj: float32 [768, 768], P(('clip', 'frame'))
- grad_space_outbias: float32 [768], P(('clip', 'frame'))
- grad_feed_gain: float32 [768], P(('clip', 'frame'))
- grad_feed_shift: float32 [768], P(('clip', 'frame'))
- grad_expand_weight: float32 [768, 3072], P(('clip', 'frame'))
- grad_expand_bias: float32 [3072], P(('clip', 'frame'))
- grad_reduce_weight: float32 [3072, 768], P(('clip', 'frame'))
- grad_reduce_bias: float32 [768], P(('clip', 'frame'))
The draws below stay inside these ranges and needn't reach their ends.
All inputs are finite; a program needn't handle non-finite values.
Results may differ from the reference program's by a relative error of at most 0.025.
Values may be sent and summed in bfloat16 or wider, within the bound.
A program may use at most 192 MiB of HBM per device.

```python
import jax
import jax.numpy as jnp
from jax import lax

D = 768
HEADS = 12
HEAD_DIM = 64
FF = 3072
FRAMES = 8
PLACES = 196
CLIPS = 8


def strengthened(values, rng, source, target, shards_of, factor):
    owner, partner = [(jnp.arange(values.shape[position]) // (values.shape[position] // shards_of)).reshape([-1 if axis == position else 1 for axis in range(values.ndim)]) for position in (source, target)]
    chosen = jax.random.permutation(rng, shards_of)[partner]
    strong = (owner == chosen) | (owner == (partner + shards_of // 2) % shards_of)
    return jnp.where(strong, factor * values, values)


def levels(key, shape, shards, smallest, high):
    factor_of = 1.0
    for dim, blocks in shards:
        steps = jax.random.uniform(jax.random.fold_in(jax.random.fold_in(key, 6), dim), (blocks,), jnp.float32, smallest / len(shards), high / len(shards))
        factor_of = factor_of * jnp.repeat(jnp.exp(steps), shape[dim] // blocks).reshape((-1,) + (1,) * (len(shape) - 1 - dim))
    return factor_of


def noise(rng, dims, width, most, shards=(), held_as=jnp.bfloat16):
    values = jax.random.normal(rng, dims, jnp.float32) * width
    if len(shards) > 0:
        values = levels(rng, dims, shards, -0.22, 0.18) * values
    return jnp.clip(values, min=-most, max=most).astype(held_as)


def heavy_noise(stream_key, extent, deviation, bound, cuts, heavy, kind=jnp.bfloat16):
    drawn = deviation * jax.random.normal(stream_key, extent, jnp.float32)
    if cuts:
        drawn = drawn * levels(stream_key, extent, cuts, -0.22, 0.18)
    return jnp.clip(strengthened(drawn, jax.random.fold_in(stream_key, 3), *heavy), -bound, bound).astype(kind)


def setup_inputs(seed: int = 0) -> dict:
    keys = jax.random.split(jax.random.key(seed), 23)
    return {
        "video_tokens": heavy_noise(keys[0], (CLIPS, FRAMES, PLACES, D), 1.0, 6.0, ((0, 8), (1, 4)), (0, 3, 8, 2.0)),
        "time_gain": jnp.clip(1.0 + 0.15 * jax.random.normal(keys[1], (D,), jnp.float32), 0.25, 1.75).astype(jnp.bfloat16),
        "time_shift": noise(keys[2], (D,), 0.5, 3.0, ((0, 32),)),
        "time_inproj": noise(keys[3], (D, 3 * D), D ** -0.5, 0.21875, ((0, 32),)),
        "time_inbias": noise(keys[4], (2 * D,), 0.5, 3.0, ((0, 32),)),
        "time_outproj": noise(keys[5], (D, D), (D // 4) ** -0.5, 0.4375, ((0, 32),)),
        "time_outbias": noise(keys[6], (D,), 0.5, 3.0, ((0, 32),)),
        "time_linear": noise(keys[7], (D, D), D ** -0.5, 0.21875, ((0, 32),)),
        "time_linbias": noise(keys[8], (D,), 0.5, 3.0, ((0, 32),)),
        "space_gain": jnp.clip(1.0 + 0.15 * jax.random.normal(keys[9], (D,), jnp.float32), 0.25, 1.75).astype(jnp.bfloat16),
        "space_shift": noise(keys[10], (D,), 0.5, 3.0, ((0, 32),)),
        "space_inproj": noise(keys[11], (D, 3 * D), D ** -0.5, 0.21875, ((0, 32),)),
        "space_inbias": noise(keys[12], (2 * D,), 0.5, 3.0, ((0, 32),)),
        "space_outproj": noise(keys[13], (D, D), (D // 64) ** -0.5, 1.75, ((0, 32),)),
        "space_outbias": noise(keys[14], (D,), 0.5, 3.0, ((0, 32),)),
        "feed_gain": jnp.clip(1.0 + 0.15 * jax.random.normal(keys[15], (D,), jnp.float32), 0.25, 1.75).astype(jnp.bfloat16),
        "feed_shift": noise(keys[16], (D,), 0.5, 3.0, ((0, 32),)),
        "expand_weight": noise(keys[17], (D, FF), D ** -0.5, 0.21875, ((0, 32),)),
        "expand_bias": noise(keys[18], (FF,), 0.5, 3.0, ((0, 32),)),
        "reduce_weight": noise(keys[19], (FF, D), FF ** -0.5, 0.109375, ((0, 32),)),
        "reduce_bias": noise(keys[20], (D,), 0.5, 3.0, ((0, 32),)),
        "cotangent": heavy_noise(keys[21], (CLIPS, FRAMES, PLACES, D), 1.0, 6.0, ((0, 8), (1, 4)), (0, 3, 8, 2.0)),
    }


norm_eps = 1e-06
space_forms = ('cfqhd,cfkhd->cfhqk', 'cfhqk,cfkhd->cfqhd')
time_forms = ('cqphd,ckphd->cphqk', 'cphqk,ckphd->cqphd')

@jax.custom_vjp
def low(v):
    return lax.optimization_barrier(v.astype(jnp.bfloat16)).astype(jnp.float32)

@jax.custom_vjp
def low_back(v):
    return v

def low_keep(v):
    return (low(v), None)

def low_pass(kept, grad):
    return (grad,)

def back_keep(v):
    return (v, None)

def back_low(kept, grad):
    return (low(grad),)
low.defvjp(low_keep, low_pass)
low_back.defvjp(back_keep, back_low)

def exact_dot(left_side, right_side):
    return jnp.dot(left_side, right_side, precision=lax.Precision.HIGHEST, preferred_element_type=jnp.float32)

def layer_norm(values, gain_vec, shift_vec):
    center = values - lax.optimization_barrier(jnp.mean(values, axis=-1, keepdims=True))
    spread = lax.optimization_barrier(jnp.mean(center * center, axis=-1, keepdims=True))
    return center * lax.rsqrt(spread + norm_eps) * gain_vec + shift_vec

def gelu_exact(values):
    return jax.nn.gelu(values, approximate=False)

def attention(normed, inproj, inbias, form_set):
    lowered = low(normed)
    part_width = inbias.shape[0] // 2
    bias_full = jnp.concatenate([inbias[:part_width], jnp.zeros((part_width,), jnp.float32), inbias[part_width:]])
    packed = low(low_back(exact_dot(lowered, inproj) + bias_full))
    pieces = packed.reshape(packed.shape[:-1] + (3, HEADS, HEAD_DIM))
    queries = pieces[..., 0, :, :]
    keys_part = pieces[..., 1, :, :]
    values_part = pieces[..., 2, :, :]
    scores = jnp.einsum(form_set[0], queries, keys_part, precision=lax.Precision.HIGHEST) * HEAD_DIM ** (-0.5)
    scores = low_back(scores)
    softmax_out = jax.nn.softmax(scores, axis=-1)
    attended = jnp.einsum(form_set[1], low(softmax_out), values_part, precision=lax.Precision.HIGHEST)
    attended = attended.reshape(attended.shape[:-2] + (D,))
    return low(low_back(attended))

def forward(params, clip_block):
    time_gain, time_shift, time_inproj, time_inbias, time_outproj, time_outbias, time_linear, time_linbias, space_gain, space_shift, space_inproj, space_inbias, space_outproj, space_outbias, feed_gain, feed_shift, expand_weight, expand_bias, reduce_weight, reduce_bias = params
    time_input = low_back(clip_block)
    time_normed = layer_norm(time_input, time_gain, time_shift)
    time_attended = attention(time_normed, time_inproj, time_inbias, time_forms)
    time_first = low(low_back(exact_dot(time_attended, time_outproj) + time_outbias))
    time_branch = low(low_back(exact_dot(time_first, time_linear) + time_linbias))
    after_time = clip_block + time_branch
    space_normed = layer_norm(after_time, space_gain, space_shift)
    space_attended = attention(space_normed, space_inproj, space_inbias, space_forms)
    after_space = after_time + low_back(exact_dot(space_attended, space_outproj) + space_outbias)
    feed_normed = low(layer_norm(after_space, feed_gain, feed_shift))
    hidden = low_back(exact_dot(feed_normed, expand_weight) + expand_bias)
    activated = low(gelu_exact(hidden))
    return after_space + low_back(exact_dot(activated, reduce_weight) + reduce_bias)

def reference(video_tokens, time_gain, time_shift, time_inproj, time_inbias, time_outproj, time_outbias, time_linear, time_linbias, space_gain, space_shift, space_inproj, space_inbias, space_outproj, space_outbias, feed_gain, feed_shift, expand_weight, expand_bias, reduce_weight, reduce_bias, cotangent):
    params = tuple((item.astype(jnp.float32) for item in (time_gain, time_shift, time_inproj, time_inbias, time_outproj, time_outbias, time_linear, time_linbias, space_gain, space_shift, space_inproj, space_inbias, space_outproj, space_outbias, feed_gain, feed_shift, expand_weight, expand_bias, reduce_weight, reduce_bias)))
    group_size = 2 if CLIPS % 2 == 0 else 1
    block_shape = (CLIPS // group_size, group_size, FRAMES, PLACES, D)
    inputs = video_tokens.astype(jnp.float32).reshape(block_shape)
    cotangents = cotangent.astype(jnp.float32).reshape(block_shape)

    def scan_step(totals, inputs_pair):
        clip_block, grad_out = inputs_pair
        result, pullback = jax.vjp(forward, params, clip_block)
        grad_params, grad_block = pullback(grad_out)
        totals = jax.tree.map(jnp.add, totals, grad_params)
        return (totals, (result.astype(jnp.bfloat16), grad_block))
    start = jax.tree.map(jnp.zeros_like, params)
    totals, (outputs, gradients) = lax.scan(scan_step, start, (inputs, cotangents))
    whole_shape = (CLIPS, FRAMES, PLACES, D)
    return (outputs.reshape(whole_shape), gradients.reshape(whole_shape), totals[0], totals[1], totals[2], totals[3], totals[4], totals[5], totals[6], totals[7], totals[8], totals[9], totals[10], totals[11], totals[12], totals[13], totals[14], totals[15], totals[16], totals[17], totals[18], totals[19])
```

```python
import functools

import jax
import jax.numpy as jnp
from jax import lax
from jax.experimental import pallas as pl
from jax.experimental.pallas import tpu as pltpu
from jax.sharding import PartitionSpec as P

HEADS = 12


norm_eps = 1e-06
space_forms = ("cfqhd,cfkhd->cfhqk", "cfhqk,cfkhd->cfqhd", "cfhqk,cfqhd->cfkhd")
time_forms = ("cqphd,ckphd->cphqk", "cphqk,ckphd->cqphd", "cphqk,cqphd->ckphd")


def layer_norm(values, gain_vec, shift_vec):
    center = values - jnp.mean(values, axis=-1, keepdims=True)
    spread = jnp.mean(center * center, axis=-1, keepdims=True)
    return center * lax.rsqrt(spread + norm_eps) * gain_vec + shift_vec


def gelu_exact(values):
    return jax.nn.gelu(values, approximate=False)


def project(lowered, weight, bias_vec):
    return jnp.dot(lowered, weight, preferred_element_type=jnp.float32) + bias_vec.astype(
        jnp.float32
    )


def back_dot(gradient, weight):
    return lax.dot_general(
        gradient,
        weight,
        (((gradient.ndim - 1,), (1,)), ((), ())),
        preferred_element_type=jnp.float32,
    )


def weight_grad(left_side, right_side):
    return jnp.einsum(
        "ti,to->io",
        left_side.reshape(-1, left_side.shape[-1]),
        right_side.reshape(-1, right_side.shape[-1]),
        preferred_element_type=jnp.float32,
    )


def bias_grad(gradient):
    return jnp.sum(gradient.reshape(-1, gradient.shape[-1]), axis=0, dtype=jnp.float32)


def flatten_heads(tensor):
    return tensor.reshape(tensor.shape[:-2] + (-1,))


def stack_rows(terms, groups):
    return tuple(
        (item.reshape((groups, item.shape[0] // groups) + item.shape[1:]) for item in terms)
    )


def fold_rows(received):
    return tuple((jnp.sum(item, axis=0) for item in received))


def attend(queries, keys_part, values_part, form_set):
    scale = queries.shape[-1] ** (-0.5)
    scores = jnp.einsum(form_set[0], queries, keys_part, preferred_element_type=jnp.float32) * scale
    row_max = jnp.max(scores, axis=-1, keepdims=True)
    row_total = jnp.sum(jnp.exp(scores - row_max), axis=-1, keepdims=True)
    log_total = row_max + jnp.log(row_total)
    softmax_low = jnp.exp(scores - log_total).astype(jnp.bfloat16)
    attended = jnp.einsum(form_set[1], softmax_low, values_part, preferred_element_type=jnp.float32)
    return (attended, log_total)


def attend_back(queries, keys_part, values_part, log_total, d_attended, form_set):
    scale = queries.shape[-1] ** (-0.5)
    scores = jnp.einsum(form_set[0], queries, keys_part, preferred_element_type=jnp.float32) * scale
    softmax_out = jnp.exp(scores - log_total)
    d_values = jnp.einsum(
        form_set[2],
        softmax_out.astype(jnp.bfloat16),
        d_attended,
        preferred_element_type=jnp.float32,
    )
    d_softmax = jnp.einsum(form_set[0], d_attended, values_part, preferred_element_type=jnp.float32)
    inner = jnp.sum(d_softmax * softmax_out, axis=-1, keepdims=True)
    d_scores = (softmax_out * (d_softmax - inner)).astype(jnp.bfloat16)
    d_queries = (
        jnp.einsum(form_set[1], d_scores, keys_part, preferred_element_type=jnp.float32) * scale
    )
    d_keys = jnp.einsum(form_set[2], d_scores, queries, preferred_element_type=jnp.float32) * scale
    return (d_queries, d_keys, d_values)


def attention_forward(normed, inproj, inbias, form_set):
    lowered = normed.astype(jnp.bfloat16)
    part_width = inbias.shape[0] // 2
    bias_full = jnp.concatenate(
        [inbias[:part_width], jnp.zeros((part_width,), inbias.dtype), inbias[part_width:]]
    )
    packed = project(lowered, inproj, bias_full).astype(jnp.bfloat16)
    pieces = packed.reshape(packed.shape[:-1] + (3, HEADS, packed.shape[-1] // (3 * HEADS)))
    queries = pieces[..., 0, :, :]
    keys_part = pieces[..., 1, :, :]
    values_part = pieces[..., 2, :, :]
    attended, log_total = attend(queries, keys_part, values_part, form_set)
    return (
        lowered,
        (queries, keys_part, values_part, log_total),
        flatten_heads(attended).astype(jnp.bfloat16),
    )


def attention_backward(lowered, kept_state, d_attended_flat, inproj, form_set):
    queries, keys_part, values_part, log_total = kept_state
    d_attended = d_attended_flat.reshape(queries.shape)
    d_queries, d_keys, d_values = attend_back(
        queries, keys_part, values_part, log_total, d_attended, form_set
    )
    d_packed = jnp.concatenate(
        [flatten_heads(d_queries), flatten_heads(d_keys), flatten_heads(d_values)], axis=-1
    ).astype(jnp.bfloat16)
    grad_proj = weight_grad(lowered, d_packed)
    part_width = d_packed.shape[-1] // 3
    summed = bias_grad(d_packed)
    grad_bias = jnp.concatenate([summed[:part_width], summed[2 * part_width :]])
    return (back_dot(d_packed, inproj), grad_proj, grad_bias)


MESH = pl.DeviceIdType.MESH
TILE_ROWS = 8
SMALL_TILE = (8, 256)


def remote(source, target, send, recv, device):
    return pltpu.make_async_remote_copy(
        src_ref=source,
        dst_ref=target,
        send_sem=send,
        recv_sem=recv,
        device_id=device,
        device_id_type=MESH,
    )


def place(split):
    nz, ny, nx, nc = split
    clip, frame = lax.axis_index("clip"), lax.axis_index("frame")
    z, y, x, c = clip // ny, clip % ny, frame // nc, frame % nc

    def mesh_at(z, y, x, c):
        return (z * ny + y, x * nc + c)

    row = [mesh_at((z + step) % nz, y, x, c) for step in range(1, nz)]
    beside = (mesh_at(z, y, 1 - x, c), mesh_at(z, 1 - y, x, c), mesh_at(z, y, x, 1 - c))
    return (z, y, x, c), row, beside


def greet(devices):
    barrier = pltpu.get_barrier_semaphore()
    for device in devices:
        pl.semaphore_signal(barrier, inc=1, device_id=device, device_id_type=MESH)
    pl.semaphore_wait(barrier, len(devices))


def gather_kernel(split, count, *refs):
    shards, full = refs[:count], refs[count : 2 * count]
    row_send, row_recv, side_send, side_recv, core_send, core_recv, own_sem = refs[2 * count :]
    (z, y, x, c), row, (across_x, across_y, twin) = place(split)
    greet(row + [across_x, across_y, twin])
    started, first, second, third, core = [], {}, {}, {}, {}

    def launch(copy):
        copy.start()
        started.append(copy)
        return copy

    def to_twin(i, step, block):
        return launch(remote(block, block, core_send.at[i, step], core_recv.at[i, step], twin))

    def spread(i):
        own = full[i].at[z, y, x, c]
        first[i] = [
            launch(remote(shards[i], own, row_send.at[i, k], row_recv.at[i, k], device))
            for k, device in enumerate(row)
        ]
        keep = pltpu.make_async_copy(shards[i], own, own_sem.at[i])
        keep.start()
        first[i].append(keep)

    def sideways(i):
        for copy in first[i][:-1]:
            copy.wait_recv()
        first[i][-1].wait()
        block = full[i].at[:, y, x, c]
        second[i] = [
            launch(remote(block, block, side_send.at[i, k], side_recv.at[i, k], device))
            for k, device in enumerate((across_x, across_y))
        ]
        core[i] = [to_twin(i, 0, block)]

    def relay(i):
        half = shards[i].shape[-1] // 2
        second[i][0].wait_recv()
        part = full[i].at[:, y, 1 - x, c, :, pl.ds(0, half)]
        third[i] = [launch(remote(part, part, side_send.at[i, 2], side_recv.at[i, 2], across_y))]
        core[i].append(to_twin(i, 1, full[i].at[:, y, 1 - x, c]))
        second[i][1].wait_recv()
        part = full[i].at[:, 1 - y, x, c, :, pl.ds(half, half)]
        third[i].append(
            launch(remote(part, part, side_send.at[i, 3], side_recv.at[i, 3], across_x))
        )
        core[i].append(to_twin(i, 2, full[i].at[:, 1 - y, x, c]))

    def finish(i):
        for copy in third[i]:
            copy.wait_recv()
        core[i].append(to_twin(i, 3, full[i].at[:, 1 - y, 1 - x, c]))

    def receive(i):
        for copy in core[i]:
            copy.wait_recv()

    ahead = 2
    for i in range(min(ahead, count)):
        spread(i)
    for step in range(count + 3):
        for lag, act in enumerate((sideways, relay, finish, receive)):
            if 0 <= step - lag < count:
                act(step - lag)
            if lag == 0 and step + ahead < count:
                spread(step + ahead)
    for copy in started:
        copy.wait_send()


def gather_shards(split, shards):
    count = len(shards)
    sem = pltpu.SemaphoreType.DMA
    full = pl.pallas_call(
        functools.partial(gather_kernel, split, count),
        out_shape=[jax.ShapeDtypeStruct(split + item.shape, item.dtype) for item in shards],
        in_specs=[pl.BlockSpec(memory_space=pl.ANY)] * count,
        out_specs=[pl.BlockSpec(memory_space=pl.ANY)] * count,
        scratch_shapes=[sem((count, split[0] - 1))] * 2 + [sem((count, 4))] * 4 + [sem((count,))],
        compiler_params=pltpu.CompilerParams(collective_id=0, has_side_effects=True),
        name="gather_shards",
    )(*shards)
    return [item.reshape((-1, item.shape[-1])) for item in full]


def sum_kernel(split, count, *refs):
    groups = [refs[k * count : (k + 1) * count] for k in range(8)]
    mine, outs, held, low_half, high_half, from_x, from_y, from_row = groups
    core_send, core_recv, side_send, side_recv, row_send, row_recv = refs[8 * count :]
    (z, y, x, c), row, (across_x, across_y, twin) = place(split)
    greet(row + [across_x, across_y, twin])
    depth = split[0]
    started, core, diagonal, side, last = [], {}, {}, {}, {}

    def launch(copy):
        copy.start()
        started.append(copy)
        return copy

    def each_row(act):
        def step(k, carry):
            act(k)
            return carry

        lax.fori_loop(0, depth, step, 0)

    def swap(i):
        block = mine[i].at[:, :, :, 1 - c]
        core[i] = launch(remote(block, held[i], core_send.at[i], core_recv.at[i], twin))

    def fold_core(i):
        core[i].wait_recv()
        half = mine[i].shape[-1] // 2

        def fold(yy, xx):
            def act(k):
                held[i][k, yy, xx] = held[i][k, yy, xx] + mine[i][k, yy, xx, c]

            each_row(act)

        fold(1 - y, 1 - x)
        low = held[i].at[:, 1 - y, 1 - x, :, pl.ds(0, half)]
        high = held[i].at[:, 1 - y, 1 - x, :, pl.ds(half, half)]
        diagonal[i] = [
            launch(remote(low, low_half[i], side_send.at[i, 0], side_recv.at[i, 0], across_x)),
            launch(remote(high, high_half[i], side_send.at[i, 1], side_recv.at[i, 1], across_y)),
        ]
        fold(1 - y, x)
        fold(y, 1 - x)
        fold(y, x)

    def fold_diagonal(i):
        half = mine[i].shape[-1] // 2
        diagonal[i][0].wait_recv()

        def act_low(k):
            held[i][k, 1 - y, x, :, :half] = held[i][k, 1 - y, x, :, :half] + low_half[i][k]

        each_row(act_low)
        block = held[i].at[:, 1 - y, x]
        side[i] = [
            launch(remote(block, from_y[i], side_send.at[i, 2], side_recv.at[i, 2], across_y))
        ]
        diagonal[i][1].wait_recv()

        def act_high(k):
            held[i][k, y, 1 - x, :, half:] = held[i][k, y, 1 - x, :, half:] + high_half[i][k]

        each_row(act_high)
        block = held[i].at[:, y, 1 - x]
        side[i].append(
            launch(remote(block, from_x[i], side_send.at[i, 3], side_recv.at[i, 3], across_x))
        )

    def fold_side(i):
        for copy in side[i]:
            copy.wait_recv()

        def act(k):
            total = held[i][k, y, x].astype(jnp.float32) + from_x[i][k].astype(jnp.float32)
            held[i][k, y, x] = (total + from_y[i][k].astype(jnp.float32)).astype(jnp.bfloat16)

        each_row(act)
        last[i] = [
            launch(
                remote(
                    held[i].at[(z + k + 1) % depth, y, x],
                    from_row[i].at[k],
                    row_send.at[i, k],
                    row_recv.at[i, k],
                    device,
                )
            )
            for k, device in enumerate(row)
        ]

    def fold_row(i):
        for copy in last[i]:
            copy.wait_recv()
        total = held[i][z, y, x].astype(jnp.float32)
        for k in range(depth - 1):
            total = total + from_row[i][k].astype(jnp.float32)
        outs[i][...] = total

    for i in range(count):
        swap(i)
    for step in range(count + 3):
        for lag, act in enumerate((fold_core, fold_diagonal, fold_side, fold_row)):
            if 0 <= step - lag < count:
                act(step - lag)
    for copy in started:
        copy.wait_send()


def sum_shards(split, terms):
    count = len(terms)
    nz, ny, nx, _ = split
    blocks = [item.reshape(split + (-1, item.shape[-1])) for item in terms]
    shapes = [item.shape[4:] for item in blocks]
    low = jnp.bfloat16
    sem = pltpu.SemaphoreType.DMA
    scratch = [pltpu.VMEM((nz, ny, nx) + s, low) for s in shapes]
    scratch += [pltpu.VMEM((nz, s[0], s[1] // 2), low) for s in shapes] * 2
    scratch += [pltpu.VMEM((nz,) + s, low) for s in shapes] * 2
    scratch += [pltpu.VMEM((nz - 1,) + s, low) for s in shapes]
    scratch += [sem((count,))] * 2 + [sem((count, 4))] * 2 + [sem((count, nz - 1))] * 2
    return pl.pallas_call(
        functools.partial(sum_kernel, split, count),
        out_shape=[jax.ShapeDtypeStruct(s, jnp.float32) for s in shapes],
        in_specs=[pl.BlockSpec(memory_space=pltpu.VMEM)] * count,
        out_specs=[pl.BlockSpec(memory_space=pltpu.VMEM)] * count,
        scratch_shapes=scratch,
        compiler_params=pltpu.CompilerParams(
            collective_id=1, has_side_effects=True, vmem_limit_bytes=60 << 20
        ),
        name="sum_shards",
    )(*blocks)


def inner_split(rows):
    clips, frames = lax.axis_size("clip"), lax.axis_size("frame")
    if frames == 4 and clips % 2 == 0 and clips > 2 and rows % TILE_ROWS == 0:
        return (clips // 2, 2, 2, 2)
    return None


def pack_small(vectors, groups):
    rows = jnp.concatenate([item.reshape(groups, -1) for item in vectors], axis=1)
    size = SMALL_TILE[0] * SMALL_TILE[1]
    rows = jnp.pad(rows, ((0, 0), (0, size - rows.shape[1])))
    return rows.reshape((groups * SMALL_TILE[0], SMALL_TILE[1]))


def unpack_small(packed, widths):
    rows = packed.reshape(-1, SMALL_TILE[0] * SMALL_TILE[1])
    pieces, at = [], 0
    for width in widths:
        pieces.append(rows[:, at : at + width].reshape(-1))
        at += width
    return pieces


def gather_all(split, params):
    if split is None:
        return [lax.all_gather(item, ("clip", "frame"), axis=0, tiled=True) for item in params]
    wide = [k for k, item in enumerate(params) if item.ndim == 2]
    thin = [k for k, item in enumerate(params) if item.ndim == 1]
    full = gather_shards(split, [pack_small([params[k] for k in thin], 1)] + [params[k] for k in wide])
    vectors = unpack_small(full[0], [params[k].shape[0] for k in thin])
    result = dict(zip(wide, full[1:])) | dict(zip(thin, vectors))
    return [result[k] for k in range(len(params))]


def sum_all(split, terms):
    if split is None:
        groups = lax.axis_size("clip")
        received = [
            lax.all_to_all(
                item.astype(jnp.bfloat16), "clip", split_axis=0, concat_axis=0, tiled=True
            ).astype(jnp.float32)
            for item in stack_rows(terms, groups)
        ]
        return [
            lax.psum_scatter(
                item.astype(jnp.bfloat16), "frame", scatter_dimension=0, tiled=True
            ).astype(jnp.float32)
            for item in fold_rows(received)
        ]
    devices = split[0] * split[1] * split[2] * split[3]
    wide = [k for k, item in enumerate(terms) if item.ndim == 2]
    thin = [k for k, item in enumerate(terms) if item.ndim == 1]
    low = [item.astype(jnp.bfloat16) for item in terms]
    order = wide[::-1]
    sums = sum_shards(split, [low[k] for k in order] + [pack_small([low[k] for k in thin], devices)])
    vectors = unpack_small(sums[-1], [terms[k].shape[0] // devices for k in thin])
    result = dict(zip(order, sums[:-1])) | dict(zip(thin, vectors))
    return [result[k] for k in range(len(terms))]


def on_device(
    video_tokens,
    time_gain,
    time_shift,
    time_inproj,
    time_inbias,
    time_outproj,
    time_outbias,
    time_linear,
    time_linbias,
    space_gain,
    space_shift,
    space_inproj,
    space_inbias,
    space_outproj,
    space_outbias,
    feed_gain,
    feed_shift,
    expand_weight,
    expand_bias,
    reduce_weight,
    reduce_bias,
    cotangent,
):
    split = inner_split(time_gain.shape[0])
    gathered = gather_all(
        split,
        [
            time_gain,
            time_shift,
            time_inproj,
            time_inbias,
            time_outproj,
            time_outbias,
            time_linear,
            time_linbias,
            space_gain,
            space_shift,
            space_inproj,
            space_inbias,
            space_outproj,
            space_outbias,
            feed_gain,
            feed_shift,
            expand_weight,
            expand_bias,
            reduce_weight,
            reduce_bias,
        ],
    )
    (
        full_time_gain,
        full_time_shift,
        full_time_inproj,
        full_time_inbias,
        full_time_outproj,
        full_time_outbias,
        full_time_linear,
        full_time_linbias,
        full_space_gain,
        full_space_shift,
        full_space_inproj,
        full_space_inbias,
        full_space_outproj,
        full_space_outbias,
        full_feed_gain,
        full_feed_shift,
        full_expand_weight,
        full_expand_bias,
        full_reduce_weight,
        full_reduce_bias,
    ) = gathered
    placed = lax.all_to_all(video_tokens, "frame", split_axis=2, concat_axis=1, tiled=True)
    time_normed, time_pullback = jax.vjp(
        layer_norm,
        placed.astype(jnp.float32),
        full_time_gain.astype(jnp.float32),
        full_time_shift.astype(jnp.float32),
    )
    time_lowered, time_kept, time_attended = attention_forward(
        time_normed, full_time_inproj, full_time_inbias, time_forms
    )
    time_first = project(time_attended, full_time_outproj, full_time_outbias).astype(jnp.bfloat16)
    time_branch = project(time_first, full_time_linear, full_time_linbias).astype(jnp.bfloat16)
    returned = lax.all_to_all(time_branch, "frame", split_axis=1, concat_axis=2, tiled=True)
    after_time = video_tokens.astype(jnp.float32) + returned.astype(jnp.float32)
    space_normed, space_pullback = jax.vjp(
        layer_norm,
        after_time,
        full_space_gain.astype(jnp.float32),
        full_space_shift.astype(jnp.float32),
    )
    space_lowered, space_kept, space_attended = attention_forward(
        space_normed, full_space_inproj, full_space_inbias, space_forms
    )
    after_space = after_time + project(space_attended, full_space_outproj, full_space_outbias)
    feed_normed, feed_pullback = jax.vjp(
        layer_norm,
        after_space,
        full_feed_gain.astype(jnp.float32),
        full_feed_shift.astype(jnp.float32),
    )
    feed_lowered = feed_normed.astype(jnp.bfloat16)
    hidden = project(feed_lowered, full_expand_weight, full_expand_bias)
    activated, gelu_pullback = jax.vjp(gelu_exact, hidden)
    activated_low = activated.astype(jnp.bfloat16)
    layer_out = (after_space + project(activated_low, full_reduce_weight, full_reduce_bias)).astype(
        jnp.bfloat16
    )
    grad_out = cotangent.astype(jnp.float32)
    g_reduce_weight = weight_grad(activated_low, cotangent)
    g_reduce_bias = bias_grad(cotangent)
    (d_hidden,) = gelu_pullback(back_dot(cotangent, full_reduce_weight))
    d_hidden_low = d_hidden.astype(jnp.bfloat16)
    g_expand_weight = weight_grad(feed_lowered, d_hidden_low)
    g_expand_bias = bias_grad(d_hidden_low)
    d_feed_in, g_feed_gain, g_feed_shift = feed_pullback(back_dot(d_hidden_low, full_expand_weight))
    d_space = grad_out + d_feed_in
    feed_terms = (
        g_feed_gain,
        g_feed_shift,
        g_expand_weight,
        g_expand_bias,
        g_reduce_weight,
        g_reduce_bias,
    )
    d_space_low = d_space.astype(jnp.bfloat16)
    g_space_outproj = weight_grad(space_attended, d_space_low)
    g_space_outbias = bias_grad(d_space_low)
    d_space_att = back_dot(d_space_low, full_space_outproj).astype(jnp.bfloat16)
    d_space_norm, g_space_inproj, g_space_inbias = attention_backward(
        space_lowered, space_kept, d_space_att, full_space_inproj, space_forms
    )
    d_space_in, g_space_gain, g_space_shift = space_pullback(d_space_norm)
    d_time = d_space + d_space_in
    space_terms = (
        g_space_gain,
        g_space_shift,
        g_space_inproj,
        g_space_inbias,
        g_space_outproj,
        g_space_outbias,
    )
    d_placed = lax.all_to_all(
        d_time.astype(jnp.bfloat16), "frame", split_axis=2, concat_axis=1, tiled=True
    )
    g_time_linear = weight_grad(time_first, d_placed)
    g_time_linbias = bias_grad(d_placed)
    d_first = back_dot(d_placed, full_time_linear).astype(jnp.bfloat16)
    g_time_outproj = weight_grad(time_attended, d_first)
    g_time_outbias = bias_grad(d_first)
    d_time_att = back_dot(d_first, full_time_outproj).astype(jnp.bfloat16)
    d_time_norm, g_time_inproj, g_time_inbias = attention_backward(
        time_lowered, time_kept, d_time_att, full_time_inproj, time_forms
    )
    d_time_in, g_time_gain, g_time_shift = time_pullback(d_time_norm)
    d_returned = lax.all_to_all(
        d_time_in.astype(jnp.bfloat16), "frame", split_axis=1, concat_axis=2, tiled=True
    )
    input_grad = d_time + d_returned.astype(jnp.float32)
    time_terms = (
        g_time_gain,
        g_time_shift,
        g_time_inproj,
        g_time_inbias,
        g_time_outproj,
        g_time_outbias,
        g_time_linear,
        g_time_linbias,
    )
    summed = sum_all(split, time_terms + space_terms + feed_terms)
    return (layer_out, input_grad) + tuple(summed)


def solution(mesh):
    return jax.shard_map(
        on_device,
        mesh=mesh,
        in_specs=(
            P("clip", "frame", None, None),
            P(("clip", "frame")),
            P(("clip", "frame")),
            P(("clip", "frame"), None),
            P(("clip", "frame")),
            P(("clip", "frame"), None),
            P(("clip", "frame")),
            P(("clip", "frame"), None),
            P(("clip", "frame")),
            P(("clip", "frame")),
            P(("clip", "frame")),
            P(("clip", "frame"), None),
            P(("clip", "frame")),
            P(("clip", "frame"), None),
            P(("clip", "frame")),
            P(("clip", "frame")),
            P(("clip", "frame")),
            P(("clip", "frame"), None),
            P(("clip", "frame")),
            P(("clip", "frame"), None),
            P(("clip", "frame")),
            P("clip", "frame", None, None),
        ),
        out_specs=(
            P("clip", "frame", None, None),
            P("clip", "frame", None, None),
            P(("clip", "frame")),
            P(("clip", "frame")),
            P(("clip", "frame"), None),
            P(("clip", "frame")),
            P(("clip", "frame"), None),
            P(("clip", "frame")),
            P(("clip", "frame"), None),
            P(("clip", "frame")),
            P(("clip", "frame")),
            P(("clip", "frame")),
            P(("clip", "frame"), None),
            P(("clip", "frame")),
            P(("clip", "frame"), None),
            P(("clip", "frame")),
            P(("clip", "frame")),
            P(("clip", "frame")),
            P(("clip", "frame"), None),
            P(("clip", "frame")),
            P(("clip", "frame"), None),
            P(("clip", "frame")),
        ),
        check_vma=False,
    )
```

```python
import functools

import jax
import jax.numpy as jnp
from jax import lax
from jax.experimental import pallas as pl
from jax.experimental.pallas import tpu as pltpu
from jax.sharding import PartitionSpec as P

LOW = jnp.bfloat16
WIDE = jnp.float32
HEADS = 12
norm_eps = 1e-06
LANES = 128
TILE = 256
T_GAIN, T_SHIFT, T_OUTB, T_LINB, S_GAIN, S_SHIFT, S_OUTB, F_GAIN, F_SHIFT, R_BIAS, T_INB, S_INB, E_BIAS = 0, 1, 2, 3, 4, 5, 6, 7, 8, 9, 10, 12, 14


def dot(a, b):
    return lax.dot_general(a, b, (((1,), (0,)), ((), ())), preferred_element_type=WIDE)


def dot_nt(a, b):
    return lax.dot_general(a, b, (((1,), (1,)), ((), ())), preferred_element_type=WIDE)


def each(count, act):
    def step(k, carry):
        act(k)
        return carry

    lax.fori_loop(0, count, step, 0)


def tiles(k, size=TILE):
    return pl.ds(pl.multiple_of(k * size, size), size)


def columns(w_ref, cut):
    block = w_ref[:, :, cut]
    return block.reshape((block.shape[0] * block.shape[1], block.shape[2]))


def normal(x):
    center = x - jnp.mean(x, axis=-1, keepdims=True)
    inverse = lax.rsqrt(jnp.mean(center * center, axis=-1, keepdims=True) + norm_eps)
    return center * inverse, inverse


def norm_stage(x_ref, vec, gain_row, a_ref, block):
    gain, shift = vec[gain_row : gain_row + 1, :], vec[gain_row + 1 : gain_row + 2, :]

    def act(k):
        rows = tiles(k, block)
        unit, _ = normal(x_ref[rows, :].astype(WIDE))
        a_ref[rows, :] = (unit * gain + shift).astype(LOW)

    each(x_ref.shape[0] // block, act)


def norm_back_stage(x_ref, vec, gain_row, da_ref, sums, block, store):
    gain = vec[gain_row : gain_row + 1, :]
    width = x_ref.shape[1]

    def step(k, carry):
        rows = tiles(k, block)
        unit, inverse = normal(x_ref[rows, :].astype(WIDE))
        da = da_ref[rows, :]
        e = da * gain
        dv = inverse * (
            e
            - jnp.mean(e, axis=-1, keepdims=True)
            - unit * jnp.mean(e * unit, axis=-1, keepdims=True)
        )
        store(rows, dv)
        grad_gain, grad_shift = carry
        fold = lambda v: jnp.sum(v.reshape(block // 8, 8, width), axis=0)
        return grad_gain + fold(da * unit), grad_shift + fold(da)

    zero = jnp.zeros((8, width), WIDE)
    grad_gain, grad_shift = lax.fori_loop(0, x_ref.shape[0] // block, step, (zero, zero))
    sums[gain_row : gain_row + 1, :] = jnp.sum(grad_gain, axis=0, keepdims=True)
    sums[gain_row + 1 : gain_row + 2, :] = jnp.sum(grad_shift, axis=0, keepdims=True)


def inproj_stage(a_ref, w_ref, vec, bias_row, z_ref):
    width = a_ref.shape[1]
    for part in range(3):

        def act(k, part=part):
            inner = tiles(k)
            cut = pl.ds(pl.multiple_of(part * width + k * TILE, TILE), TILE)
            total = dot(a_ref[...], columns(w_ref, cut))
            if part != 1:
                row = bias_row + part // 2
                total = total + vec[row : row + 1, inner]
            z_ref[:, cut] = total.astype(LOW)

        each(width // TILE, act)


def project_stage(a_ref, w_ref, vec, bias_row, store):
    def act(k):
        cut = tiles(k)
        store(cut, dot(a_ref[...], columns(w_ref, cut)) + vec[bias_row : bias_row + 1, cut])

    each(w_ref.shape[2] // TILE, act)


def back_stage(dz_ref, w_ref, acc_ref):
    width = acc_ref.shape[1]
    parts = w_ref.shape[2] // width
    acc_ref[...] = dot_nt(dz_ref[:, :width], columns(w_ref, pl.ds(0, width)))

    def act(k):
        cut = tiles(k + 1, width)
        acc_ref[...] = acc_ref[...] + dot_nt(dz_ref[:, cut], columns(w_ref, cut))

    if parts > 1:
        each(parts - 1, act)


def turn_stage(a_ref, at_ref):
    width = a_ref.shape[1]

    def act(k):
        at_ref[tiles(k), :] = a_ref[:, tiles(k)].T

    each(width // TILE, act)
    at_ref[width:, :] = jnp.ones((at_ref.shape[0] - width, at_ref.shape[1]), LOW)


def weight_stage(at_ref, dz_ref, g_ref, bias):
    depth, rows, _ = g_ref.shape
    full = depth * rows

    def act(k):
        cut = tiles(k)
        total = dot(at_ref[...], dz_ref[:, cut])
        g_ref[:, :, cut] = total[:full].astype(LOW).reshape((depth, rows, TILE))
        bias(k, total[full : full + 1])

    each(g_ref.shape[2] // TILE, act)


def bias_rows(sums, table, width):
    def act(k, total):
        per = width // TILE
        for part, row in enumerate(table):
            if row is None:
                continue

            @pl.when((k >= part * per) & (k < (part + 1) * per))
            def _():
                sums[row : row + 1, tiles(k - part * per)] = total

    return act


def low_head(rows):
    lane = lax.broadcasted_iota(jnp.int32, (rows, LANES), 1)
    return lane < LANES // 2


def space_attend(z_ref, p_ref, o_ref, frames, rows, valid, block):
    width = o_ref.shape[1]
    pairs = width // LANES
    scale = (LANES // 2) ** -0.5

    def act(step):
        f, pair = step // pairs, step % pairs
        span = tiles(f, rows)
        q = z_ref[span, pl.ds(pl.multiple_of(pair * LANES, LANES), LANES)]
        k = z_ref[span, pl.ds(pl.multiple_of(width + pair * LANES, LANES), LANES)]
        v = z_ref[span, pl.ds(pl.multiple_of(2 * width + pair * LANES, LANES), LANES)]
        first = low_head(rows)
        vt = v.T
        keep = lax.broadcasted_iota(jnp.int32, (rows, rows), 0) % block < valid
        outs = []
        for side in range(2):
            mine = first if side == 0 else ~first
            scores = dot_nt(k, jnp.where(mine, q, jnp.zeros_like(q))) * scale
            scores = jnp.where(keep, scores, -1e30)
            e = jnp.exp(scores - jnp.max(scores, axis=0, keepdims=True))
            p = (e * (1.0 / jnp.sum(e, axis=0, keepdims=True))).astype(LOW)
            p_ref[2 * step + side] = p
            outs.append(dot(vt, p))
        top = lax.broadcasted_iota(jnp.int32, (LANES, rows), 0) < LANES // 2
        o = jnp.where(top, outs[0], outs[1]).T
        o_ref[span, pl.ds(pl.multiple_of(pair * LANES, LANES), LANES)] = o.astype(LOW)

    each(frames * pairs, act)


def space_attend_back(z_ref, p_ref, do_ref, dz_ref, frames, rows):
    width = do_ref.shape[1]
    pairs = width // LANES
    scale = (LANES // 2) ** -0.5

    def act(step):
        f, pair = step // pairs, step % pairs
        span = tiles(f, rows)
        cut_q = pl.ds(pl.multiple_of(pair * LANES, LANES), LANES)
        cut_k = pl.ds(pl.multiple_of(width + pair * LANES, LANES), LANES)
        cut_v = pl.ds(pl.multiple_of(2 * width + pair * LANES, LANES), LANES)
        q, k, v, do = z_ref[span, cut_q], z_ref[span, cut_k], z_ref[span, cut_v], do_ref[span, cut_q]
        kt = k.T
        first = low_head(rows)
        dk = dv = None
        turned = []
        for side in range(2):
            mine = first if side == 0 else ~first
            q_side = jnp.where(mine, q, jnp.zeros_like(q))
            do_side = jnp.where(mine, do, jnp.zeros_like(do))
            p_low = p_ref[2 * step + side]
            p = p_low.astype(WIDE)
            dp = dot_nt(v, do_side)
            inner = jnp.sum(dp * p, axis=0, keepdims=True)
            ds = (p * (dp - inner)).astype(LOW)
            dv_side, dk_side = dot(p_low, do_side), dot(ds, q_side)
            dv = dv_side if dv is None else dv + dv_side
            dk = dk_side if dk is None else dk + dk_side
            turned.append(dot(kt, ds))
        top = lax.broadcasted_iota(jnp.int32, (LANES, rows), 0) < LANES // 2
        dq = jnp.where(top, turned[0], turned[1]).T
        dz_ref[span, cut_q] = (dq * scale).astype(LOW)
        dz_ref[span, cut_k] = (dk * scale).astype(LOW)
        dz_ref[span, cut_v] = dv.astype(LOW)

    each(frames * pairs, act)


def head_sum(width):
    row = lax.broadcasted_iota(jnp.int32, (width, LANES), 0) // (width // HEADS)
    col = lax.broadcasted_iota(jnp.int32, (width, LANES), 1)
    return (row == col).astype(WIDE).astype(LOW)


def head_spread(width):
    row = lax.broadcasted_iota(jnp.int32, (LANES, width), 0)
    col = lax.broadcasted_iota(jnp.int32, (LANES, width), 1) // (width // HEADS)
    return (row == col).astype(WIDE).astype(LOW)


def by_head(product, pick):
    high = product.astype(LOW)
    rest = (product - high.astype(WIDE)).astype(LOW)
    return dot(high, pick) + dot(rest, pick)


def time_attend(z_ref, p_ref, o_ref, frames, block):
    width = o_ref.shape[1]
    scale = (width // HEADS) ** -0.5
    pick, spread = head_sum(width), head_spread(width)
    spans = [slice(k * block, (k + 1) * block) for k in range(frames)]

    def act(pair):
        rows = tiles(pair, 2 * block)
        q = z_ref[rows, :width].astype(WIDE)
        scores = [[], []]
        for span in spans:
            k = z_ref[span, width : 2 * width].astype(WIDE)
            for half in range(2):
                scores[half].append(by_head(q[spans[half]] * k, pick) * scale)
        probs = []
        for half in range(2):
            top = functools.reduce(jnp.maximum, scores[half])
            e = [jnp.exp(s - top) for s in scores[half]]
            inverse = 1.0 / functools.reduce(jnp.add, e)
            probs.append([item * inverse for item in e])
        out = [jnp.zeros((block, width), WIDE)] * 2
        for k, span in enumerate(spans):
            v = z_ref[span, 2 * width :].astype(WIDE)
            for half in range(2):
                p = probs[half][k]
                p_ref[2 * pair + half, span, :] = p
                out[half] = out[half] + dot(p.astype(LOW), spread) * v
        o_ref[rows, :] = jnp.concatenate(out, axis=0).astype(LOW)

    each(frames // 2, act)


def time_attend_back(z_ref, p_ref, do_ref, dz_ref, dk_ref, dv_ref, frames, block):
    width = do_ref.shape[1]
    scale = (width // HEADS) ** -0.5
    pick, spread = head_sum(width), head_spread(width)
    spans = [slice(k * block, (k + 1) * block) for k in range(frames)]
    dk_ref[...] = jnp.zeros_like(dk_ref)
    dv_ref[...] = jnp.zeros_like(dv_ref)

    def act(pair):
        rows = tiles(pair, 2 * block)
        do = do_ref[rows, :].astype(WIDE)
        q = z_ref[rows, :width].astype(WIDE)
        dps = [[], []]
        inner = [jnp.zeros((block, LANES), WIDE)] * 2
        for span in spans:
            v = z_ref[span, 2 * width :].astype(WIDE)
            for half in range(2):
                dp = by_head(do[spans[half]] * v, pick)
                inner[half] = inner[half] + dp * p_ref[2 * pair + half, span, :]
                dps[half].append(dp)
        dq = [jnp.zeros((block, width), WIDE)] * 2
        for at, span in enumerate(spans):
            k = z_ref[span, width : 2 * width].astype(WIDE)
            dk, dv = dk_ref[span, :], dv_ref[span, :]
            for half in range(2):
                p = p_ref[2 * pair + half, span, :]
                ds = dot((p * (dps[half][at] - inner[half])).astype(LOW), spread)
                dq[half] = dq[half] + ds * k
                dk = dk + ds * q[spans[half]]
                dv = dv + dot(p.astype(LOW), spread) * do[spans[half]]
            dk_ref[span, :] = dk
            dv_ref[span, :] = dv
        dz_ref[rows, :width] = (jnp.concatenate(dq, axis=0) * scale).astype(LOW)

    each(frames // 2, act)

    def out(pair):
        rows = tiles(pair, 2 * block)
        dz_ref[rows, width : 2 * width] = (dk_ref[rows, :] * scale).astype(LOW)
        dz_ref[rows, 2 * width :] = dv_ref[rows, :].astype(LOW)

    each(frames // 2, out)


def expand_stage(a_ref, w_ref, vec, g_ref, slope_ref):
    width = a_ref.shape[1]
    per = width // TILE

    def act(k):
        cut = tiles(k)
        h = dot(a_ref[...], columns(w_ref, cut))
        inner = tiles(k % per)
        bias = vec[pl.ds(E_BIAS + k // per, 1), inner]
        h = h + bias
        cdf = 0.5 * (1.0 + lax.erf(h * (0.5 ** 0.5)))
        g_ref[:, cut] = (h * cdf).astype(LOW)
        slope_ref[:, cut] = (cdf + h * (jnp.exp(-0.5 * h * h) * 0.3989422804014327)).astype(LOW)

    each(w_ref.shape[2] // TILE, act)


def reduce_stage(g_ref, w_ref, vec, x_ref, out_store):
    depth, rows, width = w_ref.shape

    def act(k):
        cut = tiles(k)
        total = x_ref[:, cut] + vec[R_BIAS : R_BIAS + 1, cut]
        for z in range(depth):
            total = total + dot(g_ref[:, z * rows : (z + 1) * rows], w_ref[z, :, cut])
        out_store(cut, total)

    each(width // TILE, act)


def reduce_back_stage(dm_ref, w_ref, slope_ref, dh_ref):
    depth, rows, _ = w_ref.shape
    per = rows // TILE

    def act(k):
        cut = tiles(k)
        block = w_ref[k // per, tiles(k % per), :]
        dh_ref[:, cut] = (dot_nt(dm_ref[...], block) * slope_ref[:, cut].astype(WIDE)).astype(LOW)

    each(depth * per, act)


def reduce_grad_stage(g_ref, gt_ref, dm_ref, out_ref, sums):
    depth, rows, width = out_ref.shape

    def act(k):
        z, part = k // (rows // TILE), k % (rows // TILE)
        turned = g_ref[:, tiles(k)].T
        gt_ref[...] = turned
        out_ref[z, tiles(part), :] = dot(gt_ref[...], dm_ref[...]).astype(LOW)

    each(depth * rows // TILE, act)
    ones = jnp.ones((16, dm_ref.shape[0]), LOW)
    sums[R_BIAS : R_BIAS + 1, :] = dot(ones, dm_ref[...])[:1]


def vmem_call(body, outs, ins, scratch, name):
    return pl.pallas_call(
        body,
        out_shape=[jax.ShapeDtypeStruct(shape, kind) for shape, kind in outs],
        in_specs=[pl.BlockSpec(memory_space=pltpu.VMEM)] * len(ins),
        out_specs=[pl.BlockSpec(memory_space=pltpu.VMEM)] * len(outs),
        scratch_shapes=[pltpu.VMEM(shape, kind) for shape, kind in scratch],
        compiler_params=pltpu.CompilerParams(vmem_limit_bytes=60 << 20),
        name=name,
    )(*ins)


def time_forward(block, x, vec, w_in, w_out, w_lin):
    rows, width = x.shape
    frames = rows // block

    def body(x_ref, vec_ref, w_in, w_out, w_lin, b_ref, a_ref, z_ref, p_ref, o_ref, u_ref):
        def store(ref):
            def act(cut, total):
                ref[:, cut] = total.astype(LOW)

            return act

        norm_stage(x_ref, vec_ref, T_GAIN, a_ref, 2 * block)
        inproj_stage(a_ref, w_in, vec_ref, T_INB, z_ref)
        time_attend(z_ref, p_ref, o_ref, frames, block)
        project_stage(o_ref, w_out, vec_ref, T_OUTB, store(u_ref))
        project_stage(u_ref, w_lin, vec_ref, T_LINB, store(b_ref))

    token = ((rows, width), LOW)
    outs = [token, token, ((rows, 3 * width), LOW), ((frames, rows, LANES), WIDE), token, token]
    return vmem_call(body, outs, (x, vec, w_in, w_out, w_lin), [], "time_forward")


def space_layer(shape, x, b, dy, vec, w_in, w_out, w_up, w_down):
    frames, valid, block = shape
    rows, width = x.shape
    span = rows // frames
    hidden = w_up.shape[2]
    heads_all = frames * HEADS

    def body(x_ref, b_ref, dy_ref, vec_ref, w_in, w_out, w_up, w_down, out_ref, dx1_ref, db_ref,
             g_in, g_out, g_up, g_down, sums, x1, x2, a_s, z_s, p_s, o_s, a_m, act_g, slope, dh, acc, at, gt, low):
        sums[...] = jnp.zeros_like(sums)

        def first(k):
            r = tiles(k, 2 * block)
            x1[r, :] = x_ref[r, :].astype(WIDE) + b_ref[r, :].astype(WIDE)

        each(rows // (2 * block), first)
        norm_stage(x1, vec_ref, S_GAIN, a_s, 2 * block)
        inproj_stage(a_s, w_in, vec_ref, S_INB, z_s)
        space_attend(z_s, p_s, o_s, frames, span, valid, block)

        def add_x1(cut, total):
            x2[:, cut] = x1[:, cut] + total

        project_stage(o_s, w_out, vec_ref, S_OUTB, add_x1)
        norm_stage(x2, vec_ref, F_GAIN, a_m, 2 * block)
        expand_stage(a_m, w_up, vec_ref, act_g, slope)

        def put_out(cut, total):
            out_ref[:, cut] = total.astype(LOW)

        reduce_stage(act_g, w_down, vec_ref, x2, put_out)
        reduce_grad_stage(act_g, gt, dy_ref, g_down, sums)
        reduce_back_stage(dy_ref, w_down, slope, dh)
        turn_stage(a_m, at)
        weight_stage(at, dh, g_up, bias_rows(sums, [E_BIAS + k for k in range(hidden // width)], width))
        back_stage(dh, w_up, acc)

        def put_x2(r, dv):
            total = dy_ref[r, :].astype(WIDE) + dv
            dx1_ref[r, :] = total
            low[r, :] = total.astype(LOW)

        norm_back_stage(x2, vec_ref, F_GAIN, acc, sums, 2 * block, put_x2)
        turn_stage(o_s, at)
        weight_stage(at, low, g_out, bias_rows(sums, [S_OUTB], width))
        back_stage(low, w_out, acc)
        low[...] = acc[...].astype(LOW)
        dz = dh.at[:, : 3 * width]
        space_attend_back(z_s, p_s, low, dz, frames, span)
        turn_stage(a_s, at)
        weight_stage(at, dz, g_in, bias_rows(sums, [S_INB, None, S_INB + 1], width))
        back_stage(dz, w_in, acc)

        def put_x1(r, dv):
            total = dx1_ref[r, :] + dv
            dx1_ref[r, :] = total
            db_ref[r, :] = total.astype(LOW)

        norm_back_stage(x1, vec_ref, S_GAIN, acc, sums, 2 * block, put_x1)

    token, full = ((rows, width), LOW), ((rows, width), WIDE)
    outs = [token, full, token] + [(w.shape, LOW) for w in (w_in, w_out, w_up, w_down)] + [(vec.shape, WIDE)]
    scratch = [full, full, token, ((rows, 3 * width), LOW), ((heads_all, span, span), LOW), token, token]
    scratch += [((rows, hidden), LOW)] * 3 + [full, ((width + 16, rows), LOW), ((TILE, rows), LOW), token]
    return vmem_call(body, outs, (x, b, dy, vec, w_in, w_out, w_up, w_down), scratch, "space_layer")


def time_backward(block, db, x, a, z, p, o, u, vec, w_in, w_out, w_lin):
    rows, width = x.shape
    frames = rows // block

    def body(db_ref, x_ref, a_ref, z_ref, p_ref, o_ref, u_ref, vec_ref, w_in, w_out, w_lin,
             dt_ref, g_in, g_out, g_lin, sums, low, dz, dk, dv, acc, at):
        sums[...] = jnp.zeros_like(sums)
        turn_stage(u_ref, at)
        weight_stage(at, db_ref, g_lin, bias_rows(sums, [T_LINB], width))
        back_stage(db_ref, w_lin, acc)
        low[...] = acc[...].astype(LOW)
        turn_stage(o_ref, at)
        weight_stage(at, low, g_out, bias_rows(sums, [T_OUTB], width))
        back_stage(low, w_out, acc)
        low[...] = acc[...].astype(LOW)
        time_attend_back(z_ref, p_ref, low, dz, dk, dv, frames, block)
        turn_stage(a_ref, at)
        weight_stage(at, dz, g_in, bias_rows(sums, [T_INB, None, T_INB + 1], width))
        back_stage(dz, w_in, acc)

        def put(r, dv):
            dt_ref[r, :] = dv.astype(LOW)

        norm_back_stage(x_ref, vec_ref, T_GAIN, acc, sums, 2 * block, put)

    token, full = ((rows, width), LOW), ((rows, width), WIDE)
    outs = [token] + [(w.shape, LOW) for w in (w_in, w_out, w_lin)] + [(vec.shape, WIDE)]
    scratch = [token, ((rows, 3 * width), LOW), full, full, full, ((width + 16, rows), LOW)]
    return vmem_call(body, outs, (db, x, a, z, p, o, u, vec, w_in, w_out, w_lin), scratch, "time_backward")


def stack_rows(terms, groups):
    return tuple(
        (item.reshape((groups, item.shape[0] // groups) + item.shape[1:]) for item in terms)
    )


def fold_rows(received):
    return tuple((jnp.sum(item, axis=0) for item in received))


MESH = pl.DeviceIdType.MESH
TILE_ROWS = 8
SMALL_TILE = (8, 256)


def remote(source, target, send, recv, device):
    return pltpu.make_async_remote_copy(
        src_ref=source,
        dst_ref=target,
        send_sem=send,
        recv_sem=recv,
        device_id=device,
        device_id_type=MESH,
    )


def place(split):
    nz, ny, nx, nc = split
    clip, frame = lax.axis_index("clip"), lax.axis_index("frame")
    z, y, x, c = clip // ny, clip % ny, frame // nc, frame % nc

    def mesh_at(z, y, x, c):
        return (z * ny + y, x * nc + c)

    row = [mesh_at((z + step) % nz, y, x, c) for step in range(1, nz)]
    beside = (mesh_at(z, y, 1 - x, c), mesh_at(z, 1 - y, x, c), mesh_at(z, y, x, 1 - c))
    return (z, y, x, c), row, beside


def greet(devices):
    barrier = pltpu.get_barrier_semaphore()
    for device in devices:
        pl.semaphore_signal(barrier, inc=1, device_id=device, device_id_type=MESH)
    pl.semaphore_wait(barrier, len(devices))


def gather_kernel(split, count, *refs):
    shards, full = refs[:count], refs[count : 2 * count]
    row_send, row_recv, side_send, side_recv, core_send, core_recv, own_sem = refs[2 * count :]
    (z, y, x, c), row, (across_x, across_y, twin) = place(split)
    greet(row + [across_x, across_y, twin])
    started, first, second, third, core = [], {}, {}, {}, {}

    def launch(copy):
        copy.start()
        started.append(copy)
        return copy

    def to_twin(i, step, block):
        return launch(remote(block, block, core_send.at[i, step], core_recv.at[i, step], twin))

    def spread(i):
        own = full[i].at[z, y, x, c]
        first[i] = [
            launch(remote(shards[i], own, row_send.at[i, k], row_recv.at[i, k], device))
            for k, device in enumerate(row)
        ]
        keep = pltpu.make_async_copy(shards[i], own, own_sem.at[i])
        keep.start()
        first[i].append(keep)

    def sideways(i):
        for copy in first[i][:-1]:
            copy.wait_recv()
        first[i][-1].wait()
        block = full[i].at[:, y, x, c]
        second[i] = [
            launch(remote(block, block, side_send.at[i, k], side_recv.at[i, k], device))
            for k, device in enumerate((across_x, across_y))
        ]
        core[i] = [to_twin(i, 0, block)]

    def relay(i):
        half = shards[i].shape[-1] // 2
        second[i][0].wait_recv()
        part = full[i].at[:, y, 1 - x, c, :, pl.ds(0, half)]
        third[i] = [launch(remote(part, part, side_send.at[i, 2], side_recv.at[i, 2], across_y))]
        core[i].append(to_twin(i, 1, full[i].at[:, y, 1 - x, c]))
        second[i][1].wait_recv()
        part = full[i].at[:, 1 - y, x, c, :, pl.ds(half, half)]
        third[i].append(
            launch(remote(part, part, side_send.at[i, 3], side_recv.at[i, 3], across_x))
        )
        core[i].append(to_twin(i, 2, full[i].at[:, 1 - y, x, c]))

    def finish(i):
        for copy in third[i]:
            copy.wait_recv()
        core[i].append(to_twin(i, 3, full[i].at[:, 1 - y, 1 - x, c]))

    def receive(i):
        for copy in core[i]:
            copy.wait_recv()

    ahead = 2
    for i in range(min(ahead, count)):
        spread(i)
    for step in range(count + 3):
        for lag, act in enumerate((sideways, relay, finish, receive)):
            if 0 <= step - lag < count:
                act(step - lag)
            if lag == 0 and step + ahead < count:
                spread(step + ahead)
    for copy in started:
        copy.wait_send()


def gather_shards(split, shards):
    count = len(shards)
    sem = pltpu.SemaphoreType.DMA
    full = pl.pallas_call(
        functools.partial(gather_kernel, split, count),
        out_shape=[jax.ShapeDtypeStruct(split + item.shape, item.dtype) for item in shards],
        in_specs=[pl.BlockSpec(memory_space=pl.ANY)] * count,
        out_specs=[pl.BlockSpec(memory_space=pl.ANY)] * count,
        scratch_shapes=[sem((count, split[0] - 1))] * 2 + [sem((count, 4))] * 4 + [sem((count,))],
        compiler_params=pltpu.CompilerParams(collective_id=0, has_side_effects=True),
        name="gather_shards",
    )(*shards)
    return [item.reshape((-1, item.shape[-1])) for item in full]


def sum_kernel(split, count, *refs):
    groups = [refs[k * count : (k + 1) * count] for k in range(8)]
    mine, outs, held, low_half, high_half, from_x, from_y, from_row = groups
    core_send, core_recv, side_send, side_recv, row_send, row_recv = refs[8 * count :]
    (z, y, x, c), row, (across_x, across_y, twin) = place(split)
    greet(row + [across_x, across_y, twin])
    depth = split[0]
    started, core, diagonal, side, last = [], {}, {}, {}, {}

    def launch(copy):
        copy.start()
        started.append(copy)
        return copy

    def each_row(act):
        def step(k, carry):
            act(k)
            return carry

        lax.fori_loop(0, depth, step, 0)

    def swap(i):
        block = mine[i].at[:, :, :, 1 - c]
        core[i] = launch(remote(block, held[i], core_send.at[i], core_recv.at[i], twin))

    def fold_core(i):
        core[i].wait_recv()
        half = mine[i].shape[-1] // 2

        def fold(yy, xx):
            def act(k):
                held[i][k, yy, xx] = held[i][k, yy, xx] + mine[i][k, yy, xx, c]

            each_row(act)

        fold(1 - y, 1 - x)
        low = held[i].at[:, 1 - y, 1 - x, :, pl.ds(0, half)]
        high = held[i].at[:, 1 - y, 1 - x, :, pl.ds(half, half)]
        diagonal[i] = [
            launch(remote(low, low_half[i], side_send.at[i, 0], side_recv.at[i, 0], across_x)),
            launch(remote(high, high_half[i], side_send.at[i, 1], side_recv.at[i, 1], across_y)),
        ]
        fold(1 - y, x)
        fold(y, 1 - x)
        fold(y, x)

    def fold_diagonal(i):
        half = mine[i].shape[-1] // 2
        diagonal[i][0].wait_recv()

        def act_low(k):
            held[i][k, 1 - y, x, :, :half] = held[i][k, 1 - y, x, :, :half] + low_half[i][k]

        each_row(act_low)
        block = held[i].at[:, 1 - y, x]
        side[i] = [
            launch(remote(block, from_y[i], side_send.at[i, 2], side_recv.at[i, 2], across_y))
        ]
        diagonal[i][1].wait_recv()

        def act_high(k):
            held[i][k, y, 1 - x, :, half:] = held[i][k, y, 1 - x, :, half:] + high_half[i][k]

        each_row(act_high)
        block = held[i].at[:, y, 1 - x]
        side[i].append(
            launch(remote(block, from_x[i], side_send.at[i, 3], side_recv.at[i, 3], across_x))
        )

    def fold_side(i):
        for copy in side[i]:
            copy.wait_recv()

        def act(k):
            total = held[i][k, y, x].astype(jnp.float32) + from_x[i][k].astype(jnp.float32)
            held[i][k, y, x] = (total + from_y[i][k].astype(jnp.float32)).astype(jnp.bfloat16)

        each_row(act)
        last[i] = [
            launch(
                remote(
                    held[i].at[(z + k + 1) % depth, y, x],
                    from_row[i].at[k],
                    row_send.at[i, k],
                    row_recv.at[i, k],
                    device,
                )
            )
            for k, device in enumerate(row)
        ]

    def fold_row(i):
        for copy in last[i]:
            copy.wait_recv()
        total = held[i][z, y, x].astype(jnp.float32)
        for k in range(depth - 1):
            total = total + from_row[i][k].astype(jnp.float32)
        outs[i][...] = total

    for i in range(count):
        swap(i)
    for step in range(count + 3):
        for lag, act in enumerate((fold_core, fold_diagonal, fold_side, fold_row)):
            if 0 <= step - lag < count:
                act(step - lag)
    for copy in started:
        copy.wait_send()


def sum_shards(split, terms):
    count = len(terms)
    nz, ny, nx, _ = split
    blocks = [item.reshape(split + (-1, item.shape[-1])) for item in terms]
    shapes = [item.shape[4:] for item in blocks]
    low = jnp.bfloat16
    sem = pltpu.SemaphoreType.DMA
    scratch = [pltpu.VMEM((nz, ny, nx) + s, low) for s in shapes]
    scratch += [pltpu.VMEM((nz, s[0], s[1] // 2), low) for s in shapes] * 2
    scratch += [pltpu.VMEM((nz,) + s, low) for s in shapes] * 2
    scratch += [pltpu.VMEM((nz - 1,) + s, low) for s in shapes]
    scratch += [sem((count,))] * 2 + [sem((count, 4))] * 2 + [sem((count, nz - 1))] * 2
    return pl.pallas_call(
        functools.partial(sum_kernel, split, count),
        out_shape=[jax.ShapeDtypeStruct(s, jnp.float32) for s in shapes],
        in_specs=[pl.BlockSpec(memory_space=pltpu.VMEM)] * count,
        out_specs=[pl.BlockSpec(memory_space=pltpu.VMEM)] * count,
        scratch_shapes=scratch,
        compiler_params=pltpu.CompilerParams(
            collective_id=1, has_side_effects=True, vmem_limit_bytes=60 << 20
        ),
        name="sum_shards",
    )(*blocks)


def inner_split(rows):
    clips, frames = lax.axis_size("clip"), lax.axis_size("frame")
    if frames == 4 and clips % 2 == 0 and clips > 2 and rows % TILE_ROWS == 0:
        return (clips // 2, 2, 2, 2)
    return None


def pack_small(vectors, groups):
    rows = jnp.concatenate([item.reshape(groups, -1) for item in vectors], axis=1)
    size = SMALL_TILE[0] * SMALL_TILE[1]
    rows = jnp.pad(rows, ((0, 0), (0, size - rows.shape[1])))
    return rows.reshape((groups * SMALL_TILE[0], SMALL_TILE[1]))


def unpack_small(packed, widths):
    rows = packed.reshape(-1, SMALL_TILE[0] * SMALL_TILE[1])
    pieces, at = [], 0
    for width in widths:
        pieces.append(rows[:, at : at + width].reshape(-1))
        at += width
    return pieces


def gather_all(split, params):
    if split is None:
        return [lax.all_gather(item, ("clip", "frame"), axis=0, tiled=True) for item in params]
    wide = [k for k, item in enumerate(params) if item.ndim == 2]
    thin = [k for k, item in enumerate(params) if item.ndim == 1]
    full = gather_shards(split, [pack_small([params[k] for k in thin], 1)] + [params[k] for k in wide])
    vectors = unpack_small(full[0], [params[k].shape[0] for k in thin])
    result = dict(zip(wide, full[1:])) | dict(zip(thin, vectors))
    return [result[k] for k in range(len(params))]


def sum_all(split, terms):
    if split is None:
        groups = lax.axis_size("clip")
        received = [
            lax.all_to_all(
                item.astype(jnp.bfloat16), "clip", split_axis=0, concat_axis=0, tiled=True
            ).astype(jnp.float32)
            for item in stack_rows(terms, groups)
        ]
        return [
            lax.psum_scatter(
                item.astype(jnp.bfloat16), "frame", scatter_dimension=0, tiled=True
            ).astype(jnp.float32)
            for item in fold_rows(received)
        ]
    devices = split[0] * split[1] * split[2] * split[3]
    wide = [k for k, item in enumerate(terms) if item.ndim == 2]
    thin = [k for k, item in enumerate(terms) if item.ndim == 1]
    low = [item.astype(jnp.bfloat16) for item in terms]
    order = wide[::-1]
    sums = sum_shards(split, [low[k] for k in order] + [pack_small([low[k] for k in thin], devices)])
    vectors = unpack_small(sums[-1], [terms[k].shape[0] // devices for k in thin])
    result = dict(zip(order, sums[:-1])) | dict(zip(thin, vectors))
    return [result[k] for k in range(len(terms))]


VECTOR_ROWS = (0, 1, 10, 2, 3, 4, 5, 12, 6, 7, 8, 14, 9)


def on_device(
    video_tokens,
    time_gain,
    time_shift,
    time_inproj,
    time_inbias,
    time_outproj,
    time_outbias,
    time_linear,
    time_linbias,
    space_gain,
    space_shift,
    space_inproj,
    space_inbias,
    space_outproj,
    space_outbias,
    feed_gain,
    feed_shift,
    expand_weight,
    expand_bias,
    reduce_weight,
    reduce_bias,
    cotangent,
):
    split = inner_split(time_gain.shape[0])
    params = [
        time_gain,
        time_shift,
        time_inproj,
        time_inbias,
        time_outproj,
        time_outbias,
        time_linear,
        time_linbias,
        space_gain,
        space_shift,
        space_inproj,
        space_inbias,
        space_outproj,
        space_outbias,
        feed_gain,
        feed_shift,
        expand_weight,
        expand_bias,
        reduce_weight,
        reduce_bias,
    ]
    full = gather_all(split, params)
    frames, places, width = video_tokens.shape[1:]
    groups = lax.axis_size("frame")
    valid = places // groups
    block = -(-valid // TILE_ROWS) * TILE_ROWS
    rows = frames * groups * block

    def padded(tokens):
        cut = tokens.reshape((frames, groups, valid, width))
        return jnp.pad(cut, ((0, 0), (0, 0), (0, block - valid), (0, 0)))

    def to_places(tokens):
        return lax.all_to_all(
            tokens.reshape((frames, groups, block, width)),
            "frame",
            split_axis=1,
            concat_axis=0,
            tiled=True,
        ).reshape((rows, width))

    def to_frames(tokens):
        return lax.all_to_all(
            tokens.reshape((frames * groups, 1, block, width)),
            "frame",
            split_axis=0,
            concat_axis=1,
            tiled=True,
        ).reshape((rows, width))

    def trimmed(tokens):
        cut = tokens.reshape((frames, groups, block, width))[:, :, :valid]
        return cut.reshape((1, frames, places, width))

    def weight(item):
        return item.reshape((4, -1, item.shape[1]))

    thin = [item for item in full if item.ndim == 1]
    t_in, t_out, t_lin, s_in, s_out, w_up, w_down = [weight(item) for item in full if item.ndim == 2]
    pieces = sorted(zip(VECTOR_ROWS, thin), key=lambda pair: pair[0])
    vec = jnp.concatenate([item.reshape((-1, width)) for _, item in pieces], axis=0)
    vec = jnp.pad(vec, ((0, 24 - vec.shape[0]), (0, 0))).astype(WIDE)
    tokens, d_out = padded(video_tokens), padded(cotangent)
    own = tokens.reshape((rows, width))
    placed = to_places(tokens)
    b_t, a_t, z_t, p_t, o_t, u_t = time_forward(block, placed, vec, t_in, t_out, t_lin)
    layer_out, d_x1, d_b, g_s_in, g_s_out, g_up, g_down, sums_s = space_layer(
        (frames, valid, block),
        own,
        to_frames(b_t),
        d_out.reshape((rows, width)),
        vec,
        s_in,
        s_out,
        w_up,
        w_down,
    )
    d_t, g_t_in, g_t_out, g_t_lin, sums_t = time_backward(
        block, to_places(d_b), placed, a_t, z_t, p_t, o_t, u_t, vec, t_in, t_out, t_lin
    )
    input_grad = d_x1 + to_frames(d_t).astype(WIDE)
    sums = sums_s + sums_t
    wide = iter(
        [item.reshape((-1, width if item is g_down else item.shape[2])) for item in
         (g_t_in, g_t_out, g_t_lin, g_s_in, g_s_out, g_up, g_down)]
    )
    rows_of = iter(VECTOR_ROWS)
    terms = []
    for item in params:
        if item.ndim == 2:
            terms.append(next(wide))
        else:
            at = next(rows_of)
            count = item.shape[0] * lax.axis_size(("clip", "frame")) // width
            terms.append(sums[at : at + count].reshape(-1))
    summed = sum_all(split, terms)
    return (trimmed(layer_out), trimmed(input_grad)) + tuple(summed)


def solution(mesh):
    return jax.shard_map(
        on_device,
        mesh=mesh,
        in_specs=(
            P("clip", "frame", None, None),
            P(("clip", "frame")),
            P(("clip", "frame")),
            P(("clip", "frame"), None),
            P(("clip", "frame")),
            P(("clip", "frame"), None),
            P(("clip", "frame")),
            P(("clip", "frame"), None),
            P(("clip", "frame")),
            P(("clip", "frame")),
            P(("clip", "frame")),
            P(("clip", "frame"), None),
            P(("clip", "frame")),
            P(("clip", "frame"), None),
            P(("clip", "frame")),
            P(("clip", "frame")),
            P(("clip", "frame")),
            P(("clip", "frame"), None),
            P(("clip", "frame")),
            P(("clip", "frame"), None),
            P(("clip", "frame")),
            P("clip", "frame", None, None),
        ),
        out_specs=(
            P("clip", "frame", None, None),
            P("clip", "frame", None, None),
            P(("clip", "frame")),
            P(("clip", "frame")),
            P(("clip", "frame"), None),
            P(("clip", "frame")),
            P(("clip", "frame"), None),
            P(("clip", "frame")),
            P(("clip", "frame"), None),
            P(("clip", "frame")),
            P(("clip", "frame")),
            P(("clip", "frame")),
            P(("clip", "frame"), None),
            P(("clip", "frame")),
            P(("clip", "frame"), None),
            P(("clip", "frame")),
            P(("clip", "frame")),
            P(("clip", "frame")),
            P(("clip", "frame"), None),
            P(("clip", "frame")),
            P(("clip", "frame"), None),
            P(("clip", "frame")),
        ),
        check_vma=False,
    )
```

```python
import functools

import jax
import jax.numpy as jnp
from jax import lax
from jax.experimental import pallas as pl
from jax.experimental.pallas import tpu as pltpu
from jax.sharding import PartitionSpec as P

MESH = pl.DeviceIdType.MESH
TILE_ROWS = 8
LOW = jnp.bfloat16
WIDE = jnp.float32
HEADS = 12
norm_eps = 1e-06
LANES = 128
TILE = 256
T_GAIN, T_SHIFT, T_OUTB, T_LINB, S_GAIN, S_SHIFT, S_OUTB, F_GAIN, F_SHIFT, R_BIAS, T_INB, S_INB, E_BIAS = 0, 1, 2, 3, 4, 5, 6, 7, 8, 9, 10, 12, 14


def dot(a, b):
    return lax.dot_general(a, b, (((1,), (0,)), ((), ())), preferred_element_type=WIDE)


def dot_nt(a, b):
    return lax.dot_general(a, b, (((1,), (1,)), ((), ())), preferred_element_type=WIDE)


def each(count, act, start=0):
    def step(k, carry):
        act(k)
        return carry

    lax.fori_loop(start, count, step, 0)


def tiles(k, size=TILE):
    return pl.ds(pl.multiple_of(k * size, size), size)


def columns(w_ref, cut):
    block = w_ref[:, :, cut]
    return block.reshape((block.shape[0] * block.shape[1], block.shape[2]))


def wide_rows(ref, k, size):
    if len(ref.shape) == 2:
        return ref[tiles(k, size), :].astype(WIDE)
    per = size // ref.shape[1]
    block = ref[pl.ds(k * per, per), :, :].astype(WIDE)
    return block.reshape((size, ref.shape[2]))


def put_rows(ref, k, size, value):
    if len(ref.shape) == 2:
        ref[tiles(k, size), :] = value.astype(ref.dtype)
    else:
        per = size // ref.shape[1]
        ref[pl.ds(k * per, per), :, :] = value.reshape((per,) + ref.shape[1:]).astype(ref.dtype)


def normal(x):
    center = x - jnp.mean(x, axis=-1, keepdims=True)
    inverse = lax.rsqrt(jnp.mean(center * center, axis=-1, keepdims=True) + norm_eps)
    return center * inverse, inverse


def norm_stage(x_ref, vec, gain_row, a_ref, block):
    gain, shift = vec[gain_row : gain_row + 1, :], vec[gain_row + 1 : gain_row + 2, :]

    def act(k):
        unit, _ = normal(wide_rows(x_ref, k, block))
        a_ref[tiles(k, block), :] = (unit * gain + shift).astype(LOW)

    each(a_ref.shape[0] // block, act)


def norm_back_stage(x_ref, vec, gain_row, da_ref, sums, block, store):
    gain = vec[gain_row : gain_row + 1, :]
    width = da_ref.shape[1]

    def step(k, carry):
        unit, inverse = normal(wide_rows(x_ref, k, block))
        da = da_ref[tiles(k, block), :]
        e = da * gain
        dv = inverse * (
            e
            - jnp.mean(e, axis=-1, keepdims=True)
            - unit * jnp.mean(e * unit, axis=-1, keepdims=True)
        )
        store(k, dv)
        grad_gain, grad_shift = carry
        fold = lambda v: jnp.sum(v.reshape(block // 8, 8, width), axis=0)
        return grad_gain + fold(da * unit), grad_shift + fold(da)

    zero = jnp.zeros((8, width), WIDE)
    grad_gain, grad_shift = lax.fori_loop(0, da_ref.shape[0] // block, step, (zero, zero))
    sums[gain_row : gain_row + 1, :] = jnp.sum(grad_gain, axis=0, keepdims=True)
    sums[gain_row + 1 : gain_row + 2, :] = jnp.sum(grad_shift, axis=0, keepdims=True)


def inproj_stage(a_ref, w_ref, vec, bias_row, z_ref):
    width = a_ref.shape[1]
    for part in range(3):

        def act(k, part=part):
            inner = tiles(k)
            cut = pl.ds(pl.multiple_of(part * width + k * TILE, TILE), TILE)
            total = dot(a_ref[...], columns(w_ref, cut))
            if part != 1:
                row = bias_row + part // 2
                total = total + vec[row : row + 1, inner]
            z_ref[:, cut] = total.astype(LOW)

        each(width // TILE, act)


def project_stage(a_ref, w_ref, vec, bias_row, store):
    def act(k):
        cut = tiles(k)
        store(cut, dot(a_ref[...], columns(w_ref, cut)) + vec[bias_row : bias_row + 1, cut])

    each(w_ref.shape[2] // TILE, act)


def back_stage(dz_ref, w_ref, acc_ref):
    width = acc_ref.shape[1]
    parts = w_ref.shape[2] // width
    acc_ref[...] = dot_nt(dz_ref[:, :width], columns(w_ref, pl.ds(0, width)))

    def act(k):
        cut = tiles(k + 1, width)
        acc_ref[...] = acc_ref[...] + dot_nt(dz_ref[:, cut], columns(w_ref, cut))

    if parts > 1:
        each(parts - 1, act)


def turn_stage(a_ref, at_ref):
    width = a_ref.shape[1]

    def act(k):
        at_ref[tiles(k), :] = a_ref[:, tiles(k)].T

    each(width // TILE, act)
    at_ref[width:, :] = jnp.ones((at_ref.shape[0] - width, at_ref.shape[1]), LOW)


def weight_stage(at_ref, dz_ref, g_ref, bias):
    depth, rows, _ = g_ref.shape
    full = depth * rows

    def act(k):
        cut = tiles(k)
        total = dot(at_ref[...], dz_ref[:, cut])
        g_ref[:, :, cut] = total[:full].astype(LOW).reshape((depth, rows, TILE))
        bias(k, total[full : full + 1])

    each(g_ref.shape[2] // TILE, act)


def bias_rows(sums, table, width):
    def act(k, total):
        per = width // TILE
        for part, row in enumerate(table):
            if row is None:
                continue

            @pl.when((k >= part * per) & (k < (part + 1) * per))
            def _():
                sums[row : row + 1, tiles(k - part * per)] = total

    return act


def low_head(rows):
    lane = lax.broadcasted_iota(jnp.int32, (rows, LANES), 1)
    return lane < LANES // 2


def space_attend(z_ref, p_ref, o_ref, frames, rows, valid, block, start=0, stop=None):
    width = o_ref.shape[1]
    pairs = width // LANES
    scale = (LANES // 2) ** -0.5

    def act(step):
        f, pair = step // pairs, step % pairs
        span = tiles(f, rows)
        q = z_ref[span, pl.ds(pl.multiple_of(pair * LANES, LANES), LANES)]
        k = z_ref[span, pl.ds(pl.multiple_of(width + pair * LANES, LANES), LANES)]
        v = z_ref[span, pl.ds(pl.multiple_of(2 * width + pair * LANES, LANES), LANES)]
        first = low_head(rows)
        vt = v.T
        keep = lax.broadcasted_iota(jnp.int32, (rows, rows), 0) % block < valid
        outs = []
        for side in range(2):
            mine = first if side == 0 else ~first
            scores = dot_nt(k, jnp.where(mine, q, jnp.zeros_like(q))) * scale
            scores = jnp.where(keep, scores, -1e30)
            e = jnp.exp(scores - jnp.max(scores, axis=0, keepdims=True))
            p = (e * (1.0 / jnp.sum(e, axis=0, keepdims=True))).astype(LOW)
            p_ref[2 * step + side] = p
            outs.append(dot(vt, p))
        top = lax.broadcasted_iota(jnp.int32, (LANES, rows), 0) < LANES // 2
        o = jnp.where(top, outs[0], outs[1]).T
        o_ref[span, pl.ds(pl.multiple_of(pair * LANES, LANES), LANES)] = o.astype(LOW)

    each(frames * pairs if stop is None else stop, act, start)


def space_attend_back(z_ref, p_ref, do_ref, dz_ref, frames, rows, start=0, stop=None):
    width = do_ref.shape[1]
    pairs = width // LANES
    scale = (LANES // 2) ** -0.5

    def act(step):
        f, pair = step // pairs, step % pairs
        span = tiles(f, rows)
        cut_q = pl.ds(pl.multiple_of(pair * LANES, LANES), LANES)
        cut_k = pl.ds(pl.multiple_of(width + pair * LANES, LANES), LANES)
        cut_v = pl.ds(pl.multiple_of(2 * width + pair * LANES, LANES), LANES)
        q, k, v, do = z_ref[span, cut_q], z_ref[span, cut_k], z_ref[span, cut_v], do_ref[span, cut_q]
        kt = k.T
        first = low_head(rows)
        dk = dv = None
        turned = []
        for side in range(2):
            mine = first if side == 0 else ~first
            q_side = jnp.where(mine, q, jnp.zeros_like(q))
            do_side = jnp.where(mine, do, jnp.zeros_like(do))
            p_low = p_ref[2 * step + side]
            p = p_low.astype(WIDE)
            dp = dot_nt(v, do_side)
            inner = jnp.sum(dp * p, axis=0, keepdims=True)
            ds = (p * (dp - inner)).astype(LOW)
            dv_side, dk_side = dot(p_low, do_side), dot(ds, q_side)
            dv = dv_side if dv is None else dv + dv_side
            dk = dk_side if dk is None else dk + dk_side
            turned.append(dot(kt, ds))
        top = lax.broadcasted_iota(jnp.int32, (LANES, rows), 0) < LANES // 2
        dq = jnp.where(top, turned[0], turned[1]).T
        dz_ref[span, cut_q] = (dq * scale).astype(LOW)
        dz_ref[span, cut_k] = (dk * scale).astype(LOW)
        dz_ref[span, cut_v] = dv.astype(LOW)

    each(frames * pairs if stop is None else stop, act, start)


def head_sum(width):
    row = lax.broadcasted_iota(jnp.int32, (width, LANES), 0) // (width // HEADS)
    col = lax.broadcasted_iota(jnp.int32, (width, LANES), 1)
    return (row == col).astype(WIDE).astype(LOW)


def head_spread(width):
    row = lax.broadcasted_iota(jnp.int32, (LANES, width), 0)
    col = lax.broadcasted_iota(jnp.int32, (LANES, width), 1) // (width // HEADS)
    return (row == col).astype(WIDE).astype(LOW)


def by_head(product, pick):
    high = product.astype(LOW)
    rest = (product - high.astype(WIDE)).astype(LOW)
    return dot(high, pick) + dot(rest, pick)


def time_attend(z_ref, p_ref, o_ref, frames, block, start=0, stop=None):
    width = o_ref.shape[1]
    scale = (width // HEADS) ** -0.5
    pick, spread = head_sum(width), head_spread(width)
    spans = [slice(k * block, (k + 1) * block) for k in range(frames)]

    def act(pair):
        rows = tiles(pair, 2 * block)
        q = z_ref[rows, :width].astype(WIDE)
        scores = [[], []]
        for span in spans:
            k = z_ref[span, width : 2 * width].astype(WIDE)
            for half in range(2):
                scores[half].append(by_head(q[spans[half]] * k, pick) * scale)
        probs = []
        for half in range(2):
            top = functools.reduce(jnp.maximum, scores[half])
            e = [jnp.exp(s - top) for s in scores[half]]
            inverse = 1.0 / functools.reduce(jnp.add, e)
            probs.append([item * inverse for item in e])
        out = [jnp.zeros((block, width), WIDE)] * 2
        for k, span in enumerate(spans):
            v = z_ref[span, 2 * width :].astype(WIDE)
            for half in range(2):
                p = probs[half][k]
                p = p.astype(LOW)
                p_ref[2 * pair + half, span, :] = p
                out[half] = out[half] + dot(p, spread) * v
        o_ref[rows, :] = jnp.concatenate(out, axis=0).astype(LOW)

    each(frames // 2 if stop is None else stop, act, start)


def time_attend_back(z_ref, p_ref, do_ref, dz_ref, dk_ref, dv_ref, frames, block, between=None):
    width = do_ref.shape[1]
    scale = (width // HEADS) ** -0.5
    pick, spread = head_sum(width), head_spread(width)
    spans = [slice(k * block, (k + 1) * block) for k in range(frames)]
    dk_ref[...] = jnp.zeros_like(dk_ref)
    dv_ref[...] = jnp.zeros_like(dv_ref)

    def act(pair):
        rows = tiles(pair, 2 * block)
        do = do_ref[rows, :].astype(WIDE)
        q = z_ref[rows, :width].astype(WIDE)
        dps = [[], []]
        inner = [jnp.zeros((block, LANES), WIDE)] * 2
        for span in spans:
            v = z_ref[span, 2 * width :].astype(WIDE)
            for half in range(2):
                dp = by_head(do[spans[half]] * v, pick)
                inner[half] = inner[half] + dp * p_ref[2 * pair + half, span, :].astype(WIDE)
                dps[half].append(dp)
        dq = [jnp.zeros((block, width), WIDE)] * 2
        for at, span in enumerate(spans):
            k = z_ref[span, width : 2 * width].astype(WIDE)
            dk, dv = dk_ref[span, :], dv_ref[span, :]
            for half in range(2):
                p = p_ref[2 * pair + half, span, :]
                ds = dot((p.astype(WIDE) * (dps[half][at] - inner[half])).astype(LOW), spread)
                dq[half] = dq[half] + ds * k
                dk = dk + ds * q[spans[half]]
                dv = dv + dot(p, spread) * do[spans[half]]
            dk_ref[span, :] = dk
            dv_ref[span, :] = dv
        dz_ref[rows, :width] = (jnp.concatenate(dq, axis=0) * scale).astype(LOW)

    if between is None:
        each(frames // 2, act)
    else:
        each(frames // 4, act)
        between()
        each(frames // 2, act, frames // 4)
        between()

    def out(pair):
        rows = tiles(pair, 2 * block)
        dz_ref[rows, width : 2 * width] = (dk_ref[rows, :] * scale).astype(LOW)
        dz_ref[rows, 2 * width :] = dv_ref[rows, :].astype(LOW)

    each(frames // 2, out)


def expand_stage(a_ref, w_ref, vec, g_ref, slope_ref, start=0, stop=None):
    width = a_ref.shape[1]
    per = width // TILE

    def act(k):
        cut = tiles(k)
        h = dot(a_ref[...], columns(w_ref, cut))
        inner = tiles(k % per)
        bias = vec[pl.ds(E_BIAS + k // per, 1), inner]
        h = h + bias
        cdf = 0.5 * (1.0 + lax.erf(h * (0.5 ** 0.5)))
        g_ref[:, cut] = (h * cdf).astype(LOW)
        slope_ref[:, cut] = (cdf + h * (jnp.exp(-0.5 * h * h) * 0.3989422804014327)).astype(LOW)

    each(w_ref.shape[2] // TILE if stop is None else stop, act, start)


def reduce_stage(g_ref, w_ref, vec, x_ref, out_store):
    depth, rows, width = w_ref.shape

    def act(k):
        cut = tiles(k)
        total = x_ref[:, cut] + vec[R_BIAS : R_BIAS + 1, cut]
        for z in range(depth):
            total = total + dot(g_ref[:, z * rows : (z + 1) * rows], w_ref[z, :, cut])
        out_store(cut, total)

    each(width // TILE, act)


def reduce_back_stage(dm_ref, w_ref, slope_ref, dh_ref):
    depth, rows, _ = w_ref.shape
    per = rows // TILE

    def act(k):
        cut = tiles(k)
        block = w_ref[k // per, tiles(k % per), :]
        dh_ref[:, cut] = (dot_nt(dm_ref[...], block) * slope_ref[:, cut].astype(WIDE)).astype(LOW)

    each(depth * per, act)


def reduce_grad_stage(g_ref, gt_ref, dm_ref, out_ref, sums):
    depth, rows, width = out_ref.shape

    def act(k):
        z, part = k // (rows // TILE), k % (rows // TILE)
        turned = g_ref[:, tiles(k)].T
        gt_ref[...] = turned
        out_ref[z, tiles(part), :] = dot(gt_ref[...], dm_ref[...]).astype(LOW)

    each(depth * rows // TILE, act)
    ones = jnp.ones((16, dm_ref.shape[0]), LOW)
    sums[R_BIAS : R_BIAS + 1, :] = dot(ones, dm_ref[...])[:1]


def vmem_call(body, outs, ins, scratch, name):
    return pl.pallas_call(
        body,
        out_shape=[jax.ShapeDtypeStruct(shape, kind) for shape, kind in outs],
        in_specs=[pl.BlockSpec(memory_space=pltpu.VMEM)] * len(ins),
        out_specs=[pl.BlockSpec(memory_space=pltpu.VMEM)] * len(outs),
        scratch_shapes=[pltpu.VMEM(shape, kind) for shape, kind in scratch],
        compiler_params=pltpu.CompilerParams(vmem_limit_bytes=60 << 20),
        name=name,
    )(*ins)


def time_forward(block, x, vec, w_in, w_out, w_lin):
    rows, width = x.shape
    frames = rows // block

    def body(x_ref, vec_ref, w_in, w_out, w_lin, b_ref, a_ref, z_ref, p_ref, o_ref, u_ref):
        def store(ref):
            def act(cut, total):
                ref[:, cut] = total.astype(LOW)

            return act

        norm_stage(x_ref, vec_ref, T_GAIN, a_ref, 2 * block)
        inproj_stage(a_ref, w_in, vec_ref, T_INB, z_ref)
        time_attend(z_ref, p_ref, o_ref, frames, block)
        project_stage(o_ref, w_out, vec_ref, T_OUTB, store(u_ref))
        project_stage(u_ref, w_lin, vec_ref, T_LINB, store(b_ref))

    token = ((rows, width), LOW)
    outs = [token, token, ((rows, 3 * width), LOW), ((frames, rows, LANES), LOW), token, token]
    return vmem_call(body, outs, (x, vec, w_in, w_out, w_lin), [], "time_forward")


def space_layer(shape, x, b, dy, vec, w_in, w_out, w_up, w_down):
    frames, valid, block = shape
    rows, width = x.shape
    span = rows // frames
    hidden = w_up.shape[2]
    heads_all = frames * HEADS

    def body(x_ref, b_ref, dy_ref, vec_ref, w_in, w_out, w_up, w_down, out_ref, dx1_ref, db_ref,
             g_in, g_out, g_up, g_down, sums, x1, x2, a_s, z_s, p_s, o_s, a_m, act_g, slope, dh, acc, at, gt, low):
        sums[...] = jnp.zeros_like(sums)

        def first(k):
            r = tiles(k, 2 * block)
            x1[r, :] = x_ref[r, :].astype(WIDE) + b_ref[r, :].astype(WIDE)

        each(rows // (2 * block), first)
        norm_stage(x1, vec_ref, S_GAIN, a_s, 2 * block)
        inproj_stage(a_s, w_in, vec_ref, S_INB, z_s)
        space_attend(z_s, p_s, o_s, frames, span, valid, block)

        def add_x1(cut, total):
            x2[:, cut] = x1[:, cut] + total

        project_stage(o_s, w_out, vec_ref, S_OUTB, add_x1)
        norm_stage(x2, vec_ref, F_GAIN, a_m, 2 * block)
        expand_stage(a_m, w_up, vec_ref, act_g, slope)

        def put_out(cut, total):
            out_ref[:, cut] = total.astype(LOW)

        reduce_stage(act_g, w_down, vec_ref, x2, put_out)
        reduce_grad_stage(act_g, gt, dy_ref, g_down, sums)
        reduce_back_stage(dy_ref, w_down, slope, dh)
        turn_stage(a_m, at)
        weight_stage(at, dh, g_up, bias_rows(sums, [E_BIAS + k for k in range(hidden // width)], width))
        back_stage(dh, w_up, acc)

        def put_x2(k, dv):
            r = tiles(k, 2 * block)
            total = dy_ref[r, :].astype(WIDE) + dv
            dx1_ref[r, :] = total
            low[r, :] = total.astype(LOW)

        norm_back_stage(x2, vec_ref, F_GAIN, acc, sums, 2 * block, put_x2)
        turn_stage(o_s, at)
        weight_stage(at, low, g_out, bias_rows(sums, [S_OUTB], width))
        back_stage(low, w_out, acc)
        low[...] = acc[...].astype(LOW)
        dz = dh.at[:, : 3 * width]
        space_attend_back(z_s, p_s, low, dz, frames, span)
        turn_stage(a_s, at)
        weight_stage(at, dz, g_in, bias_rows(sums, [S_INB, None, S_INB + 1], width))
        back_stage(dz, w_in, acc)

        def put_x1(k, dv):
            r = tiles(k, 2 * block)
            total = dx1_ref[r, :] + dv
            dx1_ref[r, :] = total
            db_ref[r, :] = total.astype(LOW)

        norm_back_stage(x1, vec_ref, S_GAIN, acc, sums, 2 * block, put_x1)

    token, full = ((rows, width), LOW), ((rows, width), WIDE)
    outs = [token, full, token] + [(w.shape, LOW) for w in (w_in, w_out, w_up, w_down)] + [(vec.shape, WIDE)]
    scratch = [full, full, token, ((rows, 3 * width), LOW), ((heads_all, span, span), LOW), token, token]
    scratch += [((rows, hidden), LOW)] * 3 + [full, ((width + 16, rows), LOW), ((TILE, rows), LOW), token]
    return vmem_call(body, outs, (x, b, dy, vec, w_in, w_out, w_up, w_down), scratch, "space_layer")


def time_backward(block, db, x, a, z, p, o, u, vec, w_in, w_out, w_lin):
    rows, width = x.shape
    frames = rows // block

    def body(db_ref, x_ref, a_ref, z_ref, p_ref, o_ref, u_ref, vec_ref, w_in, w_out, w_lin,
             dt_ref, g_in, g_out, g_lin, sums, low, dz, dk, dv, acc, at):
        sums[...] = jnp.zeros_like(sums)
        turn_stage(u_ref, at)
        weight_stage(at, db_ref, g_lin, bias_rows(sums, [T_LINB], width))
        back_stage(db_ref, w_lin, acc)
        low[...] = acc[...].astype(LOW)
        turn_stage(o_ref, at)
        weight_stage(at, low, g_out, bias_rows(sums, [T_OUTB], width))
        back_stage(low, w_out, acc)
        low[...] = acc[...].astype(LOW)
        time_attend_back(z_ref, p_ref, low, dz, dk, dv, frames, block)
        turn_stage(a_ref, at)
        weight_stage(at, dz, g_in, bias_rows(sums, [T_INB, None, T_INB + 1], width))
        back_stage(dz, w_in, acc)

        def put(k, dv):
            put_rows(dt_ref, k, 2 * block, dv)

        norm_back_stage(x_ref, vec_ref, T_GAIN, acc, sums, 2 * block, put)

    token, full = ((rows, width), LOW), ((rows, width), WIDE)
    outs = [token] + [(w.shape, LOW) for w in (w_in, w_out, w_lin)] + [(vec.shape, WIDE)]
    scratch = [token, ((rows, 3 * width), LOW), full, full, full, ((width + 16, rows), LOW)]
    return vmem_call(body, outs, (db, x, a, z, p, o, u, vec, w_in, w_out, w_lin), scratch, "time_backward")


def stack_rows(terms, groups):
    return tuple(
        (item.reshape((groups, item.shape[0] // groups) + item.shape[1:]) for item in terms)
    )


def fold_rows(received):
    return tuple((jnp.sum(item, axis=0) for item in received))


def remote(source, target, send, recv, device):
    return pltpu.make_async_remote_copy(
        src_ref=source,
        dst_ref=target,
        send_sem=send,
        recv_sem=recv,
        device_id=device,
        device_id_type=MESH,
    )


def place(split):
    nz, ny, nx, nc = split
    clip, frame = lax.axis_index("clip"), lax.axis_index("frame")
    z, y, x, c = clip // ny, clip % ny, frame // nc, frame % nc

    def mesh_at(z, y, x, c):
        return (z * ny + y, x * nc + c)

    row = [mesh_at((z + step) % nz, y, x, c) for step in range(1, nz)]
    beside = (mesh_at(z, y, 1 - x, c), mesh_at(z, 1 - y, x, c), mesh_at(z, y, x, 1 - c))
    return (z, y, x, c), row, beside


def greet(devices):
    barrier = pltpu.get_barrier_semaphore()
    for device in devices:
        pl.semaphore_signal(barrier, inc=1, device_id=device, device_id_type=MESH)
    pl.semaphore_wait(barrier, len(devices))


def inner_split(rows):
    clips, frames = lax.axis_size("clip"), lax.axis_size("frame")
    if frames == 4 and clips % 2 == 0 and clips > 2 and rows % TILE_ROWS == 0:
        return (clips // 2, 2, 2, 2)
    return None


SMALL_ROWS = 16
RING = 6
STAGES = 3
SUB = 4


class Gather:
    def __init__(self, split, where, row, beside, chunks, sems):
        self.split, self.where, self.row, self.beside = split, where, row, beside
        self.chunks, self.sems = chunks, sems
        self.started, self.first, self.second, self.third, self.core = [], {}, {}, {}, {}
        self.step = 0

    def launch(self, copy):
        copy.start()
        self.started.append(copy)
        return copy

    def rows(self, i, y, x, c):
        _, ny, nx, nc = self.split
        _, full, per, low, count, _, _ = self.chunks[i]
        slot = ((y * nx) + x) * nc + c
        return pl.ds(pl.multiple_of(slot * per + low, TILE_ROWS), count)

    def block(self, i, y, x, c, half=None):
        full, low, count, start, width = (self.chunks[i][k] for k in (1, 3, 4, 5, 6))
        rows, cols = self.rows(i, y, x, c), pl.ds(start, width)
        if half is not None and width % (2 * LANES) == 0:
            cols = pl.ds(start + half * (width // 2), width // 2)
        elif half is not None:
            slot = ((y * self.split[2]) + x) * self.split[3] + c
            at = slot * self.chunks[i][2] + low + half * (count // 2)
            rows = pl.ds(pl.multiple_of(at, TILE_ROWS), count // 2)
        return full.at[:, rows, cols]

    def spread(self, i):
        z, y, x, c = self.where
        shard, full, _, low, count, start, width = self.chunks[i]
        row_send, row_recv = self.sems[0], self.sems[1]
        own = full.at[z, self.rows(i, y, x, c), pl.ds(start, width)]
        mine = shard.at[pl.ds(low, count), pl.ds(start, width)]
        self.first[i] = [
            self.launch(remote(mine, own, row_send.at[i, k], row_recv.at[i, k], device))
            for k, device in enumerate(self.row)
        ]
        keep = pltpu.make_async_copy(mine, own, self.sems[6].at[i])
        keep.start()
        self.first[i].append(keep)

    def side(self, i, k, block, device):
        return self.launch(remote(block, block, self.sems[2].at[i, k], self.sems[3].at[i, k], device))

    def to_twin(self, i, k, block):
        twin = self.beside[2]
        return self.launch(remote(block, block, self.sems[4].at[i, k], self.sems[5].at[i, k], twin))

    def sideways(self, i):
        _, y, x, c = self.where
        for copy in self.first[i][:-1]:
            copy.wait_recv()
        self.first[i][-1].wait()
        block = self.block(i, y, x, c)
        self.second[i] = [self.side(i, k, block, self.beside[k]) for k in range(2)]
        self.core[i] = [self.to_twin(i, 0, block)]

    def relay(self, i):
        _, y, x, c = self.where
        self.second[i][0].wait_recv()
        self.third[i] = [self.side(i, 2, self.block(i, y, 1 - x, c, 0), self.beside[1])]
        self.core[i].append(self.to_twin(i, 1, self.block(i, y, 1 - x, c)))
        self.second[i][1].wait_recv()
        self.third[i].append(self.side(i, 3, self.block(i, 1 - y, x, c, 1), self.beside[0]))
        self.core[i].append(self.to_twin(i, 2, self.block(i, 1 - y, x, c)))

    def finish(self, i):
        _, y, x, c = self.where
        for copy in self.third[i]:
            copy.wait_recv()
        self.core[i].append(self.to_twin(i, 3, self.block(i, 1 - y, 1 - x, c)))

    def receive(self, i):
        for copy in self.core[i]:
            copy.wait_recv()

    def begin(self, ahead):
        self.ahead = ahead
        for i in range(ahead):
            self.spread(i)

    def advance(self):
        t, count = self.step, len(self.chunks)
        self.step += 1
        if t < count:
            self.sideways(t)
        if t + self.ahead < count:
            self.spread(t + self.ahead)
        if 0 <= t - 2 < count:
            self.finish(t - 2)
        if 0 <= t - 3 < count:
            self.receive(t - 3)
        if 0 <= t - 1 < count:
            self.relay(t - 1)

    def end(self):
        for copy in self.started:
            copy.wait_send()


class Totals:
    def __init__(self, split, where, row, beside, count, bufs, sems, put):
        self.split, self.where, self.row, self.beside, self.count = split, where, row, beside, count
        self.staged, self.held, self.low, self.high, self.from_x, self.from_y, self.from_row = bufs
        self.sems, self.put = sems, put
        self.core, self.diagonal, self.aside, self.last = {}, {}, {}, {}
        self.folded = self.crossed = self.joined = self.done = self.swapped = 0

    def room(self, u):
        while self.folded < u - STAGES + 1:
            self.fold_core(self.folded)
        if u >= STAGES:
            self.core[u - STAGES].wait_send()

    def each_row(self, act):
        each(self.split[0], act)

    def swap(self, u):
        c = self.where[3]
        if u >= RING:
            while self.done < u - RING + 1:
                self.turn()
            pl.semaphore_wait(self.sems[6].at[u - RING], len(self.row) + len(self.beside))
        block = self.staged.at[u % STAGES, :, :, :, 1 - c]
        self.core[u] = remote(
            block, self.held.at[u % RING], self.sems[0].at[u], self.sems[1].at[u], self.beside[2]
        )
        self.core[u].start()
        self.swapped = u + 1

    def side(self, u, k, block, target, device):
        copy = remote(block, target, self.sems[2].at[u, k], self.sems[3].at[u, k], device)
        copy.start()
        return copy

    def fold_core(self, u):
        _, y, x, c = self.where
        s, q = u % RING, u % STAGES
        held, half = self.held, TILE // 2
        self.core[u].wait_recv()

        def fold(yy, xx):
            def act(k):
                held[s, k, yy, xx] = held[s, k, yy, xx] + self.staged[q, k, yy, xx, c]

            self.each_row(act)

        fold(1 - y, 1 - x)
        low = held.at[s, :, 1 - y, 1 - x, :, pl.ds(0, half)]
        high = held.at[s, :, 1 - y, 1 - x, :, pl.ds(half, half)]
        self.diagonal[u] = [
            self.side(u, 0, low, self.low.at[s], self.beside[0]),
            self.side(u, 1, high, self.high.at[s], self.beside[1]),
        ]
        fold(1 - y, x)
        fold(y, 1 - x)
        fold(y, x)
        self.folded = u + 1

    def fold_diagonal(self, u):
        _, y, x, _ = self.where
        s, held, half = u % RING, self.held, TILE // 2
        self.diagonal[u][0].wait_recv()

        def act_low(k):
            held[s, k, 1 - y, x, :, :half] = held[s, k, 1 - y, x, :, :half] + self.low[s, k]

        self.each_row(act_low)
        block = held.at[s, :, 1 - y, x]
        self.aside[u] = [self.side(u, 2, block, self.from_y.at[s], self.beside[1])]
        self.diagonal[u][1].wait_recv()

        def act_high(k):
            held[s, k, y, 1 - x, :, half:] = held[s, k, y, 1 - x, :, half:] + self.high[s, k]

        self.each_row(act_high)
        block = held.at[s, :, y, 1 - x]
        self.aside[u].append(self.side(u, 3, block, self.from_x.at[s], self.beside[0]))
        self.crossed = u + 1

    def fold_side(self, u):
        z, y, x, _ = self.where
        s, held, depth = u % RING, self.held, self.split[0]
        for copy in self.aside[u]:
            copy.wait_recv()

        def act(k):
            total = held[s, k, y, x].astype(WIDE) + self.from_x[s, k].astype(WIDE)
            held[s, k, y, x] = (total + self.from_y[s, k].astype(WIDE)).astype(LOW)

        self.each_row(act)
        self.last[u] = []
        for k, device in enumerate(self.row):
            copy = remote(
                held.at[s, (z + k + 1) % depth, y, x],
                self.from_row.at[s, k],
                self.sems[4].at[u, k],
                self.sems[5].at[u, k],
                device,
            )
            copy.start()
            self.last[u].append(copy)
        self.joined = u + 1

    def fold_row(self, u):
        z, y, x, _ = self.where
        s = u % RING
        for copy in self.last[u]:
            copy.wait_recv()
        total = self.held[s, z, y, x].astype(WIDE)
        for k in range(self.split[0] - 1):
            total = total + self.from_row[s, k].astype(WIDE)
        self.put(u, total)
        for copy in self.diagonal[u] + self.aside[u] + self.last[u]:
            copy.wait_send()
        if u + RING < self.count:
            for device in self.row + list(self.beside):
                pl.semaphore_signal(self.sems[6].at[u], inc=1, device_id=device, device_id_type=MESH)
        self.done = u + 1

    def turn(self):
        row, side, cross, core = self.joined, self.crossed, self.folded, self.swapped
        if self.done < row:
            self.fold_row(self.done)
        if self.joined < side:
            self.fold_side(self.joined)
        if self.crossed < cross:
            self.fold_diagonal(self.crossed)
        if self.folded < core:
            self.fold_core(self.folded)

    def end(self):
        while self.done < self.count:
            self.turn()
        for u in range(max(self.count - STAGES, 0), self.count):
            self.core[u].wait_send()


def pairs_kernel(split, shape, *refs):
    frames, groups, valid, block = shape
    it = iter(refs)
    take = lambda n: [next(it) for _ in range(n)]
    (x_in, dy_in, small_in), shards = take(3), take(7)
    out_ref, grad_ref = take(2)
    g_t_in, g_t_out, g_t_lin, g_s_in, g_s_out, g_up, g_down, g_small = take(8)
    small_all, full = next(it), take(7)
    xt, a_t, z_t, p_t, o_t, u_t, dy, x1, x2, a_s, z_s, p_s, o_s, a_m, act_g, slope, acc, at, low = take(19)
    b_recv, db_recv, dt_recv, sent, vec, sums, small_v, tile_v = take(8)
    w_a, w_b, w_up, w_down = take(4)
    bufs = take(7)
    ag_sems, rs_sems = take(7), take(7)
    ex_send, ex_recv, ex_own, load_sem, misc = take(5)

    where, row, beside = place(split)
    z, y, x, c = where
    nz, ny, nx, nc = split
    corner = (z * ny + y, (1 - x) * nc + (1 - c))
    greet(row + list(beside) + [corner])
    rows, width = x1.shape
    span = rows // frames
    pair = 2 * block
    chunk = pair
    mine = x * nc + c
    peers = [(beside[0], (1 - x) * nc + c), (beside[2], x * nc + (1 - c)), (corner, (1 - x) * nc + (1 - c))]
    waiting = []

    def cut(ref, index):
        if len(ref.shape) == 3:
            return ref.at[index]
        return ref.at[pl.ds(pl.multiple_of(index * block, TILE_ROWS), block)]

    def exchange(e, source, target, to_places):
        copies = []
        for f in range(frames):
            for k, (device, index) in enumerate(peers):
                src = f * groups + index if to_places else index * frames + f
                dst = mine * frames + f if to_places else f * groups + mine
                copy = remote(cut(source, src), cut(target, dst), ex_send.at[e, k, f], ex_recv.at[e, k, f], device)
                copy.start()
                copies.append(copy)
            src = f * groups + mine if to_places else mine * frames + f
            dst = mine * frames + f if to_places else f * groups + mine
            own = pltpu.make_async_copy(cut(source, src), cut(target, dst), ex_own.at[e, f])
            own.start()
            copies.append(own)
        return copies

    def arrive(copies):
        for copy in copies:
            copy.wait()

    moved = exchange(0, x_in, xt, True)
    dims = [s.shape for s in shards]
    chunks = [(small_in, small_all, SMALL_ROWS, 0, SMALL_ROWS, 0, LANES)]
    for k in (0, 1, 2, 3, 4):
        chunks.append((shards[k], full[k], dims[k][0], 0, dims[k][0], 0, dims[k][1]))
    half = dims[5][1] // 2
    for k in range(2):
        chunks.append((shards[5], full[5], dims[5][0], 0, dims[5][0], k * half, half))
    half = dims[6][0] // 2
    for k in range(2):
        chunks.append((shards[6], full[6], dims[6][0], k * half, half, 0, dims[6][1]))
    ag = Gather(split, where, row, beside, chunks, ag_sems)
    ag.begin(2)
    loads = {}

    def load(key, source, target):
        copy = pltpu.make_async_copy(source, target, load_sem.at[len(loads)])
        copy.start()
        loads[key] = copy

    load("dy", dy_in, dy)
    load("x", x_in, low)
    sums[...] = jnp.zeros_like(sums)
    wb = [w_b.at[:, :, pl.ds(k * width, width)] for k in range(3)]
    wa = w_a
    for _ in range(4):
        ag.advance()
    load("small", small_all, small_v)
    loads["small"].wait()
    devices = nz * ny * nx * nc
    per_row = devices * SMALL_ROWS // (nz * SMALL_ROWS)

    def small_of(r):
        k, s = r // per_row, r % per_row
        tile = small_v[k, s * SMALL_ROWS : (s + 1) * SMALL_ROWS, :].astype(WIDE)
        return jnp.concatenate([tile, jnp.zeros((SMALL_ROWS, width - LANES), WIDE)], axis=1)

    parts = {}

    def add(key, value):
        parts[key] = parts[key] + value if key in parts else value

    step = width // devices
    for r in range(devices):
        tile = small_of(r)
        add("a", pltpu.roll(tile, r * step, 1) if r else tile)
        for name, times in (("b", 2), ("c", 4)):
            at_row, at_col = r * step * times // width, r * step * times % width
            add((name, at_row), pltpu.roll(tile, at_col, 1) if at_col else tile)
    vec[0:10, :] = parts["a"][0:10]
    for k in range(2):
        vec[T_INB + k : T_INB + k + 1, :] = parts["b", k][10:11]
        vec[S_INB + k : S_INB + k + 1, :] = parts["b", k][11:12]
    for k in range(4):
        vec[E_BIAS + k : E_BIAS + k + 1, :] = parts["c", k][12:13]

    arrive(moved)
    norm_stage(xt, vec, T_GAIN, a_t, chunk)
    ag.advance()
    load("t_in", full[0], wa)
    loads["t_in"].wait()
    inproj_stage(a_t, wa, vec, T_INB, z_t)
    ag.advance()
    load("t_out", full[1], wb[0])
    all_frames = frames * groups
    time_attend(z_t, p_t, o_t, all_frames, block, 0, all_frames // 4)
    ag.advance()
    load("t_lin", full[2], wb[1])
    time_attend(z_t, p_t, o_t, all_frames, block, all_frames // 4, all_frames // 2)

    def store(ref):
        def act(cols, total):
            if len(ref.shape) == 3:
                ref[:, :, cols] = total.reshape(ref.shape[:2] + (-1,)).astype(LOW)
            else:
                ref[:, cols] = total.astype(LOW)

        return act

    loads["t_out"].wait()
    project_stage(o_t, wb[0], vec, T_OUTB, store(u_t))
    loads["t_lin"].wait()
    project_stage(u_t, wb[1], vec, T_LINB, store(sent))
    moved = exchange(1, sent, b_recv, False)
    ag.advance()
    load("s_in", full[3], wa)
    loads["x"].wait()
    arrive(moved)

    def first(k):
        r = tiles(k, chunk)
        x1[r, :] = low[r, :].astype(WIDE) + wide_rows(b_recv, k, chunk)

    each(rows // chunk, first)
    norm_stage(x1, vec, S_GAIN, a_s, chunk)
    loads["s_in"].wait()
    inproj_stage(a_s, wa, vec, S_INB, z_s)
    ag.advance()
    load("s_out", full[4], wb[2])
    heads = width // LANES * frames
    space_attend(z_s, p_s, o_s, frames, span, valid, block, 0, heads // 2)
    ag.advance()
    half = w_up.shape[2] // 2
    load("up0", full[5].at[:, :, pl.ds(0, half)], w_up.at[:, :, pl.ds(0, half)])
    space_attend(z_s, p_s, o_s, frames, span, valid, block, heads // 2, heads)

    def add_x1(cut, total):
        x2[:, cut] = x1[:, cut] + total

    loads["s_out"].wait()
    project_stage(o_s, wb[2], vec, S_OUTB, add_x1)
    norm_stage(x2, vec, F_GAIN, a_m, chunk)
    ag.advance()
    load("up1", full[5].at[:, :, pl.ds(half, half)], w_up.at[:, :, pl.ds(half, half)])
    loads["up0"].wait()
    expand_stage(a_m, w_up, vec, act_g, slope, 0, half // TILE)
    ag.advance()
    loads["up1"].wait()
    expand_stage(a_m, w_up, vec, act_g, slope, half // TILE, 2 * half // TILE)
    loads["dy"].wait()

    per = width // TILE
    plan = {}
    order = [(g_up, 4 * per), (g_s_out, per), (g_s_in, 3 * per), (g_t_lin, per), (g_t_out, per), (g_t_in, 3 * per), (g_small, 1)]
    units, sub = per - 1, SUB
    homes = {}
    for out, count in order:
        for k in range(count):
            if sub == SUB:
                units, sub = units + 1, 0
                plan[units] = []
            plan[units].append((out, k))
            homes[id(out), k] = (units, sub)
            sub += 1
    count = units + 1
    step_rows = g_up.shape[0]

    def put(u, total):
        if u < per:
            g_down[:, u * TILE : (u + 1) * TILE] = total
            return
        for b, (out, k) in enumerate(plan[u]):
            out[:, k * TILE : (k + 1) * TILE] = total[b * step_rows : (b + 1) * step_rows]

    rs = Totals(split, where, row, beside, count, bufs, rs_sems, put)
    staged = bufs[0]

    def down(k):
        at[:width, :] = act_g[:, tiles(k, width)].T
        for u in range(per):
            total = dot(at[:width, :], dy[:, u * TILE : (u + 1) * TILE])
            staged[u, k] = total.reshape((ny, nx, nc, -1, TILE)).astype(LOW)

    each(nz, down)
    ones = jnp.ones((16, rows), LOW)
    sums[R_BIAS : R_BIAS + 1, :] = dot(ones, dy[...])[:1]
    for u in range(per):
        rs.swap(u)
    ag.advance()
    load("down", full[6], w_down)
    assert ag.step == len(chunks) + 3

    def grads(out, dz_ref, table):
        count = out.shape[1] // TILE
        act_bias = bias_rows(sums, table, width)
        k = 0
        while k < count:
            u, b0 = homes[id(out), k]
            n = min(SUB - b0, count - k)
            if b0 == 0:
                rs.room(u)

            def act(i, k=k, u=u, b0=b0, n=n):
                t = k + i
                total = dot(at[...], dz_ref[:, tiles(t)])
                act_bias(t, total[width : width + 1])
                tile_v[...] = total[:width]
                for b in range(n):

                    @pl.when(i == b)
                    def _():
                        low_row = (b0 + b) * step_rows
                        staged[u % STAGES, :, :, :, :, low_row : low_row + step_rows, :] = (
                            tile_v[...].reshape((nz, ny, nx, nc, step_rows, TILE)).astype(LOW)
                        )

            each(n, act)
            k += n
            if b0 + n == SUB:
                rs.swap(u)
                rs.turn()

    loads["down"].wait()
    reduce_back_stage(dy, w_down, slope, slope)

    hidden = act_g.shape[1]
    rs.turn()
    reduce_stage(act_g, w_down, vec, x2, store(low))
    out_copy = pltpu.make_async_copy(low, out_ref, misc.at[0])
    out_copy.start()
    rs.turn()
    turn_stage(a_m, at)
    grads(g_up, slope, [E_BIAS + k for k in range(hidden // width)])
    back_stage(slope, w_up, acc)
    out_copy.wait()

    def put_x2(k, dv):
        r = tiles(k, chunk)
        total = dy[r, :].astype(WIDE) + dv
        x2[r, :] = total
        low[r, :] = total.astype(LOW)

    norm_back_stage(x2, vec, F_GAIN, acc, sums, chunk, put_x2)
    load("t_in again", full[0], w_up.at[:, :, pl.ds(0, 3 * width)])
    turn_stage(o_s, at)
    grads(g_s_out, low, [S_OUTB])
    back_stage(low, wb[2], acc)
    low[...] = acc[...].astype(LOW)
    rs.turn()
    dz = slope.at[:, pl.ds(0, 3 * width)]
    space_attend_back(z_s, p_s, low, dz, frames, span, 0, heads // 2)
    rs.turn()
    space_attend_back(z_s, p_s, low, dz, frames, span, heads // 2, heads)
    rs.turn()
    back_stage(dz, wa, acc)

    def put_x1(k, dv):
        r = tiles(k, chunk)
        total = x2[r, :] + dv
        x1[r, :] = total
        put_rows(sent, k, chunk, total)

    norm_back_stage(x1, vec, S_GAIN, acc, sums, chunk, put_x1)
    moved = exchange(2, sent, db_recv, True)
    turn_stage(a_s, at)
    grads(g_s_in, dz, [S_INB, None, S_INB + 1])
    turn_stage(u_t, at)
    arrive(moved)

    def flat(k):
        low[tiles(k, chunk), :] = wide_rows(db_recv, k, chunk).astype(LOW)

    each(rows // chunk, flat)
    grads(g_t_lin, low, [T_LINB])
    back_stage(low, wb[1], acc)
    low[...] = acc[...].astype(LOW)
    rs.turn()
    turn_stage(o_t, at)
    grads(g_t_out, low, [T_OUTB])
    back_stage(low, wb[0], acc)
    low[...] = acc[...].astype(LOW)
    rs.turn()
    time_attend_back(z_t, p_t, low, dz, x2, acc, all_frames, block, rs.turn)
    loads["t_in again"].wait()
    back_stage(dz, w_up.at[:, :, pl.ds(0, 3 * width)], acc)

    def put_t(k, dv):
        put_rows(sent, k, chunk, dv)

    norm_back_stage(xt, vec, T_GAIN, acc, sums, chunk, put_t)
    moved = exchange(3, sent, dt_recv, False)
    rs.turn()
    turn_stage(a_t, at)
    grads(g_t_in, dz, [T_INB, None, T_INB + 1])

    u, b0 = homes[id(g_small), 0]
    if b0 == 0:
        rs.room(u)
    low_row = b0 * step_rows
    lane = lax.broadcasted_iota(jnp.int32, (step_rows, width), 0)
    base = jnp.concatenate([sums[0:10, :], jnp.zeros((step_rows - 10, width), WIDE)], axis=0)

    def placed(pieces):
        out = jnp.zeros((step_rows, width), WIDE)
        for target, source in pieces:
            out = jnp.where(lane == target, sums[source : source + 1, :], out)
        return out

    twos = [placed([(10, T_INB + k), (11, S_INB + k)]) for k in range(2)]
    fours = [placed([(12, E_BIAS + k)]) for k in range(4)]
    for r in range(devices):
        def shifted(value, at_col):
            return (pltpu.roll(value, width - at_col, 1) if at_col else value)[:, :TILE]

        a = shifted(base, r * step)
        b = shifted(twos[2 * r * step // width], 2 * r * step % width)
        d = shifted(fours[4 * r * step // width], 4 * r * step % width)
        tile = jnp.where(lane[:, :TILE] < 10, a, jnp.where(lane[:, :TILE] < 12, b, d))
        slot = (r // (ny * nx * nc), r // (nx * nc) % ny, r // nc % nx, r % nc)
        staged[(u % STAGES,) + slot + (slice(low_row, low_row + step_rows), slice(None))] = tile.astype(LOW)
    rs.swap(u)
    rs.turn()
    arrive(moved)

    def last(k):
        r = tiles(k, chunk)
        x1[r, :] = x1[r, :] + wide_rows(dt_recv, k, chunk)

    each(rows // chunk, last)
    grad_copy = pltpu.make_async_copy(x1, grad_ref, misc.at[1])
    grad_copy.start()
    rs.end()
    ag.end()
    grad_copy.wait()


def whole_layer(split, shape, x, dy, small, shards):
    frames, groups, valid, block = shape
    rows, width = x.shape
    nz, ny, nx, nc = split
    slots = ny * nx * nc
    low, wide = LOW, WIDE
    hidden = shards[5].shape[1]
    step = shards[0].shape[0]
    shapes = [(item.shape, wide) for item in shards] + [((step, TILE), wide)]
    token, full = ((rows, width), low), ((rows, width), wide)
    gathered = [((nz, slots * SMALL_ROWS, LANES), low)]
    gathered += [((nz, slots * item.shape[0], item.shape[1]), low) for item in shards]
    hbm = pl.BlockSpec(memory_space=pl.ANY)
    vmem = pl.BlockSpec(memory_space=pltpu.VMEM)
    outs = [token, full] + shapes + gathered
    out_specs = [hbm, hbm] + [vmem] * len(shapes) + [hbm] * len(gathered)
    span = rows // frames
    three, big = ((rows, 3 * width), low), ((rows, hidden), low)
    cuts = ((frames * groups, block, width), low)
    scratch = [cuts, token, three, ((frames * groups, rows, LANES), low), token, token, token, full, full]
    scratch += [token, three, ((frames * HEADS, span, span), low), token, token, big, big, full]
    scratch += [((width + 16, rows), low), token, cuts, cuts, cuts, cuts, ((24, width), wide), ((24, width), wide)]
    scratch += [gathered[0], ((width, TILE), wide)]
    scratch += [gathered[1], gathered[1], gathered[6], gathered[7]]
    deep = SUB * step
    scratch += [((STAGES, nz, ny, nx, nc, deep, TILE), low), ((RING, nz, ny, nx, deep, TILE), low)]
    scratch += [((RING, nz, deep, TILE // 2), low)] * 2 + [((RING, nz, deep, TILE), low)] * 2
    scratch += [((RING, nz - 1, deep, TILE), low)]
    sem = pltpu.SemaphoreType.DMA
    chunks, units = 10, (hidden // TILE + 5 * width * 3 // TILE) // SUB + 8
    sems = [sem((chunks, nz - 1))] * 2 + [sem((chunks, 4))] * 4 + [sem((chunks,))]
    sems += [sem((units,))] * 2 + [sem((units, 4))] * 2 + [sem((units, nz - 1))] * 2
    sems += [pltpu.SemaphoreType.REGULAR((units,))]
    sems += [sem((4, 3, frames))] * 2 + [sem((4, frames)), sem((12,)), sem((2,))]
    result = pl.pallas_call(
        functools.partial(pairs_kernel, split, shape),
        out_shape=[jax.ShapeDtypeStruct(s, kind) for s, kind in outs],
        in_specs=[hbm] * (3 + len(shards)),
        out_specs=out_specs,
        scratch_shapes=[pltpu.VMEM(s, kind) for s, kind in scratch] + sems,
        compiler_params=pltpu.CompilerParams(
            collective_id=0, has_side_effects=True, vmem_limit_bytes=63 << 20
        ),
        name="whole_layer",
    )(x, dy, small, *shards)
    return result[:10]


VECTOR_ROWS = (0, 1, 10, 2, 3, 4, 5, 12, 6, 7, 8, 14, 9)


SMALL_PLACES = {row: (row, 0) for row in range(10)} | {10: (10, 0), 12: (11, 0), 14: (12, 0)}


def pack_small(vectors):
    rows = {SMALL_PLACES[at][0]: item for at, item in zip(VECTOR_ROWS, vectors)}
    lines = [jnp.pad(rows[k], (0, LANES - rows[k].shape[0])) for k in range(len(rows))]
    lines += [jnp.zeros((LANES,), LOW)] * (SMALL_ROWS - len(lines))
    return jnp.stack(lines)


def sum_native(terms):
    received = [
        lax.all_to_all(
            item.astype(LOW), "clip", split_axis=0, concat_axis=0, tiled=True
        ).astype(WIDE)
        for item in stack_rows(terms, lax.axis_size("clip"))
    ]
    return [
        lax.psum_scatter(item.astype(LOW), "frame", scatter_dimension=0, tiled=True).astype(WIDE)
        for item in fold_rows(received)
    ]


def on_device(
    video_tokens,
    time_gain,
    time_shift,
    time_inproj,
    time_inbias,
    time_outproj,
    time_outbias,
    time_linear,
    time_linbias,
    space_gain,
    space_shift,
    space_inproj,
    space_inbias,
    space_outproj,
    space_outbias,
    feed_gain,
    feed_shift,
    expand_weight,
    expand_bias,
    reduce_weight,
    reduce_bias,
    cotangent,
):
    split = inner_split(time_gain.shape[0])
    params = [
        time_gain,
        time_shift,
        time_inproj,
        time_inbias,
        time_outproj,
        time_outbias,
        time_linear,
        time_linbias,
        space_gain,
        space_shift,
        space_inproj,
        space_inbias,
        space_outproj,
        space_outbias,
        feed_gain,
        feed_shift,
        expand_weight,
        expand_bias,
        reduce_weight,
        reduce_bias,
    ]
    frames, places, width = video_tokens.shape[1:]
    groups = lax.axis_size("frame")
    valid = places // groups
    block = -(-valid // TILE_ROWS) * TILE_ROWS
    rows = frames * groups * block

    def padded(tokens):
        cut = tokens.reshape((frames, groups, valid, width))
        return jnp.pad(cut, ((0, 0), (0, 0), (0, block - valid), (0, 0)))

    def to_places(tokens):
        return lax.all_to_all(
            tokens.reshape((frames, groups, block, width)),
            "frame",
            split_axis=1,
            concat_axis=0,
            tiled=True,
        ).reshape((rows, width))

    def to_frames(tokens):
        return lax.all_to_all(
            tokens.reshape((frames * groups, 1, block, width)),
            "frame",
            split_axis=0,
            concat_axis=1,
            tiled=True,
        ).reshape((rows, width))

    def trimmed(tokens):
        cut = tokens.reshape((frames, groups, block, width))[:, :, :valid]
        return cut.reshape((1, frames, places, width))

    def weight(item):
        return item.reshape((4, -1, item.shape[1]))

    if split is not None:
        small = pack_small([item for item in params if item.ndim == 1])
        layer_out, input_grad, *sums = whole_layer(
            split,
            (frames, groups, valid, block),
            padded(video_tokens).reshape((rows, width)),
            padded(cotangent).reshape((rows, width)),
            small,
            [item for item in params if item.ndim == 2],
        )
        wide, thin = iter(sums[:7]), iter(zip(VECTOR_ROWS, [item for item in params if item.ndim == 1]))
        summed = []
        for item in params:
            if item.ndim == 2:
                summed.append(next(wide))
            else:
                at, like = next(thin)
                row, _ = SMALL_PLACES[at]
                summed.append(sums[7][row, : like.shape[0]])
        return (trimmed(layer_out), trimmed(input_grad)) + tuple(summed)

    full = [lax.all_gather(item, ("clip", "frame"), axis=0, tiled=True) for item in params]
    thin = [item for item in full if item.ndim == 1]
    t_in, t_out, t_lin, s_in, s_out, w_up, w_down = [weight(item) for item in full if item.ndim == 2]
    pieces = sorted(zip(VECTOR_ROWS, thin), key=lambda pair: pair[0])
    vec = jnp.concatenate([item.reshape((-1, width)) for _, item in pieces], axis=0)
    vec = jnp.pad(vec, ((0, 24 - vec.shape[0]), (0, 0))).astype(WIDE)
    tokens, d_out = padded(video_tokens), padded(cotangent)
    own = tokens.reshape((rows, width))
    placed = to_places(tokens)
    b_t, a_t, z_t, p_t, o_t, u_t = time_forward(block, placed, vec, t_in, t_out, t_lin)
    layer_out, d_x1, d_b, g_s_in, g_s_out, g_up, g_down, sums_s = space_layer(
        (frames, valid, block),
        own,
        to_frames(b_t),
        d_out.reshape((rows, width)),
        vec,
        s_in,
        s_out,
        w_up,
        w_down,
    )
    d_t, g_t_in, g_t_out, g_t_lin, sums_t = time_backward(
        block, to_places(d_b), placed, a_t, z_t, p_t, o_t, u_t, vec, t_in, t_out, t_lin
    )
    input_grad = d_x1 + to_frames(d_t).astype(WIDE)
    sums = sums_s + sums_t
    wide = iter(
        [item.reshape((-1, width if item is g_down else item.shape[2])) for item in
         (g_t_in, g_t_out, g_t_lin, g_s_in, g_s_out, g_up, g_down)]
    )
    rows_of = iter(VECTOR_ROWS)
    terms = []
    for item in params:
        if item.ndim == 2:
            terms.append(next(wide))
        else:
            at = next(rows_of)
            count = item.shape[0] * lax.axis_size(("clip", "frame")) // width
            terms.append(sums[at : at + count].reshape(-1))
    summed = sum_native(terms)
    return (trimmed(layer_out), trimmed(input_grad)) + tuple(summed)


def solution(mesh):
    return jax.shard_map(
        on_device,
        mesh=mesh,
        in_specs=(
            P("clip", "frame", None, None),
            P(("clip", "frame")),
            P(("clip", "frame")),
            P(("clip", "frame"), None),
            P(("clip", "frame")),
            P(("clip", "frame"), None),
            P(("clip", "frame")),
            P(("clip", "frame"), None),
            P(("clip", "frame")),
            P(("clip", "frame")),
            P(("clip", "frame")),
            P(("clip", "frame"), None),
            P(("clip", "frame")),
            P(("clip", "frame"), None),
            P(("clip", "frame")),
            P(("clip", "frame")),
            P(("clip", "frame")),
            P(("clip", "frame"), None),
            P(("clip", "frame")),
            P(("clip", "frame"), None),
            P(("clip", "frame")),
            P("clip", "frame", None, None),
        ),
        out_specs=(
            P("clip", "frame", None, None),
            P("clip", "frame", None, None),
            P(("clip", "frame")),
            P(("clip", "frame")),
            P(("clip", "frame"), None),
            P(("clip", "frame")),
            P(("clip", "frame"), None),
            P(("clip", "frame")),
            P(("clip", "frame"), None),
            P(("clip", "frame")),
            P(("clip", "frame")),
            P(("clip", "frame")),
            P(("clip", "frame"), None),
            P(("clip", "frame")),
            P(("clip", "frame"), None),
            P(("clip", "frame")),
            P(("clip", "frame")),
            P(("clip", "frame")),
            P(("clip", "frame"), None),
            P(("clip", "frame")),
            P(("clip", "frame"), None),
            P(("clip", "frame")),
        ),
        check_vma=False,
    )
```

```python
import functools

import jax
import jax.numpy as jnp
from jax import lax
from jax.experimental import pallas as pl
from jax.experimental.pallas import tpu as pltpu
from jax.sharding import PartitionSpec as P

MESH = pl.DeviceIdType.MESH
TILE_ROWS = 8
LOW = jnp.bfloat16
WIDE = jnp.float32
HEADS = 12
norm_eps = 1e-06
LANES = 128
TILE = 256
T_GAIN, T_SHIFT, T_OUTB, T_LINB, S_GAIN, S_SHIFT, S_OUTB, F_GAIN, F_SHIFT, R_BIAS, T_INB, S_INB, E_BIAS = 0, 1, 2, 3, 4, 5, 6, 7, 8, 9, 10, 12, 14


def dot(a, b):
    return lax.dot_general(a, b, (((1,), (0,)), ((), ())), preferred_element_type=WIDE)


def dot_nt(a, b):
    return lax.dot_general(a, b, (((1,), (1,)), ((), ())), preferred_element_type=WIDE)


def each(count, act, start=0, pump=None, every=1):
    def step(k, carry):
        act(k)
        return carry

    stride = count - start if pump is None else every
    for at in range(start, count, stride):
        lax.fori_loop(at, min(at + stride, count), step, 0)
        if pump is not None:
            pump()


def tiles(k, size=TILE):
    return pl.ds(pl.multiple_of(k * size, size), size)


def columns(w_ref, cut):
    block = w_ref[:, :, cut]
    return block.reshape((block.shape[0] * block.shape[1], block.shape[2]))


def wide_rows(ref, k, size):
    if len(ref.shape) == 2:
        return ref[tiles(k, size), :].astype(WIDE)
    per = size // ref.shape[1]
    block = ref[pl.ds(k * per, per), :, :].astype(WIDE)
    return block.reshape((size, ref.shape[2]))


def put_rows(ref, k, size, value):
    if len(ref.shape) == 2:
        ref[tiles(k, size), :] = value.astype(ref.dtype)
    else:
        per = size // ref.shape[1]
        ref[pl.ds(k * per, per), :, :] = value.reshape((per,) + ref.shape[1:]).astype(ref.dtype)


def normal(x):
    center = x - jnp.mean(x, axis=-1, keepdims=True)
    inverse = lax.rsqrt(jnp.mean(center * center, axis=-1, keepdims=True) + norm_eps)
    return center * inverse, inverse


def norm_stage(x_ref, vec, gain_row, a_ref, block, pump=None):
    gain, shift = vec[gain_row : gain_row + 1, :], vec[gain_row + 1 : gain_row + 2, :]

    def act(k):
        unit, _ = normal(wide_rows(x_ref, k, block))
        a_ref[tiles(k, block), :] = (unit * gain + shift).astype(LOW)

    each(a_ref.shape[0] // block, act, 0, pump, 2)


def norm_back_stage(x_ref, vec, gain_row, da_ref, sums, block, store):
    gain = vec[gain_row : gain_row + 1, :]
    width = da_ref.shape[1]

    def step(k, carry):
        unit, inverse = normal(wide_rows(x_ref, k, block))
        da = da_ref[tiles(k, block), :]
        e = da * gain
        dv = inverse * (
            e
            - jnp.mean(e, axis=-1, keepdims=True)
            - unit * jnp.mean(e * unit, axis=-1, keepdims=True)
        )
        store(k, dv)
        grad_gain, grad_shift = carry
        fold = lambda v: jnp.sum(v.reshape(block // 8, 8, width), axis=0)
        return grad_gain + fold(da * unit), grad_shift + fold(da)

    zero = jnp.zeros((8, width), WIDE)
    grad_gain, grad_shift = lax.fori_loop(0, da_ref.shape[0] // block, step, (zero, zero))
    sums[gain_row : gain_row + 1, :] = jnp.sum(grad_gain, axis=0, keepdims=True)
    sums[gain_row + 1 : gain_row + 2, :] = jnp.sum(grad_shift, axis=0, keepdims=True)


def inproj_stage(a_ref, w_ref, vec, bias_row, z_ref, pump=None):
    width = a_ref.shape[1]
    for part in range(3):

        def act(k, part=part):
            inner = tiles(k)
            cut = pl.ds(pl.multiple_of(part * width + k * TILE, TILE), TILE)
            total = dot(a_ref[...], columns(w_ref, cut))
            if part != 1:
                row = bias_row + part // 2
                total = total + vec[row : row + 1, inner]
            z_ref[:, cut] = total.astype(LOW)

        each(width // TILE, act, 0, pump, 3)


def project_stage(a_ref, w_ref, vec, bias_row, store, pump=None):
    def act(k):
        cut = tiles(k)
        store(cut, dot(a_ref[...], columns(w_ref, cut)) + vec[bias_row : bias_row + 1, cut])

    each(w_ref.shape[2] // TILE, act, 0, pump, 3)


def back_stage(dz_ref, w_ref, acc_ref, pump=None):
    width = acc_ref.shape[1]
    parts = w_ref.shape[2] // width
    acc_ref[...] = dot_nt(dz_ref[:, :width], columns(w_ref, pl.ds(0, width)))

    def act(k):
        cut = tiles(k + 1, width)
        acc_ref[...] = acc_ref[...] + dot_nt(dz_ref[:, cut], columns(w_ref, cut))

    if parts > 1:
        each(parts - 1, act, 0, pump)


def turn_stage(a_ref, at_ref, pump=None):
    width = a_ref.shape[1]

    def act(k):
        at_ref[tiles(k), :] = a_ref[:, tiles(k)].T

    each(width // TILE, act, 0, pump, 3)
    at_ref[width:, :] = jnp.ones((at_ref.shape[0] - width, at_ref.shape[1]), LOW)


def weight_stage(at_ref, dz_ref, g_ref, bias):
    depth, rows, _ = g_ref.shape
    full = depth * rows

    def act(k):
        cut = tiles(k)
        total = dot(at_ref[...], dz_ref[:, cut])
        g_ref[:, :, cut] = total[:full].astype(LOW).reshape((depth, rows, TILE))
        bias(k, total[full : full + 1])

    each(g_ref.shape[2] // TILE, act)


def bias_rows(sums, table, width):
    def act(k, total):
        per = width // TILE
        for part, row in enumerate(table):
            if row is None:
                continue

            @pl.when((k >= part * per) & (k < (part + 1) * per))
            def _():
                sums[row : row + 1, tiles(k - part * per)] = total

    return act


def low_head(rows):
    lane = lax.broadcasted_iota(jnp.int32, (rows, LANES), 1)
    return lane < LANES // 2


def space_attend(z_ref, p_ref, o_ref, frames, rows, valid, block, start=0, stop=None, pump=None):
    width = o_ref.shape[1]
    pairs = width // LANES
    scale = (LANES // 2) ** -0.5

    def act(step):
        f, pair = step // pairs, step % pairs
        span = tiles(f, rows)
        q = z_ref[span, pl.ds(pl.multiple_of(pair * LANES, LANES), LANES)]
        k = z_ref[span, pl.ds(pl.multiple_of(width + pair * LANES, LANES), LANES)]
        v = z_ref[span, pl.ds(pl.multiple_of(2 * width + pair * LANES, LANES), LANES)]
        first = low_head(rows)
        vt = v.T
        keep = lax.broadcasted_iota(jnp.int32, (rows, rows), 0) % block < valid
        outs = []
        for side in range(2):
            mine = first if side == 0 else ~first
            scores = dot_nt(k, jnp.where(mine, q, jnp.zeros_like(q))) * scale
            scores = jnp.where(keep, scores, -1e30)
            e = jnp.exp(scores - jnp.max(scores, axis=0, keepdims=True))
            p = (e * (1.0 / jnp.sum(e, axis=0, keepdims=True))).astype(LOW)
            p_ref[2 * step + side] = p
            outs.append(dot(vt, p))
        top = lax.broadcasted_iota(jnp.int32, (LANES, rows), 0) < LANES // 2
        o = jnp.where(top, outs[0], outs[1]).T
        o_ref[span, pl.ds(pl.multiple_of(pair * LANES, LANES), LANES)] = o.astype(LOW)

    each(frames * pairs if stop is None else stop, act, start, pump, 2)


def space_attend_back(z_ref, p_ref, do_ref, dz_ref, frames, rows, start=0, stop=None, pump=None):
    width = do_ref.shape[1]
    pairs = width // LANES
    scale = (LANES // 2) ** -0.5

    def act(step):
        f, pair = step // pairs, step % pairs
        span = tiles(f, rows)
        cut_q = pl.ds(pl.multiple_of(pair * LANES, LANES), LANES)
        cut_k = pl.ds(pl.multiple_of(width + pair * LANES, LANES), LANES)
        cut_v = pl.ds(pl.multiple_of(2 * width + pair * LANES, LANES), LANES)
        q, k, v, do = z_ref[span, cut_q], z_ref[span, cut_k], z_ref[span, cut_v], do_ref[span, cut_q]
        kt = k.T
        first = low_head(rows)
        dk = dv = None
        turned = []
        for side in range(2):
            mine = first if side == 0 else ~first
            q_side = jnp.where(mine, q, jnp.zeros_like(q))
            do_side = jnp.where(mine, do, jnp.zeros_like(do))
            p_low = p_ref[2 * step + side]
            p = p_low.astype(WIDE)
            dp = dot_nt(v, do_side)
            inner = jnp.sum(dp * p, axis=0, keepdims=True)
            ds = (p * (dp - inner)).astype(LOW)
            dv_side, dk_side = dot(p_low, do_side), dot(ds, q_side)
            dv = dv_side if dv is None else dv + dv_side
            dk = dk_side if dk is None else dk + dk_side
            turned.append(dot(kt, ds))
        top = lax.broadcasted_iota(jnp.int32, (LANES, rows), 0) < LANES // 2
        dq = jnp.where(top, turned[0], turned[1]).T
        dz_ref[span, cut_q] = (dq * scale).astype(LOW)
        dz_ref[span, cut_k] = (dk * scale).astype(LOW)
        dz_ref[span, cut_v] = dv.astype(LOW)

    each(frames * pairs if stop is None else stop, act, start, pump, 2)


def head_sum(width):
    row = lax.broadcasted_iota(jnp.int32, (width, LANES), 0) // (width // HEADS)
    col = lax.broadcasted_iota(jnp.int32, (width, LANES), 1)
    return (row == col).astype(WIDE).astype(LOW)


def head_spread(width):
    row = lax.broadcasted_iota(jnp.int32, (LANES, width), 0)
    col = lax.broadcasted_iota(jnp.int32, (LANES, width), 1) // (width // HEADS)
    return (row == col).astype(WIDE).astype(LOW)


def by_head(product, pick):
    high = product.astype(LOW)
    rest = (product - high.astype(WIDE)).astype(LOW)
    return dot(high, pick) + dot(rest, pick)


def time_attend(z_ref, p_ref, o_ref, frames, block, start=0, stop=None, pump=None):
    width = o_ref.shape[1]
    scale = (width // HEADS) ** -0.5
    pick, spread = head_sum(width), head_spread(width)
    spans = [slice(k * block, (k + 1) * block) for k in range(frames)]

    def act(pair):
        rows = tiles(pair, 2 * block)
        q = z_ref[rows, :width].astype(WIDE)
        scores = [[], []]
        for span in spans:
            k = z_ref[span, width : 2 * width].astype(WIDE)
            for half in range(2):
                scores[half].append(by_head(q[spans[half]] * k, pick) * scale)
        probs = []
        for half in range(2):
            top = functools.reduce(jnp.maximum, scores[half])
            e = [jnp.exp(s - top) for s in scores[half]]
            inverse = 1.0 / functools.reduce(jnp.add, e)
            probs.append([item * inverse for item in e])
        out = [jnp.zeros((block, width), WIDE)] * 2
        for k, span in enumerate(spans):
            v = z_ref[span, 2 * width :].astype(WIDE)
            for half in range(2):
                p = probs[half][k]
                p = p.astype(LOW)
                p_ref[2 * pair + half, span, :] = p
                out[half] = out[half] + dot(p, spread) * v
        o_ref[rows, :] = jnp.concatenate(out, axis=0).astype(LOW)

    each(frames // 2 if stop is None else stop, act, start, pump)


def time_attend_back(z_ref, p_ref, do_ref, dz_ref, dk_ref, dv_ref, frames, block, pump=None):
    width = do_ref.shape[1]
    scale = (width // HEADS) ** -0.5
    pick, spread = head_sum(width), head_spread(width)
    spans = [slice(k * block, (k + 1) * block) for k in range(frames)]
    dk_ref[...] = jnp.zeros_like(dk_ref)
    dv_ref[...] = jnp.zeros_like(dv_ref)

    def act(pair):
        rows = tiles(pair, 2 * block)
        do = do_ref[rows, :].astype(WIDE)
        q = z_ref[rows, :width].astype(WIDE)
        dps = [[], []]
        inner = [jnp.zeros((block, LANES), WIDE)] * 2
        for span in spans:
            v = z_ref[span, 2 * width :].astype(WIDE)
            for half in range(2):
                dp = by_head(do[spans[half]] * v, pick)
                inner[half] = inner[half] + dp * p_ref[2 * pair + half, span, :].astype(WIDE)
                dps[half].append(dp)
        dq = [jnp.zeros((block, width), WIDE)] * 2
        for at, span in enumerate(spans):
            k = z_ref[span, width : 2 * width].astype(WIDE)
            dk, dv = dk_ref[span, :], dv_ref[span, :]
            for half in range(2):
                p = p_ref[2 * pair + half, span, :]
                ds = dot((p.astype(WIDE) * (dps[half][at] - inner[half])).astype(LOW), spread)
                dq[half] = dq[half] + ds * k
                dk = dk + ds * q[spans[half]]
                dv = dv + dot(p, spread) * do[spans[half]]
            dk_ref[span, :] = dk
            dv_ref[span, :] = dv
        dz_ref[rows, :width] = (jnp.concatenate(dq, axis=0) * scale).astype(LOW)

    each(frames // 2, act, 0, pump)

    def out(pair):
        rows = tiles(pair, 2 * block)
        dz_ref[rows, width : 2 * width] = (dk_ref[rows, :] * scale).astype(LOW)
        dz_ref[rows, 2 * width :] = dv_ref[rows, :].astype(LOW)

    each(frames // 2, out)


def expand_stage(a_ref, w_ref, vec, g_ref, slope_ref, start=0, stop=None, pump=None):
    width = a_ref.shape[1]
    per = width // TILE

    def act(k):
        cut = tiles(k)
        h = dot(a_ref[...], columns(w_ref, cut))
        inner = tiles(k % per)
        bias = vec[pl.ds(E_BIAS + k // per, 1), inner]
        h = h + bias
        cdf = 0.5 * (1.0 + lax.erf(h * (0.5 ** 0.5)))
        g_ref[:, cut] = (h * cdf).astype(LOW)
        slope_ref[:, cut] = (cdf + h * (jnp.exp(-0.5 * h * h) * 0.3989422804014327)).astype(LOW)

    each(w_ref.shape[2] // TILE if stop is None else stop, act, start, pump, 2)


def reduce_stage(g_ref, w_ref, vec, x_ref, out_store, pump=None):
    depth, rows, width = w_ref.shape

    def act(k):
        cut = tiles(k)
        total = x_ref[:, cut] + vec[R_BIAS : R_BIAS + 1, cut]
        for z in range(depth):
            total = total + dot(g_ref[:, z * rows : (z + 1) * rows], w_ref[z, :, cut])
        out_store(cut, total)

    each(width // TILE, act, 0, pump, 3)


def reduce_back_stage(dm_ref, w_ref, slope_ref, dh_ref, pump=None):
    depth, rows, _ = w_ref.shape
    per = rows // TILE

    def act(k):
        cut = tiles(k)
        block = w_ref[k // per, tiles(k % per), :]
        dh_ref[:, cut] = (dot_nt(dm_ref[...], block) * slope_ref[:, cut].astype(WIDE)).astype(LOW)

    each(depth * per, act, 0, pump, 4)


def reduce_grad_stage(g_ref, gt_ref, dm_ref, out_ref, sums):
    depth, rows, width = out_ref.shape

    def act(k):
        z, part = k // (rows // TILE), k % (rows // TILE)
        turned = g_ref[:, tiles(k)].T
        gt_ref[...] = turned
        out_ref[z, tiles(part), :] = dot(gt_ref[...], dm_ref[...]).astype(LOW)

    each(depth * rows // TILE, act)
    ones = jnp.ones((16, dm_ref.shape[0]), LOW)
    sums[R_BIAS : R_BIAS + 1, :] = dot(ones, dm_ref[...])[:1]


def vmem_call(body, outs, ins, scratch, name):
    return pl.pallas_call(
        body,
        out_shape=[jax.ShapeDtypeStruct(shape, kind) for shape, kind in outs],
        in_specs=[pl.BlockSpec(memory_space=pltpu.VMEM)] * len(ins),
        out_specs=[pl.BlockSpec(memory_space=pltpu.VMEM)] * len(outs),
        scratch_shapes=[pltpu.VMEM(shape, kind) for shape, kind in scratch],
        compiler_params=pltpu.CompilerParams(vmem_limit_bytes=60 << 20),
        name=name,
    )(*ins)


def time_forward(block, x, vec, w_in, w_out, w_lin):
    rows, width = x.shape
    frames = rows // block

    def body(x_ref, vec_ref, w_in, w_out, w_lin, b_ref, a_ref, z_ref, p_ref, o_ref, u_ref):
        def store(ref):
            def act(cut, total):
                ref[:, cut] = total.astype(LOW)

            return act

        norm_stage(x_ref, vec_ref, T_GAIN, a_ref, 2 * block)
        inproj_stage(a_ref, w_in, vec_ref, T_INB, z_ref)
        time_attend(z_ref, p_ref, o_ref, frames, block)
        project_stage(o_ref, w_out, vec_ref, T_OUTB, store(u_ref))
        project_stage(u_ref, w_lin, vec_ref, T_LINB, store(b_ref))

    token = ((rows, width), LOW)
    outs = [token, token, ((rows, 3 * width), LOW), ((frames, rows, LANES), LOW), token, token]
    return vmem_call(body, outs, (x, vec, w_in, w_out, w_lin), [], "time_forward")


def space_layer(shape, x, b, dy, vec, w_in, w_out, w_up, w_down):
    frames, valid, block = shape
    rows, width = x.shape
    span = rows // frames
    hidden = w_up.shape[2]
    heads_all = frames * HEADS

    def body(x_ref, b_ref, dy_ref, vec_ref, w_in, w_out, w_up, w_down, out_ref, dx1_ref, db_ref,
             g_in, g_out, g_up, g_down, sums, x1, x2, a_s, z_s, p_s, o_s, a_m, act_g, slope, dh, acc, at, gt, low):
        sums[...] = jnp.zeros_like(sums)

        def first(k):
            r = tiles(k, 2 * block)
            x1[r, :] = x_ref[r, :].astype(WIDE) + b_ref[r, :].astype(WIDE)

        each(rows // (2 * block), first)
        norm_stage(x1, vec_ref, S_GAIN, a_s, 2 * block)
        inproj_stage(a_s, w_in, vec_ref, S_INB, z_s)
        space_attend(z_s, p_s, o_s, frames, span, valid, block)

        def add_x1(cut, total):
            x2[:, cut] = x1[:, cut] + total

        project_stage(o_s, w_out, vec_ref, S_OUTB, add_x1)
        norm_stage(x2, vec_ref, F_GAIN, a_m, 2 * block)
        expand_stage(a_m, w_up, vec_ref, act_g, slope)

        def put_out(cut, total):
            out_ref[:, cut] = total.astype(LOW)

        reduce_stage(act_g, w_down, vec_ref, x2, put_out)
        reduce_grad_stage(act_g, gt, dy_ref, g_down, sums)
        reduce_back_stage(dy_ref, w_down, slope, dh)
        turn_stage(a_m, at)
        weight_stage(at, dh, g_up, bias_rows(sums, [E_BIAS + k for k in range(hidden // width)], width))
        back_stage(dh, w_up, acc)

        def put_x2(k, dv):
            r = tiles(k, 2 * block)
            total = dy_ref[r, :].astype(WIDE) + dv
            dx1_ref[r, :] = total
            low[r, :] = total.astype(LOW)

        norm_back_stage(x2, vec_ref, F_GAIN, acc, sums, 2 * block, put_x2)
        turn_stage(o_s, at)
        weight_stage(at, low, g_out, bias_rows(sums, [S_OUTB], width))
        back_stage(low, w_out, acc)
        low[...] = acc[...].astype(LOW)
        dz = dh.at[:, : 3 * width]
        space_attend_back(z_s, p_s, low, dz, frames, span)
        turn_stage(a_s, at)
        weight_stage(at, dz, g_in, bias_rows(sums, [S_INB, None, S_INB + 1], width))
        back_stage(dz, w_in, acc)

        def put_x1(k, dv):
            r = tiles(k, 2 * block)
            total = dx1_ref[r, :] + dv
            dx1_ref[r, :] = total
            db_ref[r, :] = total.astype(LOW)

        norm_back_stage(x1, vec_ref, S_GAIN, acc, sums, 2 * block, put_x1)

    token, full = ((rows, width), LOW), ((rows, width), WIDE)
    outs = [token, full, token] + [(w.shape, LOW) for w in (w_in, w_out, w_up, w_down)] + [(vec.shape, WIDE)]
    scratch = [full, full, token, ((rows, 3 * width), LOW), ((heads_all, span, span), LOW), token, token]
    scratch += [((rows, hidden), LOW)] * 3 + [full, ((width + 16, rows), LOW), ((TILE, rows), LOW), token]
    return vmem_call(body, outs, (x, b, dy, vec, w_in, w_out, w_up, w_down), scratch, "space_layer")


def time_backward(block, db, x, a, z, p, o, u, vec, w_in, w_out, w_lin):
    rows, width = x.shape
    frames = rows // block

    def body(db_ref, x_ref, a_ref, z_ref, p_ref, o_ref, u_ref, vec_ref, w_in, w_out, w_lin,
             dt_ref, g_in, g_out, g_lin, sums, low, dz, dk, dv, acc, at):
        sums[...] = jnp.zeros_like(sums)
        turn_stage(u_ref, at)
        weight_stage(at, db_ref, g_lin, bias_rows(sums, [T_LINB], width))
        back_stage(db_ref, w_lin, acc)
        low[...] = acc[...].astype(LOW)
        turn_stage(o_ref, at)
        weight_stage(at, low, g_out, bias_rows(sums, [T_OUTB], width))
        back_stage(low, w_out, acc)
        low[...] = acc[...].astype(LOW)
        time_attend_back(z_ref, p_ref, low, dz, dk, dv, frames, block)
        turn_stage(a_ref, at)
        weight_stage(at, dz, g_in, bias_rows(sums, [T_INB, None, T_INB + 1], width))
        back_stage(dz, w_in, acc)

        def put(k, dv):
            put_rows(dt_ref, k, 2 * block, dv)

        norm_back_stage(x_ref, vec_ref, T_GAIN, acc, sums, 2 * block, put)

    token, full = ((rows, width), LOW), ((rows, width), WIDE)
    outs = [token] + [(w.shape, LOW) for w in (w_in, w_out, w_lin)] + [(vec.shape, WIDE)]
    scratch = [token, ((rows, 3 * width), LOW), full, full, full, ((width + 16, rows), LOW)]
    return vmem_call(body, outs, (db, x, a, z, p, o, u, vec, w_in, w_out, w_lin), scratch, "time_backward")


def stack_rows(terms, groups):
    return tuple(
        (item.reshape((groups, item.shape[0] // groups) + item.shape[1:]) for item in terms)
    )


def fold_rows(received):
    return tuple((jnp.sum(item, axis=0) for item in received))


def remote(source, target, send, recv, device):
    return pltpu.make_async_remote_copy(
        src_ref=source,
        dst_ref=target,
        send_sem=send,
        recv_sem=recv,
        device_id=device,
        device_id_type=MESH,
    )


def place(split):
    nz, ny, nx, nc = split
    clip, frame = lax.axis_index("clip"), lax.axis_index("frame")
    z, y, x, c = clip // ny, clip % ny, frame // nc, frame % nc

    def mesh_at(z, y, x, c):
        return (z * ny + y, x * nc + c)

    row = [mesh_at((z + step) % nz, y, x, c) for step in range(1, nz)]
    beside = (mesh_at(z, y, 1 - x, c), mesh_at(z, 1 - y, x, c), mesh_at(z, y, x, 1 - c))
    return (z, y, x, c), row, beside


def greet(devices):
    barrier = pltpu.get_barrier_semaphore()
    for device in devices:
        pl.semaphore_signal(barrier, inc=1, device_id=device, device_id_type=MESH)
    pl.semaphore_wait(barrier, len(devices))


def inner_split(rows):
    clips, frames = lax.axis_size("clip"), lax.axis_size("frame")
    if frames == 4 and clips % 2 == 0 and clips > 2 and rows % TILE_ROWS == 0:
        return (clips // 2, 2, 2, 2)
    return None


SMALL_ROWS = 16
RING = 6
AHEAD = 2
PIECES = 2
FIRST = 1
TALL = 4
LATE = 2
LATE_RELAY = 1
LATE_SEND = 5
LATE_STEP = 2
OVER_Y = ()
THIRD = 1
TWO = 1
THREE = 1
TB = 3
STAGES = 3
SUB = 4


class Move:
    def __init__(self, make):
        self.make = make
        make().start()

    def wait(self):
        self.make().wait()

    def wait_recv(self):
        self.make().wait_recv()

    def wait_send(self):
        self.make().wait_send()


class Gather:
    def __init__(self, split, where, row, beside, chunks, sems, ahead):
        self.split, self.where, self.row, self.beside = split, where, row, beside
        self.chunks, self.sems = chunks, sems
        self.started, self.first, self.second, self.third, self.core = [], {}, {}, {}, {}
        self.along = {}
        plain = [i for i, item in enumerate(chunks) if item[7] != 2]
        late = [i for i, item in enumerate(chunks) if item[7] == 2]
        self.here, count = set(), len(plain)
        self.events, self.ends = [], set()

        def then(call, i):
            self.events.append(lambda: call(i))

        for i in plain[:ahead]:
            then(self.spread, i)
        for i in late:
            then(self.sideways, i)
        for t in range(count + 3):
            if t < count:
                then(self.sideways, plain[t])
            if t + ahead < count:
                then(self.spread, plain[t + ahead])
            if 0 <= t - 2 < count:
                then(self.finish, plain[t - 2])
            if 0 <= t - 3 < count:
                then(self.receive, plain[t - 3])
            if 0 <= t - 1 < count:
                then(self.relay_x, plain[t - 1])
                then(self.relay_y, plain[t - 1])
            for k, i in enumerate(late):
                if t == LATE_RELAY:
                    then(self.relay_x, i)
                    then(self.relay_y, i)
                if t == LATE_SEND + LATE_STEP * k:
                    then(self.lengthwise, i)
                if t == count + 1:
                    then(self.finish, i)
                if t == count + 2:
                    then(self.receive, i)
            self.ends.add(len(self.events))
        self.next = 0

    def pump(self, times=1):
        for _ in range(times):
            if self.next < len(self.events):
                self.next += 1
                self.events[self.next - 1]()

    def need(self, i):
        while i not in self.here or self.next not in self.ends:
            self.pump()

    def launch(self, make):
        move = Move(make)
        self.started.append(move)
        return move

    def block(self, i, y, x, c, half=None):
        _, full, per, low, count, start, width, way = self.chunks[i]
        first = c * per + low
        if half is not None and width % (2 * LANES) == 0:
            start, width = start + half * (width // 2), width // 2
        elif half is not None:
            first, count = first + half * (count // 2), count // 2
        rows = pl.ds(pl.multiple_of(first, TILE_ROWS), count)
        places = self.where[0] if way == 2 else slice(None)
        return full.at[places, y * self.split[2] + x, rows, pl.ds(start, width)]

    def own(self, i):
        z, y, x, c = self.where
        _, full, per, low, count, start, width, _ = self.chunks[i]
        rows = pl.ds(pl.multiple_of(c * per + low, TILE_ROWS), count)
        return full.at[z, y * self.split[2] + x, rows, pl.ds(start, width)]

    def core_part(self, i, place):
        c = self.where[3]
        _, full, per, low, count, start, width, _ = self.chunks[i]
        rows = pl.ds(pl.multiple_of(c * per + low, TILE_ROWS), count)
        return full.at[place, :, rows, pl.ds(start, width)]

    def mine(self, i):
        shard, _, _, low, count, start, width, _ = self.chunks[i]
        return shard.at[pl.ds(low, count), pl.ds(start, width)]

    def keep(self, i):
        return Move(lambda: pltpu.make_async_copy(self.mine(i), self.own(i), self.sems[6].at[i]))

    def to_row(self, i, source, target):
        send, recv = self.sems[0], self.sems[1]
        return [
            self.launch(
                lambda k=k, device=device: remote(source(), target(), send.at[i, k], recv.at[i, k], device)
            )
            for k, device in enumerate(self.row)
        ]

    def spread(self, i):
        self.first[i] = self.to_row(i, lambda: self.mine(i), lambda: self.own(i))
        self.first[i].append(self.keep(i))

    def side(self, i, k, block, device):
        send, recv = self.sems[2], self.sems[3]
        return self.launch(lambda: remote(block(), block(), send.at[i, k], recv.at[i, k], device))

    def to_twin(self, i, k, block):
        send, recv, twin = self.sems[4], self.sems[5], self.beside[2]
        return self.launch(lambda: remote(block(), block(), send.at[i, k], recv.at[i, k], twin))

    def sideways(self, i):
        _, y, x, c = self.where
        if self.chunks[i][7] == 2:
            self.first[i] = [self.keep(i)]
        for copy in self.first[i][:-1]:
            copy.wait_recv()
        self.first[i][-1].wait()
        block = lambda: self.block(i, y, x, c)
        self.second[i] = [self.side(i, k, block, self.beside[k]) for k in range(2)]
        self.core[i] = [] if self.chunks[i][7] == 2 else [self.to_twin(i, 0, block)]

    def relay_x(self, i):
        _, y, x, c = self.where
        way = self.chunks[i][7]
        self.second[i][0].wait_recv()
        part = None if way == 1 else 0
        self.third[i] = [self.side(i, 2, lambda: self.block(i, y, 1 - x, c, part), self.beside[1])]
        if way != 2:
            self.core[i].append(self.to_twin(i, 1, lambda: self.block(i, y, 1 - x, c)))

    def relay_y(self, i):
        _, y, x, c = self.where
        way = self.chunks[i][7]
        self.second[i][1].wait_recv()
        if way != 1:
            block = lambda: self.block(i, 1 - y, x, c, 1)
            self.third[i].append(self.side(i, 3, block, self.beside[0]))
        if way != 2:
            self.core[i].append(self.to_twin(i, 2, lambda: self.block(i, 1 - y, x, c)))

    def lengthwise(self, i):
        for copy in self.third[i]:
            copy.wait_recv()
        part = lambda: self.core_part(i, self.where[0])
        self.along[i] = self.to_row(i, part, part)

    def finish(self, i):
        _, y, x, c = self.where
        if self.chunks[i][7] == 2:
            for copy in self.along[i]:
                copy.wait_recv()
            self.core[i].append(self.to_twin(i, 3, lambda: self.core_part(i, slice(None))))
            return
        for copy in self.third[i]:
            copy.wait_recv()
        self.core[i].append(self.to_twin(i, 3, lambda: self.block(i, 1 - y, 1 - x, c)))

    def receive(self, i):
        for copy in self.core[i]:
            copy.wait_recv()
        self.here.add(i)

    def end(self):
        for i in range(len(self.chunks)):
            self.need(i)
        for copy in self.started:
            copy.wait_send()


class Totals:
    def __init__(self, split, where, row, beside, count, bufs, sems, put):
        self.split, self.where, self.row, self.beside, self.count = split, where, row, beside, count
        self.staged, self.held, self.low, self.high, self.from_x, self.from_y, self.from_row = bufs
        self.sems, self.put = sems, put
        self.core, self.diagonal, self.aside, self.last = {}, {}, {}, {}
        self.folded = self.crossing = self.crossed = self.joined = self.done = self.swapped = 0
        self.round = []

    def room(self, u):
        while self.folded < u - STAGES + 1:
            self.pump()
        if u >= STAGES:
            self.core[u - STAGES].wait_send()

    def each_row(self, act):
        each(self.split[0], act)

    def swap(self, u):
        c = self.where[3]
        if u >= RING:
            while self.done < u - RING + 1:
                self.pump()
            pl.semaphore_wait(self.sems[6].at[u - RING], len(self.row) + len(self.beside))
        self.core[u] = Move(
            lambda: remote(
                self.staged.at[u % STAGES, :, :, :, 1 - c],
                self.held.at[u % RING],
                self.sems[0].at[u],
                self.sems[1].at[u],
                self.beside[2],
            )
        )
        self.swapped = u + 1

    def side(self, u, k, block, target, device):
        send, recv = self.sems[2], self.sems[3]
        return Move(lambda: remote(block(), target.at[u % RING], send.at[u, k], recv.at[u, k], device))

    def part(self, u, yy, xx, half=None):
        cols = slice(None) if half is None else pl.ds(half * (TILE // 2), TILE // 2)
        return self.held.at[u % RING, :, yy, xx, :, cols]

    def fold_core(self):
        u = self.folded
        _, y, x, c = self.where
        s, q, held = u % RING, u % STAGES, self.held
        self.core[u].wait_recv()

        def fold(yy, xx):
            def act(k):
                held[s, k, yy, xx] = held[s, k, yy, xx] + self.staged[q, k, yy, xx, c]

            self.each_row(act)

        fold(1 - y, 1 - x)
        self.diagonal[u] = [
            self.side(u, 0, lambda: self.part(u, 1 - y, 1 - x, 0), self.low, self.beside[0]),
            self.side(u, 1, lambda: self.part(u, 1 - y, 1 - x, 1), self.high, self.beside[1]),
        ]
        fold(1 - y, x)
        fold(y, 1 - x)
        fold(y, x)
        self.folded = u + 1

    def fold_low(self):
        u = self.crossing
        _, y, x, _ = self.where
        s, held, half = u % RING, self.held, TILE // 2
        self.diagonal[u][0].wait_recv()

        def act_low(k):
            held[s, k, 1 - y, x, :, :half] = held[s, k, 1 - y, x, :, :half] + self.low[s, k]

        self.each_row(act_low)
        self.aside[u] = [self.side(u, 2, lambda: self.part(u, 1 - y, x), self.from_y, self.beside[1])]
        self.crossing = u + 1

    def fold_high(self):
        u = self.crossed
        _, y, x, _ = self.where
        s, held, half = u % RING, self.held, TILE // 2
        self.diagonal[u][1].wait_recv()

        def act_high(k):
            held[s, k, y, 1 - x, :, half:] = held[s, k, y, 1 - x, :, half:] + self.high[s, k]

        self.each_row(act_high)
        self.aside[u].append(
            self.side(u, 3, lambda: self.part(u, y, 1 - x), self.from_x, self.beside[0])
        )
        self.crossed = u + 1

    def fold_side(self):
        u = self.joined
        z, y, x, _ = self.where
        s, held, depth = u % RING, self.held, self.split[0]
        for copy in self.aside[u]:
            copy.wait_recv()

        def act(k):
            total = held[s, k, y, x].astype(WIDE) + self.from_x[s, k].astype(WIDE)
            held[s, k, y, x] = (total + self.from_y[s, k].astype(WIDE)).astype(LOW)

        self.each_row(act)
        self.last[u] = [
            Move(
                lambda k=k, device=device: remote(
                    held.at[s, (z + k + 1) % depth, y, x],
                    self.from_row.at[s, k],
                    self.sems[4].at[u, k],
                    self.sems[5].at[u, k],
                    device,
                )
            )
            for k, device in enumerate(self.row)
        ]
        self.joined = u + 1

    def fold_row(self):
        u = self.done
        z, y, x, _ = self.where
        s = u % RING
        for copy in self.last[u]:
            copy.wait_recv()
        total = self.held[s, z, y, x].astype(WIDE)
        for k in range(self.split[0] - 1):
            total = total + self.from_row[s, k].astype(WIDE)
        self.put(u, total)
        for copy in self.diagonal[u] + self.aside[u] + self.last[u]:
            copy.wait_send()
        if u + RING < self.count:
            for device in self.row + list(self.beside):
                pl.semaphore_signal(self.sems[6].at[u], inc=1, device_id=device, device_id_type=MESH)
        self.done = u + 1

    def pump(self, times=1):
        for _ in range(times):
            if not self.round:
                if self.folded < self.swapped:
                    self.round.append(self.fold_core)
                if self.crossed < self.folded:
                    self.round += [self.fold_low, self.fold_high]
                if self.joined < self.crossed:
                    self.round.append(self.fold_side)
                if self.done < self.joined:
                    self.round.append(self.fold_row)
            if self.round:
                self.round.pop(0)()

    def end(self):
        while self.done < self.count:
            self.pump()
        for u in range(max(self.count - STAGES, 0), self.count):
            self.core[u].wait_send()


def pairs_kernel(split, shape, *refs):
    frames, groups, valid, block = shape
    it = iter(refs)
    take = lambda n: [next(it) for _ in range(n)]
    (x_in, dy_in, small_in), shards = take(3), take(7)
    out_ref, grad_ref = take(2)
    g_t_in, g_t_out, g_t_lin, g_s_in, g_s_out, g_up, g_down, g_small = take(8)
    small_all, full = next(it), take(7)
    xt, a_t, z_t, p_t, o_t, u_t, dy, x1, x2, a_s, z_s, p_s, o_s, a_m, act_g, slope, acc, at, low = take(19)
    b_recv, db_recv, dt_recv, sent, vec, sums, small_v, tile_v = take(8)
    w_a, w_b, w_up, w_down = take(4)
    bufs = take(7)
    ag_sems, rs_sems = take(7), take(7)
    ex_send, ex_recv, ex_own, load_sem, misc = take(5)

    where, row, beside = place(split)
    z, y, x, c = where
    nz, ny, nx, nc = split
    corner = (z * ny + y, (1 - x) * nc + (1 - c))
    greet(row + list(beside) + [corner])
    rows, width = x1.shape
    span = rows // frames
    pair = 2 * block
    chunk = pair
    mine = x * nc + c
    peers = [(beside[0], (1 - x) * nc + c), (beside[2], x * nc + (1 - c)), (corner, (1 - x) * nc + (1 - c))]
    waiting = []

    def cut(ref, index):
        if len(ref.shape) == 3:
            return ref.at[index]
        return ref.at[pl.ds(pl.multiple_of(index * block, TILE_ROWS), block)]

    def exchange(e, source, target, to_places):
        copies = []
        for f in range(frames):
            for k, (device, index) in enumerate(peers):
                src = f * groups + index if to_places else index * frames + f
                dst = mine * frames + f if to_places else f * groups + mine
                copies.append(
                    Move(
                        lambda src=src, dst=dst, k=k, f=f, device=device: remote(
                            cut(source, src), cut(target, dst), ex_send.at[e, k, f], ex_recv.at[e, k, f], device
                        )
                    )
                )
            src = f * groups + mine if to_places else mine * frames + f
            dst = mine * frames + f if to_places else f * groups + mine
            copies.append(
                Move(
                    lambda src=src, dst=dst, f=f: pltpu.make_async_copy(
                        cut(source, src), cut(target, dst), ex_own.at[e, f]
                    )
                )
            )
        return copies

    def arrive(copies):
        for copy in copies:
            copy.wait()

    moved = exchange(0, x_in, xt, True)
    dims = [s.shape for s in shards]
    chunks, ready = [(small_in, small_all, SMALL_ROWS, 0, SMALL_ROWS, 0, LANES, 0)], {}
    for k, (deep, wide) in enumerate(dims):
        tall = TALL if deep > dims[0][0] else 1
        cuts = PIECES if wide > 3 * width else FIRST if k == 0 else THIRD if k == 3 else 1
        for part in range(tall * cuts):
            count, cols = deep // tall, wide // cuts
            top, left = (part * count, 0) if tall > 1 else (0, part * cols)
            way = 2 if tall > 1 and part >= tall - LATE else 1 if k in OVER_Y else 0
            chunks.append((shards[k], full[k], deep, top, count, left, cols, way))
            ready[k, part] = len(chunks) - 1
    ag = Gather(split, where, row, beside, chunks, ag_sems, AHEAD)
    ag.pump(AHEAD)
    loads = {}

    class Load:
        def __init__(self, pairs):
            index = len(loads)
            self.copies = [
                Move(lambda a=a, b=b, k=k: pltpu.make_async_copy(a, b, load_sem.at[index, k]))
                for k, (a, b) in enumerate(pairs)
            ]

        def wait(self):
            for copy in self.copies:
                copy.wait()

    def load(key, source, target):
        if len(source.shape) == 2:
            pairs = [(source, target)]
        else:
            per = source.shape[2]
            pairs = [
                (source.at[:, k], target.at[:, pl.ds(k * per, per)]) for k in range(source.shape[1])
            ]
        loads[key] = Load(pairs)

    def fetch(key, k, target):
        for (which, _), i in ready.items():
            if which == k:
                ag.need(i)
        load(key, full[k], target)

    load("x", x_in, low)
    load("dy", dy_in, dy)
    sums[...] = jnp.zeros_like(sums)
    wb = [w_b.at[:, :, pl.ds(k * width, width)] for k in range(3)]
    wa = w_a
    ag.need(0)
    load("small", small_all, small_v)
    loads["small"].wait()
    devices = nz * ny * nx * nc
    per_row = devices * SMALL_ROWS // (nz * SMALL_ROWS)

    def small_of(r):
        k, s = r // per_row, r % per_row
        tile = small_v[k, s * SMALL_ROWS : (s + 1) * SMALL_ROWS, :].astype(WIDE)
        return jnp.concatenate([tile, jnp.zeros((SMALL_ROWS, width - LANES), WIDE)], axis=1)

    parts = {}

    def add(key, value):
        parts[key] = parts[key] + value if key in parts else value

    step = width // devices
    for r in range(devices):
        tile = small_of(r)
        add("a", pltpu.roll(tile, r * step, 1) if r else tile)
        for name, times in (("b", 2), ("c", 4)):
            at_row, at_col = r * step * times // width, r * step * times % width
            add((name, at_row), pltpu.roll(tile, at_col, 1) if at_col else tile)
    vec[0:10, :] = parts["a"][0:10]
    for k in range(2):
        vec[T_INB + k : T_INB + k + 1, :] = parts["b", k][10:11]
        vec[S_INB + k : S_INB + k + 1, :] = parts["b", k][11:12]
    for k in range(4):
        vec[E_BIAS + k : E_BIAS + k + 1, :] = parts["c", k][12:13]

    arrive(moved)
    norm_stage(xt, vec, T_GAIN, a_t, chunk)
    fetch("t_in", 0, wa)
    two, three = (lambda: ag.pump(TWO)), (lambda: ag.pump(THREE))
    loads["t_in"].wait()
    inproj_stage(a_t, wa, vec, T_INB, z_t)
    all_frames = frames * groups
    fetch("t_out", 1, wb[0])
    time_attend(z_t, p_t, o_t, all_frames, block, 0, all_frames // 4)
    fetch("t_lin", 2, wb[1])
    time_attend(z_t, p_t, o_t, all_frames, block, all_frames // 4, all_frames // 2)

    def store(ref):
        def act(cols, total):
            if len(ref.shape) == 3:
                ref[:, :, cols] = total.reshape(ref.shape[:2] + (-1,)).astype(LOW)
            else:
                ref[:, cols] = total.astype(LOW)

        return act

    loads["t_out"].wait()
    project_stage(o_t, wb[0], vec, T_OUTB, store(u_t))
    loads["t_lin"].wait()
    project_stage(u_t, wb[1], vec, T_LINB, store(sent))
    moved = exchange(1, sent, b_recv, False)
    fetch("s_in", 3, wa)
    loads["x"].wait()
    arrive(moved)

    def first(k):
        r = tiles(k, chunk)
        x1[r, :] = low[r, :].astype(WIDE) + wide_rows(b_recv, k, chunk)

    each(rows // chunk, first)
    norm_stage(x1, vec, S_GAIN, a_s, chunk)
    loads["s_in"].wait()
    inproj_stage(a_s, wa, vec, S_INB, z_s)
    fetch("s_out", 4, wb[2])
    heads = width // LANES * frames
    space_attend(z_s, p_s, o_s, frames, span, valid, block, 0, heads // 2)
    ag.need(ready[5, 0])
    space_attend(z_s, p_s, o_s, frames, span, valid, block, heads // 2, heads)

    def add_x1(cut, total):
        x2[:, cut] = x1[:, cut] + total

    loads["s_out"].wait()
    project_stage(o_s, wb[2], vec, S_OUTB, add_x1)
    norm_stage(x2, vec, F_GAIN, a_m, chunk)
    for part in range(PIECES):
        half = w_up.shape[2] // PIECES
        cols = pl.ds(part * half, half)
        ag.need(min(ready[5, part] + 1, ready[6, 0]))
        load(f"up{part}", full[5].at[:, :, :, cols], w_up.at[:, :, cols])
        loads[f"up{part}"].wait()
        per = half // TILE
        expand_stage(a_m, w_up, vec, act_g, slope, part * per, (part + 1) * per)
    loads["dy"].wait()

    per = width // TILE
    plan = {}
    order = [(g_up, 4 * per), (g_s_out, per), (g_s_in, 3 * per), (g_t_lin, per), (g_t_out, per), (g_t_in, 3 * per), (g_small, 1)]
    units, sub = per - 1, SUB
    homes = {}
    for out, count in order:
        for k in range(count):
            if sub == SUB:
                units, sub = units + 1, 0
                plan[units] = []
            plan[units].append((out, k))
            homes[id(out), k] = (units, sub)
            sub += 1
    count = units + 1
    step_rows = g_up.shape[0]

    def put(u, total):
        if u < per:
            g_down[:, u * TILE : (u + 1) * TILE] = total
            return
        for b, (out, k) in enumerate(plan[u]):
            out[:, k * TILE : (k + 1) * TILE] = total[b * step_rows : (b + 1) * step_rows]

    rs = Totals(split, where, row, beside, count, bufs, rs_sems, put)
    staged = bufs[0]

    def down(k):
        at[:width, :] = act_g[:, tiles(k, width)].T
        for u in range(per):
            total = dot(at[:width, :], dy[:, u * TILE : (u + 1) * TILE])
            staged[u, k] = total.reshape((ny, nx, nc, -1, TILE)).astype(LOW)

    each(nz, down)
    ones = jnp.ones((16, rows), LOW)
    sums[R_BIAS : R_BIAS + 1, :] = dot(ones, dy[...])[:1]
    for u in range(per):
        rs.swap(u)
    fetch("down", 6, w_down)
    one = rs.pump

    def grads(out, dz_ref, table):
        count = out.shape[1] // TILE
        act_bias = bias_rows(sums, table, width)
        k = 0
        while k < count:
            u, b0 = homes[id(out), k]
            n = min(SUB - b0, count - k)
            if b0 == 0:
                rs.room(u)

            def act(i, k=k, u=u, b0=b0, n=n):
                t = k + i
                total = dot(at[...], dz_ref[:, tiles(t)])
                act_bias(t, total[width : width + 1])
                tile_v[...] = total[:width]
                for b in range(n):

                    @pl.when(i == b)
                    def _():
                        low_row = (b0 + b) * step_rows
                        staged[u % STAGES, :, :, :, :, low_row : low_row + step_rows, :] = (
                            tile_v[...].reshape((nz, ny, nx, nc, step_rows, TILE)).astype(LOW)
                        )

            each(n, act, 0, one, 4)
            k += n
            if b0 + n == SUB:
                rs.swap(u)
                rs.pump()

    loads["down"].wait()
    reduce_back_stage(dy, w_down, slope, slope, one)

    hidden = act_g.shape[1]
    reduce_stage(act_g, w_down, vec, x2, store(low), one)
    out_copy = pltpu.make_async_copy(low, out_ref, misc.at[0])
    out_copy.start()
    turn_stage(a_m, at, one)
    grads(g_up, slope, [E_BIAS + k for k in range(hidden // width)])
    back_stage(slope, w_up, acc, one)
    out_copy.wait()

    def put_x2(k, dv):
        r = tiles(k, chunk)
        total = dy[r, :].astype(WIDE) + dv
        x2[r, :] = total
        low[r, :] = total.astype(LOW)

    norm_back_stage(x2, vec, F_GAIN, acc, sums, chunk, put_x2)
    load("t_in again", full[0], w_up.at[:, :, pl.ds(0, 3 * width)])
    turn_stage(o_s, at, one)
    grads(g_s_out, low, [S_OUTB])
    back_stage(low, wb[2], acc)
    rs.pump()
    low[...] = acc[...].astype(LOW)
    dz = slope.at[:, pl.ds(0, 3 * width)]
    space_attend_back(z_s, p_s, low, dz, frames, span, pump=one)
    back_stage(dz, wa, acc, one)

    def put_x1(k, dv):
        r = tiles(k, chunk)
        total = x2[r, :] + dv
        x1[r, :] = total
        put_rows(sent, k, chunk, total)

    norm_back_stage(x1, vec, S_GAIN, acc, sums, chunk, put_x1)
    moved = exchange(2, sent, db_recv, True)
    turn_stage(a_s, at, one)
    grads(g_s_in, dz, [S_INB, None, S_INB + 1])
    turn_stage(u_t, at, one)
    arrive(moved)

    def flat(k):
        low[tiles(k, chunk), :] = wide_rows(db_recv, k, chunk).astype(LOW)

    each(rows // chunk, flat)
    grads(g_t_lin, low, [T_LINB])
    back_stage(low, wb[1], acc)
    rs.pump()
    low[...] = acc[...].astype(LOW)
    turn_stage(o_t, at, one)
    grads(g_t_out, low, [T_OUTB])
    back_stage(low, wb[0], acc)
    rs.pump()
    low[...] = acc[...].astype(LOW)
    time_attend_back(z_t, p_t, low, dz, x2, acc, all_frames, block, lambda: rs.pump(TB))
    loads["t_in again"].wait()
    back_stage(dz, w_up.at[:, :, pl.ds(0, 3 * width)], acc, one)

    def put_t(k, dv):
        put_rows(sent, k, chunk, dv)

    norm_back_stage(xt, vec, T_GAIN, acc, sums, chunk, put_t)
    moved = exchange(3, sent, dt_recv, False)
    turn_stage(a_t, at, one)
    grads(g_t_in, dz, [T_INB, None, T_INB + 1])

    u, b0 = homes[id(g_small), 0]
    if b0 == 0:
        rs.room(u)
    low_row = b0 * step_rows
    lane = lax.broadcasted_iota(jnp.int32, (step_rows, width), 0)
    base = jnp.concatenate([sums[0:10, :], jnp.zeros((step_rows - 10, width), WIDE)], axis=0)

    def placed(pieces):
        out = jnp.zeros((step_rows, width), WIDE)
        for target, source in pieces:
            out = jnp.where(lane == target, sums[source : source + 1, :], out)
        return out

    twos = [placed([(10, T_INB + k), (11, S_INB + k)]) for k in range(2)]
    fours = [placed([(12, E_BIAS + k)]) for k in range(4)]
    for r in range(devices):
        def shifted(value, at_col):
            return (pltpu.roll(value, width - at_col, 1) if at_col else value)[:, :TILE]

        a = shifted(base, r * step)
        b = shifted(twos[2 * r * step // width], 2 * r * step % width)
        d = shifted(fours[4 * r * step // width], 4 * r * step % width)
        tile = jnp.where(lane[:, :TILE] < 10, a, jnp.where(lane[:, :TILE] < 12, b, d))
        slot = (r // (ny * nx * nc), r // (nx * nc) % ny, r // nc % nx, r % nc)
        staged[(u % STAGES,) + slot + (slice(low_row, low_row + step_rows), slice(None))] = tile.astype(LOW)
    rs.swap(u)
    arrive(moved)

    def last(k):
        r = tiles(k, chunk)
        x1[r, :] = x1[r, :] + wide_rows(dt_recv, k, chunk)

    each(rows // chunk, last)
    grad_copy = pltpu.make_async_copy(x1, grad_ref, misc.at[1])
    grad_copy.start()
    rs.end()
    ag.end()
    grad_copy.wait()


def whole_layer(split, shape, x, dy, small, shards):
    frames, groups, valid, block = shape
    rows, width = x.shape
    nz, ny, nx, nc = split
    low, wide = LOW, WIDE
    hidden = shards[5].shape[1]
    step = shards[0].shape[0]
    shapes = [(item.shape, wide) for item in shards] + [((step, TILE), wide)]
    token, full = ((rows, width), low), ((rows, width), wide)
    gathered = [((nz, ny * nx, nc * SMALL_ROWS, LANES), low)]
    gathered += [((nz, ny * nx, nc * item.shape[0], item.shape[1]), low) for item in shards]
    joined = [((s[0], s[1] * s[2], s[3]), kind) for s, kind in gathered]
    hbm = pl.BlockSpec(memory_space=pl.ANY)
    vmem = pl.BlockSpec(memory_space=pltpu.VMEM)
    outs = [token, full] + shapes + gathered
    out_specs = [hbm, hbm] + [vmem] * len(shapes) + [hbm] * len(gathered)
    span = rows // frames
    three, big = ((rows, 3 * width), low), ((rows, hidden), low)
    cuts = ((frames * groups, block, width), low)
    scratch = [cuts, token, three, ((frames * groups, rows, LANES), low), token, token, token, full, full]
    scratch += [token, three, ((frames * HEADS, span, span), low), token, token, big, big, full]
    scratch += [((width + 16, rows), low), token, cuts, cuts, cuts, cuts, ((24, width), wide), ((24, width), wide)]
    scratch += [joined[0], ((width, TILE), wide)]
    scratch += [joined[1], joined[1], joined[6], joined[7]]
    deep = SUB * step
    scratch += [((STAGES, nz, ny, nx, nc, deep, TILE), low), ((RING, nz, ny, nx, deep, TILE), low)]
    scratch += [((RING, nz, deep, TILE // 2), low)] * 2 + [((RING, nz, deep, TILE), low)] * 2
    scratch += [((RING, nz - 1, deep, TILE), low)]
    sem = pltpu.SemaphoreType.DMA
    chunks, units = 1 + 17, (hidden // TILE + 5 * width * 3 // TILE) // SUB + 8
    sems = [sem((chunks, nz - 1))] * 2 + [sem((chunks, 4))] * 4 + [sem((chunks,))]
    sems += [sem((units,))] * 2 + [sem((units, 4))] * 2 + [sem((units, nz - 1))] * 2
    sems += [pltpu.SemaphoreType.REGULAR((units,))]
    sems += [sem((4, 3, frames))] * 2 + [sem((4, frames)), sem((16, ny * nx)), sem((2,))]
    result = pl.pallas_call(
        functools.partial(pairs_kernel, split, shape),
        out_shape=[jax.ShapeDtypeStruct(s, kind) for s, kind in outs],
        in_specs=[hbm] * (3 + len(shards)),
        out_specs=out_specs,
        scratch_shapes=[pltpu.VMEM(s, kind) for s, kind in scratch] + sems,
        compiler_params=pltpu.CompilerParams(
            collective_id=0, has_side_effects=True, vmem_limit_bytes=63 << 20
        ),
        name="whole_layer",
    )(x, dy, small, *shards)
    return result[:10]


VECTOR_ROWS = (0, 1, 10, 2, 3, 4, 5, 12, 6, 7, 8, 14, 9)


SMALL_PLACES = {row: (row, 0) for row in range(10)} | {10: (10, 0), 12: (11, 0), 14: (12, 0)}


def pack_small(vectors):
    rows = {SMALL_PLACES[at][0]: item for at, item in zip(VECTOR_ROWS, vectors)}
    line = []
    for k in range(len(rows)):
        line.append(rows[k].reshape((1, -1)))
        line.append(jnp.zeros((1, LANES - rows[k].shape[0]), LOW))
    line.append(jnp.zeros((1, (SMALL_ROWS - len(rows)) * LANES), LOW))
    return jnp.concatenate(line, axis=1).reshape((SMALL_ROWS, LANES))


def hand_out(blocks, tile, widths):
    count = len(blocks)

    def body(*refs):
        ins, tile_ref = refs[:count], refs[count]
        outs, thin = refs[count + 1 : 2 * count + 1], refs[2 * count + 1 : -1]
        sems = refs[-1]
        copies = [pltpu.make_async_copy(a, b, sems.at[k]) for k, (a, b) in enumerate(zip(ins, outs))]
        for copy in copies:
            copy.start()
        for k, (row, width) in enumerate(widths):
            thin[k][...] = tile_ref[row : row + 1, :width]
        for copy in copies:
            copy.wait()

    hbm, vmem = pl.BlockSpec(memory_space=pl.ANY), pl.BlockSpec(memory_space=pltpu.VMEM)
    out = pl.pallas_call(
        body,
        out_shape=[jax.ShapeDtypeStruct(item.shape, WIDE) for item in blocks]
        + [jax.ShapeDtypeStruct((1, width), WIDE) for _, width in widths],
        in_specs=[vmem] * (count + 1),
        out_specs=[hbm] * count + [vmem] * len(widths),
        scratch_shapes=[pltpu.SemaphoreType.DMA((count,))],
        name="hand_out",
    )(*blocks, tile)
    return out[:count], [item.reshape(-1) for item in out[count:]]


def sum_native(terms):
    received = [
        lax.all_to_all(
            item.astype(LOW), "clip", split_axis=0, concat_axis=0, tiled=True
        ).astype(WIDE)
        for item in stack_rows(terms, lax.axis_size("clip"))
    ]
    return [
        lax.psum_scatter(item.astype(LOW), "frame", scatter_dimension=0, tiled=True).astype(WIDE)
        for item in fold_rows(received)
    ]


def on_device(
    video_tokens,
    time_gain,
    time_shift,
    time_inproj,
    time_inbias,
    time_outproj,
    time_outbias,
    time_linear,
    time_linbias,
    space_gain,
    space_shift,
    space_inproj,
    space_inbias,
    space_outproj,
    space_outbias,
    feed_gain,
    feed_shift,
    expand_weight,
    expand_bias,
    reduce_weight,
    reduce_bias,
    cotangent,
):
    split = inner_split(time_gain.shape[0])
    params = [
        time_gain,
        time_shift,
        time_inproj,
        time_inbias,
        time_outproj,
        time_outbias,
        time_linear,
        time_linbias,
        space_gain,
        space_shift,
        space_inproj,
        space_inbias,
        space_outproj,
        space_outbias,
        feed_gain,
        feed_shift,
        expand_weight,
        expand_bias,
        reduce_weight,
        reduce_bias,
    ]
    frames, places, width = video_tokens.shape[1:]
    groups = lax.axis_size("frame")
    valid = places // groups
    block = -(-valid // TILE_ROWS) * TILE_ROWS
    rows = frames * groups * block

    def padded(tokens):
        cut = tokens.reshape((frames, groups, valid, width))
        return jnp.pad(cut, ((0, 0), (0, 0), (0, block - valid), (0, 0)))

    def to_places(tokens):
        return lax.all_to_all(
            tokens.reshape((frames, groups, block, width)),
            "frame",
            split_axis=1,
            concat_axis=0,
            tiled=True,
        ).reshape((rows, width))

    def to_frames(tokens):
        return lax.all_to_all(
            tokens.reshape((frames * groups, 1, block, width)),
            "frame",
            split_axis=0,
            concat_axis=1,
            tiled=True,
        ).reshape((rows, width))

    def trimmed(tokens):
        cut = tokens.reshape((frames, groups, block, width))[:, :, :valid]
        return cut.reshape((1, frames, places, width))

    def weight(item):
        return item.reshape((4, -1, item.shape[1]))

    if split is not None:
        small = pack_small([item for item in params if item.ndim == 1])
        layer_out, input_grad, *sums = whole_layer(
            split,
            (frames, groups, valid, block),
            padded(video_tokens).reshape((rows, width)),
            padded(cotangent).reshape((rows, width)),
            small,
            [item for item in params if item.ndim == 2],
        )
        widths = [
            (SMALL_PLACES[at][0], item.shape[0])
            for at, item in zip(VECTOR_ROWS, [item for item in params if item.ndim == 1])
        ]
        wide, thin = hand_out(sums[:7], sums[7], widths)
        wide, thin = iter(wide), iter(thin)
        summed = [next(wide) if item.ndim == 2 else next(thin) for item in params]
        return (trimmed(layer_out), trimmed(input_grad)) + tuple(summed)

    full = [lax.all_gather(item, ("clip", "frame"), axis=0, tiled=True) for item in params]
    thin = [item for item in full if item.ndim == 1]
    t_in, t_out, t_lin, s_in, s_out, w_up, w_down = [weight(item) for item in full if item.ndim == 2]
    pieces = sorted(zip(VECTOR_ROWS, thin), key=lambda pair: pair[0])
    vec = jnp.concatenate([item.reshape((-1, width)) for _, item in pieces], axis=0)
    vec = jnp.pad(vec, ((0, 24 - vec.shape[0]), (0, 0))).astype(WIDE)
    tokens, d_out = padded(video_tokens), padded(cotangent)
    own = tokens.reshape((rows, width))
    placed = to_places(tokens)
    b_t, a_t, z_t, p_t, o_t, u_t = time_forward(block, placed, vec, t_in, t_out, t_lin)
    layer_out, d_x1, d_b, g_s_in, g_s_out, g_up, g_down, sums_s = space_layer(
        (frames, valid, block),
        own,
        to_frames(b_t),
        d_out.reshape((rows, width)),
        vec,
        s_in,
        s_out,
        w_up,
        w_down,
    )
    d_t, g_t_in, g_t_out, g_t_lin, sums_t = time_backward(
        block, to_places(d_b), placed, a_t, z_t, p_t, o_t, u_t, vec, t_in, t_out, t_lin
    )
    input_grad = d_x1 + to_frames(d_t).astype(WIDE)
    sums = sums_s + sums_t
    wide = iter(
        [item.reshape((-1, width if item is g_down else item.shape[2])) for item in
         (g_t_in, g_t_out, g_t_lin, g_s_in, g_s_out, g_up, g_down)]
    )
    rows_of = iter(VECTOR_ROWS)
    terms = []
    for item in params:
        if item.ndim == 2:
            terms.append(next(wide))
        else:
            at = next(rows_of)
            count = item.shape[0] * lax.axis_size(("clip", "frame")) // width
            terms.append(sums[at : at + count].reshape(-1))
    summed = sum_native(terms)
    return (trimmed(layer_out), trimmed(input_grad)) + tuple(summed)


def solution(mesh):
    return jax.shard_map(
        on_device,
        mesh=mesh,
        in_specs=(
            P("clip", "frame", None, None),
            P(("clip", "frame")),
            P(("clip", "frame")),
            P(("clip", "frame"), None),
            P(("clip", "frame")),
            P(("clip", "frame"), None),
            P(("clip", "frame")),
            P(("clip", "frame"), None),
            P(("clip", "frame")),
            P(("clip", "frame")),
            P(("clip", "frame")),
            P(("clip", "frame"), None),
            P(("clip", "frame")),
            P(("clip", "frame"), None),
            P(("clip", "frame")),
            P(("clip", "frame")),
            P(("clip", "frame")),
            P(("clip", "frame"), None),
            P(("clip", "frame")),
            P(("clip", "frame"), None),
            P(("clip", "frame")),
            P("clip", "frame", None, None),
        ),
        out_specs=(
            P("clip", "frame", None, None),
            P("clip", "frame", None, None),
            P(("clip", "frame")),
            P(("clip", "frame")),
            P(("clip", "frame"), None),
            P(("clip", "frame")),
            P(("clip", "frame"), None),
            P(("clip", "frame")),
            P(("clip", "frame"), None),
            P(("clip", "frame")),
            P(("clip", "frame")),
            P(("clip", "frame")),
            P(("clip", "frame"), None),
            P(("clip", "frame")),
            P(("clip", "frame"), None),
            P(("clip", "frame")),
            P(("clip", "frame")),
            P(("clip", "frame")),
            P(("clip", "frame"), None),
            P(("clip", "frame")),
            P(("clip", "frame"), None),
            P(("clip", "frame")),
        ),
        check_vma=False,
    )
```

```python
import functools

import jax
import jax.numpy as jnp
from jax import lax
from jax.experimental import pallas as pl
from jax.experimental.pallas import tpu as pltpu
from jax.sharding import PartitionSpec as P

MESH = pl.DeviceIdType.MESH
TILE_ROWS = 8
LOW = jnp.bfloat16
WIDE = jnp.float32
HEADS = 12
norm_eps = 1e-06
LANES = 128
TILE = 256
T_GAIN, T_SHIFT, T_OUTB, T_LINB, S_GAIN, S_SHIFT, S_OUTB, F_GAIN, F_SHIFT, R_BIAS, T_INB, S_INB, E_BIAS = 0, 1, 2, 3, 4, 5, 6, 7, 8, 9, 10, 12, 14


def dot(a, b):
    return lax.dot_general(a, b, (((1,), (0,)), ((), ())), preferred_element_type=WIDE)


def dot_nt(a, b):
    return lax.dot_general(a, b, (((1,), (1,)), ((), ())), preferred_element_type=WIDE)


def each(count, act, start=0, pump=None, every=1):
    def step(k, carry):
        act(k)
        return carry

    stride = count - start if pump is None else every
    for at in range(start, count, stride):
        lax.fori_loop(at, min(at + stride, count), step, 0)
        if pump is not None:
            pump()


def tiles(k, size=TILE):
    return pl.ds(pl.multiple_of(k * size, size), size)


def columns(w_ref, cut):
    block = w_ref[:, :, cut]
    return block.reshape((block.shape[0] * block.shape[1], block.shape[2]))


def wide_rows(ref, k, size):
    if len(ref.shape) == 2:
        return ref[tiles(k, size), :].astype(WIDE)
    per = size // ref.shape[1]
    block = ref[pl.ds(k * per, per), :, :].astype(WIDE)
    return block.reshape((size, ref.shape[2]))


def put_rows(ref, k, size, value):
    if len(ref.shape) == 2:
        ref[tiles(k, size), :] = value.astype(ref.dtype)
    else:
        per = size // ref.shape[1]
        ref[pl.ds(k * per, per), :, :] = value.reshape((per,) + ref.shape[1:]).astype(ref.dtype)


def normal(x):
    center = x - jnp.mean(x, axis=-1, keepdims=True)
    inverse = lax.rsqrt(jnp.mean(center * center, axis=-1, keepdims=True) + norm_eps)
    return center * inverse, inverse


def norm_stage(x_ref, vec, gain_row, a_ref, block, pump=None):
    gain, shift = vec[gain_row : gain_row + 1, :], vec[gain_row + 1 : gain_row + 2, :]

    def act(k):
        unit, _ = normal(wide_rows(x_ref, k, block))
        a_ref[tiles(k, block), :] = (unit * gain + shift).astype(LOW)

    each(a_ref.shape[0] // block, act, 0, pump, 2)


def norm_back_stage(x_ref, vec, gain_row, da_ref, sums, block, store):
    gain = vec[gain_row : gain_row + 1, :]
    width = da_ref.shape[1]

    def step(k, carry):
        unit, inverse = normal(wide_rows(x_ref, k, block))
        da = da_ref[tiles(k, block), :]
        e = da * gain
        dv = inverse * (
            e
            - jnp.mean(e, axis=-1, keepdims=True)
            - unit * jnp.mean(e * unit, axis=-1, keepdims=True)
        )
        store(k, dv)
        grad_gain, grad_shift = carry
        fold = lambda v: jnp.sum(v.reshape(block // 8, 8, width), axis=0)
        return grad_gain + fold(da * unit), grad_shift + fold(da)

    zero = jnp.zeros((8, width), WIDE)
    grad_gain, grad_shift = lax.fori_loop(0, da_ref.shape[0] // block, step, (zero, zero))
    sums[gain_row : gain_row + 1, :] = jnp.sum(grad_gain, axis=0, keepdims=True)
    sums[gain_row + 1 : gain_row + 2, :] = jnp.sum(grad_shift, axis=0, keepdims=True)


def inproj_stage(a_ref, w_ref, vec, bias_row, z_ref, pump=None):
    width = a_ref.shape[1]
    for part in range(3):

        def act(k, part=part):
            inner = tiles(k)
            cut = pl.ds(pl.multiple_of(part * width + k * TILE, TILE), TILE)
            total = dot(a_ref[...], columns(w_ref, cut))
            if part != 1:
                row = bias_row + part // 2
                total = total + vec[row : row + 1, inner]
            z_ref[:, cut] = total.astype(LOW)

        each(width // TILE, act, 0, pump, 3)


def project_stage(a_ref, w_ref, vec, bias_row, store, pump=None):
    def act(k):
        cut = tiles(k)
        store(cut, dot(a_ref[...], columns(w_ref, cut)) + vec[bias_row : bias_row + 1, cut])

    each(w_ref.shape[2] // TILE, act, 0, pump, 3)


def back_stage(dz_ref, w_ref, acc_ref, pump=None):
    width = acc_ref.shape[1]
    parts = w_ref.shape[2] // width
    acc_ref[...] = dot_nt(dz_ref[:, :width], columns(w_ref, pl.ds(0, width)))

    def act(k):
        cut = tiles(k + 1, width)
        acc_ref[...] = acc_ref[...] + dot_nt(dz_ref[:, cut], columns(w_ref, cut))

    if parts > 1:
        each(parts - 1, act, 0, pump)


def turn_stage(a_ref, at_ref, pump=None):
    width = a_ref.shape[1]

    def act(k):
        at_ref[tiles(k), :] = a_ref[:, tiles(k)].T

    each(width // TILE, act, 0, pump, 3)
    at_ref[width:, :] = jnp.ones((at_ref.shape[0] - width, at_ref.shape[1]), LOW)


def weight_stage(at_ref, dz_ref, g_ref, bias):
    depth, rows, _ = g_ref.shape
    full = depth * rows

    def act(k):
        cut = tiles(k)
        total = dot(at_ref[...], dz_ref[:, cut])
        g_ref[:, :, cut] = total[:full].astype(LOW).reshape((depth, rows, TILE))
        bias(k, total[full : full + 1])

    each(g_ref.shape[2] // TILE, act)


def bias_rows(sums, table, width):
    def act(k, total):
        per = width // TILE
        for part, row in enumerate(table):
            if row is None:
                continue

            @pl.when((k >= part * per) & (k < (part + 1) * per))
            def _():
                sums[row : row + 1, tiles(k - part * per)] = total

    return act


def low_head(rows):
    lane = lax.broadcasted_iota(jnp.int32, (rows, LANES), 1)
    return lane < LANES // 2


def space_attend(z_ref, p_ref, o_ref, frames, rows, valid, block, start=0, stop=None, pump=None):
    width = o_ref.shape[1]
    pairs = width // LANES
    scale = (LANES // 2) ** -0.5

    def act(step):
        f, pair = step // pairs, step % pairs
        span = tiles(f, rows)
        q = z_ref[span, pl.ds(pl.multiple_of(pair * LANES, LANES), LANES)]
        k = z_ref[span, pl.ds(pl.multiple_of(width + pair * LANES, LANES), LANES)]
        v = z_ref[span, pl.ds(pl.multiple_of(2 * width + pair * LANES, LANES), LANES)]
        first = low_head(rows)
        vt = v.T
        keep = lax.broadcasted_iota(jnp.int32, (rows, rows), 0) % block < valid
        outs = []
        for side in range(2):
            mine = first if side == 0 else ~first
            scores = dot_nt(k, jnp.where(mine, q, jnp.zeros_like(q))) * scale
            scores = jnp.where(keep, scores, -1e30)
            e = jnp.exp(scores - jnp.max(scores, axis=0, keepdims=True))
            p = (e * (1.0 / jnp.sum(e, axis=0, keepdims=True))).astype(LOW)
            p_ref[2 * step + side] = p
            outs.append(dot(vt, p))
        top = lax.broadcasted_iota(jnp.int32, (LANES, rows), 0) < LANES // 2
        o = jnp.where(top, outs[0], outs[1]).T
        o_ref[span, pl.ds(pl.multiple_of(pair * LANES, LANES), LANES)] = o.astype(LOW)

    each(frames * pairs if stop is None else stop, act, start, pump, 2)


def space_attend_back(z_ref, p_ref, do_ref, dz_ref, frames, rows, start=0, stop=None, pump=None):
    width = do_ref.shape[1]
    pairs = width // LANES
    scale = (LANES // 2) ** -0.5

    def act(step):
        f, pair = step // pairs, step % pairs
        span = tiles(f, rows)
        cut_q = pl.ds(pl.multiple_of(pair * LANES, LANES), LANES)
        cut_k = pl.ds(pl.multiple_of(width + pair * LANES, LANES), LANES)
        cut_v = pl.ds(pl.multiple_of(2 * width + pair * LANES, LANES), LANES)
        q, k, v, do = z_ref[span, cut_q], z_ref[span, cut_k], z_ref[span, cut_v], do_ref[span, cut_q]
        kt = k.T
        first = low_head(rows)
        dk = dv = None
        turned = []
        for side in range(2):
            mine = first if side == 0 else ~first
            q_side = jnp.where(mine, q, jnp.zeros_like(q))
            do_side = jnp.where(mine, do, jnp.zeros_like(do))
            p_low = p_ref[2 * step + side]
            p = p_low.astype(WIDE)
            dp = dot_nt(v, do_side)
            inner = jnp.sum(dp * p, axis=0, keepdims=True)
            ds = (p * (dp - inner)).astype(LOW)
            dv_side, dk_side = dot(p_low, do_side), dot(ds, q_side)
            dv = dv_side if dv is None else dv + dv_side
            dk = dk_side if dk is None else dk + dk_side
            turned.append(dot(kt, ds))
        top = lax.broadcasted_iota(jnp.int32, (LANES, rows), 0) < LANES // 2
        dq = jnp.where(top, turned[0], turned[1]).T
        dz_ref[span, cut_q] = (dq * scale).astype(LOW)
        dz_ref[span, cut_k] = (dk * scale).astype(LOW)
        dz_ref[span, cut_v] = dv.astype(LOW)

    each(frames * pairs if stop is None else stop, act, start, pump, 2)


def head_sum(width):
    row = lax.broadcasted_iota(jnp.int32, (width, LANES), 0) // (width // HEADS)
    col = lax.broadcasted_iota(jnp.int32, (width, LANES), 1)
    return (row == col).astype(WIDE).astype(LOW)


def head_spread(width):
    row = lax.broadcasted_iota(jnp.int32, (LANES, width), 0)
    col = lax.broadcasted_iota(jnp.int32, (LANES, width), 1) // (width // HEADS)
    return (row == col).astype(WIDE).astype(LOW)


def by_head(product, pick):
    high = product.astype(LOW)
    rest = (product - high.astype(WIDE)).astype(LOW)
    return dot(high, pick) + dot(rest, pick)


def time_attend(z_ref, p_ref, o_ref, frames, block, start=0, stop=None, pump=None):
    width = o_ref.shape[1]
    scale = (width // HEADS) ** -0.5
    pick, spread = head_sum(width), head_spread(width)
    spans = [slice(k * block, (k + 1) * block) for k in range(frames)]

    def act(pair):
        rows = tiles(pair, 2 * block)
        q = z_ref[rows, :width].astype(WIDE)
        scores = [[], []]
        for span in spans:
            k = z_ref[span, width : 2 * width].astype(WIDE)
            for half in range(2):
                scores[half].append(by_head(q[spans[half]] * k, pick) * scale)
        probs = []
        for half in range(2):
            top = functools.reduce(jnp.maximum, scores[half])
            e = [jnp.exp(s - top) for s in scores[half]]
            inverse = 1.0 / functools.reduce(jnp.add, e)
            probs.append([item * inverse for item in e])
        out = [jnp.zeros((block, width), WIDE)] * 2
        for k, span in enumerate(spans):
            v = z_ref[span, 2 * width :].astype(WIDE)
            for half in range(2):
                p = probs[half][k]
                p = p.astype(LOW)
                p_ref[2 * pair + half, span, :] = p
                out[half] = out[half] + dot(p, spread) * v
        o_ref[rows, :] = jnp.concatenate(out, axis=0).astype(LOW)

    each(frames // 2 if stop is None else stop, act, start, pump)


def time_attend_back(z_ref, p_ref, do_ref, dz_ref, dk_ref, dv_ref, frames, block, pump=None):
    width = do_ref.shape[1]
    scale = (width // HEADS) ** -0.5
    pick, spread = head_sum(width), head_spread(width)
    spans = [slice(k * block, (k + 1) * block) for k in range(frames)]
    dk_ref[...] = jnp.zeros_like(dk_ref)
    dv_ref[...] = jnp.zeros_like(dv_ref)

    def act(pair):
        rows = tiles(pair, 2 * block)
        do = do_ref[rows, :].astype(WIDE)
        q = z_ref[rows, :width].astype(WIDE)
        dps = [[], []]
        inner = [jnp.zeros((block, LANES), WIDE)] * 2
        for span in spans:
            v = z_ref[span, 2 * width :].astype(WIDE)
            for half in range(2):
                dp = by_head(do[spans[half]] * v, pick)
                inner[half] = inner[half] + dp * p_ref[2 * pair + half, span, :].astype(WIDE)
                dps[half].append(dp)
        dq = [jnp.zeros((block, width), WIDE)] * 2
        for at, span in enumerate(spans):
            k = z_ref[span, width : 2 * width].astype(WIDE)
            dk, dv = dk_ref[span, :], dv_ref[span, :]
            for half in range(2):
                p = p_ref[2 * pair + half, span, :]
                ds = dot((p.astype(WIDE) * (dps[half][at] - inner[half])).astype(LOW), spread)
                dq[half] = dq[half] + ds * k
                dk = dk + ds * q[spans[half]]
                dv = dv + dot(p, spread) * do[spans[half]]
            dk_ref[span, :] = dk
            dv_ref[span, :] = dv
        dz_ref[rows, :width] = (jnp.concatenate(dq, axis=0) * scale).astype(LOW)

    each(frames // 2, act, 0, pump)

    def out(pair):
        rows = tiles(pair, 2 * block)
        dz_ref[rows, width : 2 * width] = (dk_ref[rows, :] * scale).astype(LOW)
        dz_ref[rows, 2 * width :] = dv_ref[rows, :].astype(LOW)

    each(frames // 2, out)


def expand_stage(a_ref, w_ref, vec, g_ref, slope_ref, start=0, stop=None, pump=None):
    width = a_ref.shape[1]
    per = width // TILE

    def act(k):
        cut = tiles(k)
        h = dot(a_ref[...], columns(w_ref, cut))
        inner = tiles(k % per)
        bias = vec[pl.ds(E_BIAS + k // per, 1), inner]
        h = h + bias
        cdf = 0.5 * (1.0 + lax.erf(h * (0.5 ** 0.5)))
        g_ref[:, cut] = (h * cdf).astype(LOW)
        slope_ref[:, cut] = (cdf + h * (jnp.exp(-0.5 * h * h) * 0.3989422804014327)).astype(LOW)

    each(w_ref.shape[2] // TILE if stop is None else stop, act, start, pump, 2)


def reduce_stage(g_ref, w_ref, vec, x_ref, out_store, pump=None):
    depth, rows, width = w_ref.shape

    def act(k):
        cut = tiles(k)
        total = x_ref[:, cut] + vec[R_BIAS : R_BIAS + 1, cut]
        for z in range(depth):
            total = total + dot(g_ref[:, z * rows : (z + 1) * rows], w_ref[z, :, cut])
        out_store(cut, total)

    each(width // TILE, act, 0, pump, 3)


def reduce_back_stage(dm_ref, w_ref, slope_ref, dh_ref, pump=None):
    depth, rows, _ = w_ref.shape
    per = rows // TILE

    def act(k):
        cut = tiles(k)
        block = w_ref[k // per, tiles(k % per), :]
        dh_ref[:, cut] = (dot_nt(dm_ref[...], block) * slope_ref[:, cut].astype(WIDE)).astype(LOW)

    each(depth * per, act, 0, pump, 4)


def reduce_grad_stage(g_ref, gt_ref, dm_ref, out_ref, sums):
    depth, rows, width = out_ref.shape

    def act(k):
        z, part = k // (rows // TILE), k % (rows // TILE)
        turned = g_ref[:, tiles(k)].T
        gt_ref[...] = turned
        out_ref[z, tiles(part), :] = dot(gt_ref[...], dm_ref[...]).astype(LOW)

    each(depth * rows // TILE, act)
    ones = jnp.ones((16, dm_ref.shape[0]), LOW)
    sums[R_BIAS : R_BIAS + 1, :] = dot(ones, dm_ref[...])[:1]


def vmem_call(body, outs, ins, scratch, name):
    return pl.pallas_call(
        body,
        out_shape=[jax.ShapeDtypeStruct(shape, kind) for shape, kind in outs],
        in_specs=[pl.BlockSpec(memory_space=pltpu.VMEM)] * len(ins),
        out_specs=[pl.BlockSpec(memory_space=pltpu.VMEM)] * len(outs),
        scratch_shapes=[pltpu.VMEM(shape, kind) for shape, kind in scratch],
        compiler_params=pltpu.CompilerParams(vmem_limit_bytes=60 << 20),
        name=name,
    )(*ins)


def time_forward(block, x, vec, w_in, w_out, w_lin):
    rows, width = x.shape
    frames = rows // block

    def body(x_ref, vec_ref, w_in, w_out, w_lin, b_ref, a_ref, z_ref, p_ref, o_ref, u_ref):
        def store(ref):
            def act(cut, total):
                ref[:, cut] = total.astype(LOW)

            return act

        norm_stage(x_ref, vec_ref, T_GAIN, a_ref, 2 * block)
        inproj_stage(a_ref, w_in, vec_ref, T_INB, z_ref)
        time_attend(z_ref, p_ref, o_ref, frames, block)
        project_stage(o_ref, w_out, vec_ref, T_OUTB, store(u_ref))
        project_stage(u_ref, w_lin, vec_ref, T_LINB, store(b_ref))

    token = ((rows, width), LOW)
    outs = [token, token, ((rows, 3 * width), LOW), ((frames, rows, LANES), LOW), token, token]
    return vmem_call(body, outs, (x, vec, w_in, w_out, w_lin), [], "time_forward")


def space_layer(shape, x, b, dy, vec, w_in, w_out, w_up, w_down):
    frames, valid, block = shape
    rows, width = x.shape
    span = rows // frames
    hidden = w_up.shape[2]
    heads_all = frames * HEADS

    def body(x_ref, b_ref, dy_ref, vec_ref, w_in, w_out, w_up, w_down, out_ref, dx1_ref, db_ref,
             g_in, g_out, g_up, g_down, sums, x1, x2, a_s, z_s, p_s, o_s, a_m, act_g, slope, dh, acc, at, gt, low):
        sums[...] = jnp.zeros_like(sums)

        def first(k):
            r = tiles(k, 2 * block)
            x1[r, :] = x_ref[r, :].astype(WIDE) + b_ref[r, :].astype(WIDE)

        each(rows // (2 * block), first)
        norm_stage(x1, vec_ref, S_GAIN, a_s, 2 * block)
        inproj_stage(a_s, w_in, vec_ref, S_INB, z_s)
        space_attend(z_s, p_s, o_s, frames, span, valid, block)

        def add_x1(cut, total):
            x2[:, cut] = x1[:, cut] + total

        project_stage(o_s, w_out, vec_ref, S_OUTB, add_x1)
        norm_stage(x2, vec_ref, F_GAIN, a_m, 2 * block)
        expand_stage(a_m, w_up, vec_ref, act_g, slope)

        def put_out(cut, total):
            out_ref[:, cut] = total.astype(LOW)

        reduce_stage(act_g, w_down, vec_ref, x2, put_out)
        reduce_grad_stage(act_g, gt, dy_ref, g_down, sums)
        reduce_back_stage(dy_ref, w_down, slope, dh)
        turn_stage(a_m, at)
        weight_stage(at, dh, g_up, bias_rows(sums, [E_BIAS + k for k in range(hidden // width)], width))
        back_stage(dh, w_up, acc)

        def put_x2(k, dv):
            r = tiles(k, 2 * block)
            total = dy_ref[r, :].astype(WIDE) + dv
            dx1_ref[r, :] = total
            low[r, :] = total.astype(LOW)

        norm_back_stage(x2, vec_ref, F_GAIN, acc, sums, 2 * block, put_x2)
        turn_stage(o_s, at)
        weight_stage(at, low, g_out, bias_rows(sums, [S_OUTB], width))
        back_stage(low, w_out, acc)
        low[...] = acc[...].astype(LOW)
        dz = dh.at[:, : 3 * width]
        space_attend_back(z_s, p_s, low, dz, frames, span)
        turn_stage(a_s, at)
        weight_stage(at, dz, g_in, bias_rows(sums, [S_INB, None, S_INB + 1], width))
        back_stage(dz, w_in, acc)

        def put_x1(k, dv):
            r = tiles(k, 2 * block)
            total = dx1_ref[r, :] + dv
            dx1_ref[r, :] = total
            db_ref[r, :] = total.astype(LOW)

        norm_back_stage(x1, vec_ref, S_GAIN, acc, sums, 2 * block, put_x1)

    token, full = ((rows, width), LOW), ((rows, width), WIDE)
    outs = [token, full, token] + [(w.shape, LOW) for w in (w_in, w_out, w_up, w_down)] + [(vec.shape, WIDE)]
    scratch = [full, full, token, ((rows, 3 * width), LOW), ((heads_all, span, span), LOW), token, token]
    scratch += [((rows, hidden), LOW)] * 3 + [full, ((width + 16, rows), LOW), ((TILE, rows), LOW), token]
    return vmem_call(body, outs, (x, b, dy, vec, w_in, w_out, w_up, w_down), scratch, "space_layer")


def time_backward(block, db, x, a, z, p, o, u, vec, w_in, w_out, w_lin):
    rows, width = x.shape
    frames = rows // block

    def body(db_ref, x_ref, a_ref, z_ref, p_ref, o_ref, u_ref, vec_ref, w_in, w_out, w_lin,
             dt_ref, g_in, g_out, g_lin, sums, low, dz, dk, dv, acc, at):
        sums[...] = jnp.zeros_like(sums)
        turn_stage(u_ref, at)
        weight_stage(at, db_ref, g_lin, bias_rows(sums, [T_LINB], width))
        back_stage(db_ref, w_lin, acc)
        low[...] = acc[...].astype(LOW)
        turn_stage(o_ref, at)
        weight_stage(at, low, g_out, bias_rows(sums, [T_OUTB], width))
        back_stage(low, w_out, acc)
        low[...] = acc[...].astype(LOW)
        time_attend_back(z_ref, p_ref, low, dz, dk, dv, frames, block)
        turn_stage(a_ref, at)
        weight_stage(at, dz, g_in, bias_rows(sums, [T_INB, None, T_INB + 1], width))
        back_stage(dz, w_in, acc)

        def put(k, dv):
            put_rows(dt_ref, k, 2 * block, dv)

        norm_back_stage(x_ref, vec_ref, T_GAIN, acc, sums, 2 * block, put)

    token, full = ((rows, width), LOW), ((rows, width), WIDE)
    outs = [token] + [(w.shape, LOW) for w in (w_in, w_out, w_lin)] + [(vec.shape, WIDE)]
    scratch = [token, ((rows, 3 * width), LOW), full, full, full, ((width + 16, rows), LOW)]
    return vmem_call(body, outs, (db, x, a, z, p, o, u, vec, w_in, w_out, w_lin), scratch, "time_backward")


def stack_rows(terms, groups):
    return tuple(
        (item.reshape((groups, item.shape[0] // groups) + item.shape[1:]) for item in terms)
    )


def fold_rows(received):
    return tuple((jnp.sum(item, axis=0) for item in received))


def remote(source, target, send, recv, device):
    return pltpu.make_async_remote_copy(
        src_ref=source,
        dst_ref=target,
        send_sem=send,
        recv_sem=recv,
        device_id=device,
        device_id_type=MESH,
    )


def place(split):
    nz, ny, nx, nc = split
    clip, frame = lax.axis_index("clip"), lax.axis_index("frame")
    z, y, x, c = clip // ny, clip % ny, frame // nc, frame % nc

    def mesh_at(z, y, x, c):
        return (z * ny + y, x * nc + c)

    row = [mesh_at((z + step) % nz, y, x, c) for step in range(1, nz)]
    beside = (mesh_at(z, y, 1 - x, c), mesh_at(z, 1 - y, x, c), mesh_at(z, y, x, 1 - c))
    return (z, y, x, c), row, beside


def greet(devices):
    barrier = pltpu.get_barrier_semaphore()
    for device in devices:
        pl.semaphore_signal(barrier, inc=1, device_id=device, device_id_type=MESH)
    pl.semaphore_wait(barrier, len(devices))


def inner_split(rows):
    clips, frames = lax.axis_size("clip"), lax.axis_size("frame")
    if frames == 4 and clips % 2 == 0 and clips > 2 and rows % TILE_ROWS == 0:
        return (clips // 2, 2, 2, 2)
    return None


SMALL_ROWS = 16
RING = 6
AHEAD = 2
PIECES = 2
FIRST = 1
TALL = 4
LATE = 2
LATE_RELAY = 1
LATE_SEND = 5
LATE_STEP = 2
OVER_Y = ()
THIRD = 1
TWO = 1
THREE = 1
TB = 2
SB = 1
GB = 0
RB = 1
RD = 1
TN = 1
BK = 1
GT = 1
BL = 1
STAGES = 3
SUB = 4


class Move:
    def __init__(self, make):
        self.make = make
        make().start()

    def wait(self):
        self.make().wait()

    def wait_recv(self):
        self.make().wait_recv()

    def wait_send(self):
        self.make().wait_send()


class Gather:
    def __init__(self, split, where, row, beside, chunks, sems, ahead):
        self.split, self.where, self.row, self.beside = split, where, row, beside
        self.chunks, self.sems = chunks, sems
        self.started, self.first, self.second, self.third, self.core = [], {}, {}, {}, {}
        self.along = {}
        plain = [i for i, item in enumerate(chunks) if item[7] != 2]
        late = [i for i, item in enumerate(chunks) if item[7] == 2]
        self.here, count = set(), len(plain)
        self.events, self.ends = [], set()

        def then(call, i):
            self.events.append(lambda: call(i))

        for i in plain[:ahead]:
            then(self.spread, i)
        for i in late:
            then(self.sideways, i)
        for t in range(count + 3):
            if t < count:
                then(self.sideways, plain[t])
            if t + ahead < count:
                then(self.spread, plain[t + ahead])
            if 0 <= t - 2 < count:
                then(self.finish, plain[t - 2])
            if 0 <= t - 3 < count:
                then(self.receive, plain[t - 3])
            if 0 <= t - 1 < count:
                then(self.relay_x, plain[t - 1])
                then(self.relay_y, plain[t - 1])
            for k, i in enumerate(late):
                if t == LATE_RELAY:
                    then(self.relay_x, i)
                    then(self.relay_y, i)
                if t == LATE_SEND + LATE_STEP * k:
                    then(self.lengthwise, i)
                if t == count + 1:
                    then(self.finish, i)
                if t == count + 2:
                    then(self.receive, i)
            self.ends.add(len(self.events))
        self.next = 0

    def pump(self, times=1):
        for _ in range(times):
            if self.next < len(self.events):
                self.next += 1
                self.events[self.next - 1]()

    def need(self, i):
        while i not in self.here or self.next not in self.ends:
            self.pump()

    def launch(self, make):
        move = Move(make)
        self.started.append(move)
        return move

    def block(self, i, y, x, c, half=None):
        _, full, per, low, count, start, width, way = self.chunks[i]
        first = c * per + low
        if half is not None and width % (2 * LANES) == 0:
            start, width = start + half * (width // 2), width // 2
        elif half is not None:
            first, count = first + half * (count // 2), count // 2
        rows = pl.ds(pl.multiple_of(first, TILE_ROWS), count)
        places = self.where[0] if way == 2 else slice(None)
        return full.at[places, y * self.split[2] + x, rows, pl.ds(start, width)]

    def own(self, i):
        z, y, x, c = self.where
        _, full, per, low, count, start, width, _ = self.chunks[i]
        rows = pl.ds(pl.multiple_of(c * per + low, TILE_ROWS), count)
        return full.at[z, y * self.split[2] + x, rows, pl.ds(start, width)]

    def core_part(self, i, place):
        c = self.where[3]
        _, full, per, low, count, start, width, _ = self.chunks[i]
        rows = pl.ds(pl.multiple_of(c * per + low, TILE_ROWS), count)
        return full.at[place, :, rows, pl.ds(start, width)]

    def mine(self, i):
        shard, _, _, low, count, start, width, _ = self.chunks[i]
        return shard.at[pl.ds(low, count), pl.ds(start, width)]

    def keep(self, i):
        return Move(lambda: pltpu.make_async_copy(self.mine(i), self.own(i), self.sems[6].at[i]))

    def to_row(self, i, source, target):
        send, recv = self.sems[0], self.sems[1]
        return [
            self.launch(
                lambda k=k, device=device: remote(source(), target(), send.at[i, k], recv.at[i, k], device)
            )
            for k, device in enumerate(self.row)
        ]

    def spread(self, i):
        self.first[i] = self.to_row(i, lambda: self.mine(i), lambda: self.own(i))
        self.first[i].append(self.keep(i))

    def side(self, i, k, block, device):
        send, recv = self.sems[2], self.sems[3]
        return self.launch(lambda: remote(block(), block(), send.at[i, k], recv.at[i, k], device))

    def to_twin(self, i, k, block):
        send, recv, twin = self.sems[4], self.sems[5], self.beside[2]
        return self.launch(lambda: remote(block(), block(), send.at[i, k], recv.at[i, k], twin))

    def sideways(self, i):
        _, y, x, c = self.where
        if self.chunks[i][7] == 2:
            self.first[i] = [self.keep(i)]
        for copy in self.first[i][:-1]:
            copy.wait_recv()
        self.first[i][-1].wait()
        block = lambda: self.block(i, y, x, c)
        self.second[i] = [self.side(i, k, block, self.beside[k]) for k in range(2)]
        self.core[i] = [] if self.chunks[i][7] == 2 else [self.to_twin(i, 0, block)]

    def relay_x(self, i):
        _, y, x, c = self.where
        way = self.chunks[i][7]
        self.second[i][0].wait_recv()
        part = None if way == 1 else 0
        self.third[i] = [self.side(i, 2, lambda: self.block(i, y, 1 - x, c, part), self.beside[1])]
        if way != 2:
            self.core[i].append(self.to_twin(i, 1, lambda: self.block(i, y, 1 - x, c)))

    def relay_y(self, i):
        _, y, x, c = self.where
        way = self.chunks[i][7]
        self.second[i][1].wait_recv()
        if way != 1:
            block = lambda: self.block(i, 1 - y, x, c, 1)
            self.third[i].append(self.side(i, 3, block, self.beside[0]))
        if way != 2:
            self.core[i].append(self.to_twin(i, 2, lambda: self.block(i, 1 - y, x, c)))

    def lengthwise(self, i):
        for copy in self.third[i]:
            copy.wait_recv()
        part = lambda: self.core_part(i, self.where[0])
        self.along[i] = self.to_row(i, part, part)

    def finish(self, i):
        _, y, x, c = self.where
        if self.chunks[i][7] == 2:
            for copy in self.along[i]:
                copy.wait_recv()
            self.core[i].append(self.to_twin(i, 3, lambda: self.core_part(i, slice(None))))
            return
        for copy in self.third[i]:
            copy.wait_recv()
        self.core[i].append(self.to_twin(i, 3, lambda: self.block(i, 1 - y, 1 - x, c)))

    def receive(self, i):
        for copy in self.core[i]:
            copy.wait_recv()
        self.here.add(i)

    def end(self):
        for i in range(len(self.chunks)):
            self.need(i)
        for copy in self.started:
            copy.wait_send()


class Totals:
    def __init__(self, split, where, row, beside, count, bufs, sems, put):
        self.split, self.where, self.row, self.beside, self.count = split, where, row, beside, count
        self.staged, self.held, self.low, self.high, self.from_x, self.from_y, self.from_row = bufs
        self.sems, self.put = sems, put
        self.core, self.diagonal, self.aside, self.last = {}, {}, {}, {}
        self.folded = self.crossing = self.crossed = self.joined = self.done = self.swapped = 0
        self.round = []

    def room(self, u):
        while self.folded < u - STAGES + 1:
            self.pump()
        if u >= STAGES:
            self.core[u - STAGES].wait_send()

    def each_row(self, act):
        each(self.split[0], act)

    def swap(self, u):
        c = self.where[3]
        if u >= RING:
            while self.done < u - RING + 1:
                self.pump()
            pl.semaphore_wait(self.sems[6].at[u - RING], len(self.row) + len(self.beside))
        self.core[u] = Move(
            lambda: remote(
                self.staged.at[u % STAGES, :, :, :, 1 - c],
                self.held.at[u % RING],
                self.sems[0].at[u % RING],
                self.sems[1].at[u % RING],
                self.beside[2],
            )
        )
        self.swapped = u + 1

    def side(self, u, k, block, target, device):
        send, recv = self.sems[2], self.sems[3]
        return Move(lambda: remote(block(), target.at[u % RING], send.at[u % RING, k], recv.at[u % RING, k], device))

    def part(self, u, yy, xx, half=None):
        cols = slice(None) if half is None else pl.ds(half * (TILE // 2), TILE // 2)
        return self.held.at[u % RING, :, yy, xx, :, cols]

    def fold_core(self):
        u = self.folded
        _, y, x, c = self.where
        s, q, held = u % RING, u % STAGES, self.held
        self.core[u].wait_recv()

        def fold(yy, xx):
            def act(k):
                held[s, k, yy, xx] = held[s, k, yy, xx] + self.staged[q, k, yy, xx, c]

            self.each_row(act)

        fold(1 - y, 1 - x)
        self.diagonal[u] = [
            self.side(u, 0, lambda: self.part(u, 1 - y, 1 - x, 0), self.low, self.beside[0]),
            self.side(u, 1, lambda: self.part(u, 1 - y, 1 - x, 1), self.high, self.beside[1]),
        ]
        fold(1 - y, x)
        fold(y, 1 - x)
        fold(y, x)
        self.folded = u + 1

    def fold_low(self):
        u = self.crossing
        _, y, x, _ = self.where
        s, held, half = u % RING, self.held, TILE // 2
        self.diagonal[u][0].wait_recv()

        def act_low(k):
            held[s, k, 1 - y, x, :, :half] = held[s, k, 1 - y, x, :, :half] + self.low[s, k]

        self.each_row(act_low)
        self.aside[u] = [self.side(u, 2, lambda: self.part(u, 1 - y, x), self.from_y, self.beside[1])]
        self.crossing = u + 1

    def fold_high(self):
        u = self.crossed
        _, y, x, _ = self.where
        s, held, half = u % RING, self.held, TILE // 2
        self.diagonal[u][1].wait_recv()

        def act_high(k):
            held[s, k, y, 1 - x, :, half:] = held[s, k, y, 1 - x, :, half:] + self.high[s, k]

        self.each_row(act_high)
        self.aside[u].append(
            self.side(u, 3, lambda: self.part(u, y, 1 - x), self.from_x, self.beside[0])
        )
        self.crossed = u + 1

    def fold_side(self):
        u = self.joined
        z, y, x, _ = self.where
        s, held, depth = u % RING, self.held, self.split[0]
        for copy in self.aside[u]:
            copy.wait_recv()

        def act(k):
            total = held[s, k, y, x].astype(WIDE) + self.from_x[s, k].astype(WIDE)
            held[s, k, y, x] = (total + self.from_y[s, k].astype(WIDE)).astype(LOW)

        self.each_row(act)
        self.last[u] = [
            Move(
                lambda k=k, device=device: remote(
                    held.at[s, (z + k + 1) % depth, y, x],
                    self.from_row.at[s, k],
                    self.sems[4].at[u % RING, k],
                    self.sems[5].at[u % RING, k],
                    device,
                )
            )
            for k, device in enumerate(self.row)
        ]
        self.joined = u + 1

    def fold_row(self):
        u = self.done
        z, y, x, _ = self.where
        s = u % RING
        for copy in self.last[u]:
            copy.wait_recv()
        total = self.held[s, z, y, x].astype(WIDE)
        for k in range(self.split[0] - 1):
            total = total + self.from_row[s, k].astype(WIDE)
        self.put(u, total)
        for copy in self.diagonal[u] + self.aside[u] + self.last[u]:
            copy.wait_send()
        if u + RING < self.count:
            for device in self.row + list(self.beside):
                pl.semaphore_signal(self.sems[6].at[u], inc=1, device_id=device, device_id_type=MESH)
        self.done = u + 1

    def pump(self, times=1):
        for _ in range(times):
            if not self.round:
                if self.folded < self.swapped:
                    self.round.append(self.fold_core)
                if self.crossed < self.folded:
                    self.round += [self.fold_low, self.fold_high]
                if self.joined < self.crossed:
                    self.round.append(self.fold_side)
                if self.done < self.joined:
                    self.round.append(self.fold_row)
            if self.round:
                self.round.pop(0)()

    def end(self):
        while self.done < self.count:
            self.pump()
        for u in range(max(self.count - STAGES, 0), self.count):
            self.core[u].wait_send()


def pairs_kernel(split, shape, *refs):
    frames, groups, valid, block = shape
    it = iter(refs)
    take = lambda n: [next(it) for _ in range(n)]
    (x_in, dy_in, small_in), shards = take(3), take(7)
    out_ref, grad_ref = take(2)
    g_t_in, g_t_out, g_t_lin, g_s_in, g_s_out, g_up, g_down, g_small = take(8)
    small_all, full = next(it), take(7)
    xt, a_t, z_t, p_t, o_t, u_t, dy, x1, x2, a_s, z_s, p_s, o_s, a_m, act_g, slope, acc, at, low = take(19)
    b_recv, db_recv, dt_recv, sent, vec, sums, small_v, tile_v = take(8)
    w_a, w_b, w_up, w_down = take(4)
    bufs = take(7)
    ag_sems, rs_sems = take(7), take(7)
    ex_send, ex_recv, ex_own, load_sem, misc = take(5)

    where, row, beside = place(split)
    z, y, x, c = where
    nz, ny, nx, nc = split
    corner = (z * ny + y, (1 - x) * nc + (1 - c))
    greet(row + list(beside) + [corner])
    rows, width = x1.shape
    span = rows // frames
    pair = 2 * block
    chunk = pair
    mine = x * nc + c
    peers = [(beside[0], (1 - x) * nc + c), (beside[2], x * nc + (1 - c)), (corner, (1 - x) * nc + (1 - c))]
    waiting = []

    def cut(ref, index):
        if len(ref.shape) == 3:
            return ref.at[index]
        return ref.at[pl.ds(pl.multiple_of(index * block, TILE_ROWS), block)]

    def exchange(e, source, target, to_places):
        copies = []
        for f in range(frames):
            for k, (device, index) in enumerate(peers):
                src = f * groups + index if to_places else index * frames + f
                dst = mine * frames + f if to_places else f * groups + mine
                copies.append(
                    Move(
                        lambda src=src, dst=dst, k=k, f=f, device=device: remote(
                            cut(source, src), cut(target, dst), ex_send.at[e, k, f], ex_recv.at[e, k, f], device
                        )
                    )
                )
            src = f * groups + mine if to_places else mine * frames + f
            dst = mine * frames + f if to_places else f * groups + mine
            copies.append(
                Move(
                    lambda src=src, dst=dst, f=f: pltpu.make_async_copy(
                        cut(source, src), cut(target, dst), ex_own.at[e, f]
                    )
                )
            )
        return copies

    def arrive(copies):
        for copy in copies:
            copy.wait()

    moved = exchange(0, x_in, xt, True)
    dims = [s.shape for s in shards]
    chunks, ready = [(small_in, small_all, SMALL_ROWS, 0, SMALL_ROWS, 0, LANES, 0)], {}
    for k, (deep, wide) in enumerate(dims):
        tall = TALL if deep > dims[0][0] else 1
        cuts = PIECES if wide > 3 * width else FIRST if k == 0 else THIRD if k == 3 else 1
        for part in range(tall * cuts):
            count, cols = deep // tall, wide // cuts
            top, left = (part * count, 0) if tall > 1 else (0, part * cols)
            way = 2 if tall > 1 and part >= tall - LATE else 1 if k in OVER_Y else 0
            chunks.append((shards[k], full[k], deep, top, count, left, cols, way))
            ready[k, part] = len(chunks) - 1
    ag = Gather(split, where, row, beside, chunks, ag_sems, AHEAD)
    ag.pump(AHEAD)
    loads = {}

    class Load:
        def __init__(self, pairs):
            index = len(loads)
            self.copies = [
                Move(lambda a=a, b=b, k=k: pltpu.make_async_copy(a, b, load_sem.at[index, k]))
                for k, (a, b) in enumerate(pairs)
            ]

        def wait(self):
            for copy in self.copies:
                copy.wait()

    def load(key, source, target):
        if len(source.shape) == 2:
            pairs = [(source, target)]
        else:
            per = source.shape[2]
            pairs = [
                (source.at[:, k], target.at[:, pl.ds(k * per, per)]) for k in range(source.shape[1])
            ]
        loads[key] = Load(pairs)

    def fetch(key, k, target):
        for (which, _), i in ready.items():
            if which == k:
                ag.need(i)
        load(key, full[k], target)

    load("x", x_in, low)
    load("dy", dy_in, dy)
    sums[...] = jnp.zeros_like(sums)
    wb = [w_b.at[:, :, pl.ds(k * width, width)] for k in range(3)]
    wa = w_a
    ag.need(0)
    load("small", small_all, small_v)
    loads["small"].wait()
    devices = nz * ny * nx * nc
    per_row = devices * SMALL_ROWS // (nz * SMALL_ROWS)

    parts, step = {}, width // devices
    lanes = lax.broadcasted_iota(jnp.int32, (SMALL_ROWS, LANES), 1)

    def add(key, value):
        parts[key] = parts[key] + value if key in parts else value

    def put_at(name, tile, column, size):
        block_at, shift = column // LANES, column % LANES
        moved = pltpu.roll(tile, shift, 1) if shift else tile
        if shift + size <= LANES:
            add((name, block_at), moved)
        else:
            add((name, block_at), jnp.where(lanes >= shift, moved, 0.0))
            add((name, block_at + 1), jnp.where(lanes < shift, moved, 0.0))

    for r in range(devices):
        k, s = r // per_row, r % per_row
        tile = small_v[k, s * SMALL_ROWS : (s + 1) * SMALL_ROWS, :].astype(WIDE)
        for name, times in (("a", 1), ("b", 2), ("c", 4)):
            put_at(name, tile, r * step * times, step * times)
    per_line = width // LANES
    for k in range(per_line):
        vec[0:10, k * LANES : (k + 1) * LANES] = parts["a", k][0:10]
    for name, tile_row, top_line in (("b", 10, T_INB), ("b", 11, S_INB), ("c", 12, E_BIAS)):
        for k in range(per_line * (2 if name == "b" else 4)):
            to_line, col = top_line + k // per_line, k % per_line * LANES
            vec[to_line : to_line + 1, col : col + LANES] = parts[name, k][tile_row : tile_row + 1]

    arrive(moved)
    norm_stage(xt, vec, T_GAIN, a_t, chunk)
    fetch("t_in", 0, wa)
    two, three = (lambda: ag.pump(TWO)), (lambda: ag.pump(THREE))
    loads["t_in"].wait()
    inproj_stage(a_t, wa, vec, T_INB, z_t)
    all_frames = frames * groups
    fetch("t_out", 1, wb[0])
    time_attend(z_t, p_t, o_t, all_frames, block, 0, all_frames // 4)
    fetch("t_lin", 2, wb[1])
    time_attend(z_t, p_t, o_t, all_frames, block, all_frames // 4, all_frames // 2)

    def store(ref):
        def act(cols, total):
            if len(ref.shape) == 3:
                ref[:, :, cols] = total.reshape(ref.shape[:2] + (-1,)).astype(LOW)
            else:
                ref[:, cols] = total.astype(LOW)

        return act

    loads["t_out"].wait()
    project_stage(o_t, wb[0], vec, T_OUTB, store(u_t))
    loads["t_lin"].wait()
    project_stage(u_t, wb[1], vec, T_LINB, store(sent))
    moved = exchange(1, sent, b_recv, False)
    fetch("s_in", 3, wa)
    loads["x"].wait()
    arrive(moved)

    def first(k):
        r = tiles(k, chunk)
        x1[r, :] = low[r, :].astype(WIDE) + wide_rows(b_recv, k, chunk)

    each(rows // chunk, first)
    norm_stage(x1, vec, S_GAIN, a_s, chunk)
    loads["s_in"].wait()
    inproj_stage(a_s, wa, vec, S_INB, z_s)
    fetch("s_out", 4, wb[2])
    heads = width // LANES * frames
    space_attend(z_s, p_s, o_s, frames, span, valid, block, 0, heads // 2)
    ag.need(ready[5, 0])
    space_attend(z_s, p_s, o_s, frames, span, valid, block, heads // 2, heads)

    def add_x1(cut, total):
        x2[:, cut] = x1[:, cut] + total

    loads["s_out"].wait()
    project_stage(o_s, wb[2], vec, S_OUTB, add_x1)
    norm_stage(x2, vec, F_GAIN, a_m, chunk)
    for part in range(PIECES):
        half = w_up.shape[2] // PIECES
        cols = pl.ds(part * half, half)
        ag.need(min(ready[5, part] + 1, ready[6, 0]))
        load(f"up{part}", full[5].at[:, :, :, cols], w_up.at[:, :, cols])
        loads[f"up{part}"].wait()
        per = half // TILE
        expand_stage(a_m, w_up, vec, act_g, slope, part * per, (part + 1) * per)
    loads["dy"].wait()

    per = width // TILE
    plan = {}
    order = [(g_up, 4 * per), (g_s_out, per), (g_s_in, 3 * per), (g_t_lin, per), (g_t_out, per), (g_t_in, 3 * per), (g_small, 1)]
    units, sub = per - 1, SUB
    homes = {}
    for out, count in order:
        for k in range(count):
            if sub == SUB:
                units, sub = units + 1, 0
                plan[units] = []
            plan[units].append((out, k))
            homes[id(out), k] = (units, sub)
            sub += 1
    count = units + 1
    step_rows = g_up.shape[0]

    def put(u, total):
        if u < per:
            g_down[:, u * TILE : (u + 1) * TILE] = total
            return
        for b, (out, k) in enumerate(plan[u]):
            out[:, k * TILE : (k + 1) * TILE] = total[b * step_rows : (b + 1) * step_rows]

    rs = Totals(split, where, row, beside, count, bufs, rs_sems, put)
    staged = bufs[0]

    def down(k):
        at[:width, :] = act_g[:, tiles(k, width)].T
        for u in range(per):
            total = dot(at[:width, :], dy[:, u * TILE : (u + 1) * TILE])
            staged[u, k] = total.reshape((ny, nx, nc, -1, TILE)).astype(LOW)

    each(nz, down)
    ones = jnp.ones((16, rows), LOW)
    sums[R_BIAS : R_BIAS + 1, :] = dot(ones, dy[...])[:1]
    for u in range(per):
        rs.swap(u)
    fetch("down", 6, w_down)
    turns = lambda times: (lambda: rs.pump(times))

    def grads(out, dz_ref, table):
        count = out.shape[1] // TILE
        act_bias = bias_rows(sums, table, width)
        k = 0
        while k < count:
            u, b0 = homes[id(out), k]
            n = min(SUB - b0, count - k)
            if b0 == 0:
                rs.room(u)

            def act(i, k=k, u=u, b0=b0, n=n):
                t = k + i
                total = dot(at[...], dz_ref[:, tiles(t)])
                act_bias(t, total[width : width + 1])
                tile_v[...] = total[:width]
                for b in range(n):

                    @pl.when(i == b)
                    def _():
                        low_row = (b0 + b) * step_rows
                        staged[u % STAGES, :, :, :, :, low_row : low_row + step_rows, :] = (
                            tile_v[...].reshape((nz, ny, nx, nc, step_rows, TILE)).astype(LOW)
                        )

            each(n, act, 0, turns(GT), 4)
            k += n
            if b0 + n == SUB:
                rs.swap(u)
                rs.pump(GB)

    loads["down"].wait()
    reduce_back_stage(dy, w_down, slope, slope, turns(RB))

    hidden = act_g.shape[1]
    reduce_stage(act_g, w_down, vec, x2, store(low), turns(RD))
    out_copy = pltpu.make_async_copy(low, out_ref, misc.at[0])
    out_copy.start()
    turn_stage(a_m, at, turns(TN))
    grads(g_up, slope, [E_BIAS + k for k in range(hidden // width)])
    back_stage(slope, w_up, acc, turns(BK))
    out_copy.wait()

    def put_x2(k, dv):
        r = tiles(k, chunk)
        total = dy[r, :].astype(WIDE) + dv
        x2[r, :] = total
        low[r, :] = total.astype(LOW)

    norm_back_stage(x2, vec, F_GAIN, acc, sums, chunk, put_x2)
    load("t_in again", full[0], w_up.at[:, :, pl.ds(0, 3 * width)])
    turn_stage(o_s, at, turns(TN))
    grads(g_s_out, low, [S_OUTB])
    back_stage(low, wb[2], acc)
    rs.pump(BL)
    low[...] = acc[...].astype(LOW)
    dz = slope.at[:, pl.ds(0, 3 * width)]
    space_attend_back(z_s, p_s, low, dz, frames, span, pump=lambda: rs.pump(SB))
    back_stage(dz, wa, acc, turns(BK))

    def put_x1(k, dv):
        r = tiles(k, chunk)
        total = x2[r, :] + dv
        x1[r, :] = total
        put_rows(sent, k, chunk, total)

    norm_back_stage(x1, vec, S_GAIN, acc, sums, chunk, put_x1)
    moved = exchange(2, sent, db_recv, True)
    turn_stage(a_s, at, turns(TN))
    grads(g_s_in, dz, [S_INB, None, S_INB + 1])
    turn_stage(u_t, at, turns(TN))
    arrive(moved)

    def flat(k):
        low[tiles(k, chunk), :] = wide_rows(db_recv, k, chunk).astype(LOW)

    each(rows // chunk, flat)
    grads(g_t_lin, low, [T_LINB])
    back_stage(low, wb[1], acc)
    rs.pump(BL)
    low[...] = acc[...].astype(LOW)
    turn_stage(o_t, at, turns(TN))
    grads(g_t_out, low, [T_OUTB])
    back_stage(low, wb[0], acc)
    rs.pump(BL)
    low[...] = acc[...].astype(LOW)
    time_attend_back(z_t, p_t, low, dz, x2, acc, all_frames, block, lambda: rs.pump(TB))
    loads["t_in again"].wait()
    back_stage(dz, w_up.at[:, :, pl.ds(0, 3 * width)], acc, turns(BK))

    def put_t(k, dv):
        put_rows(sent, k, chunk, dv)

    norm_back_stage(xt, vec, T_GAIN, acc, sums, chunk, put_t)
    moved = exchange(3, sent, dt_recv, False)
    turn_stage(a_t, at, turns(TN))
    grads(g_t_in, dz, [T_INB, None, T_INB + 1])

    u, b0 = homes[id(g_small), 0]
    if b0 == 0:
        rs.room(u)
    low_row = b0 * step_rows
    line = lax.broadcasted_iota(jnp.int32, (step_rows, LANES), 0)
    lanes = lax.broadcasted_iota(jnp.int32, (step_rows, LANES), 1)
    blocks = {}

    def source(name, k):
        if (name, k) not in blocks:
            row, cols = k // per_line, pl.ds(k % per_line * LANES, LANES)
            if name == "a":
                rest = jnp.zeros((step_rows - SMALL_ROWS, LANES), WIDE)
                value = jnp.concatenate([sums[0:SMALL_ROWS, cols], rest], axis=0)
            elif name == "b":
                first, second = sums[T_INB + row : T_INB + row + 1, cols], sums[S_INB + row : S_INB + row + 1, cols]
                value = jnp.where(line == 10, first, second)
            else:
                value = sums[E_BIAS + row : E_BIAS + row + 1, cols] + jnp.zeros((step_rows, LANES), WIDE)
            blocks[name, k] = value
        return blocks[name, k]

    def taken(name, column, size):
        block_at, shift = column // LANES, column % LANES
        value = source(name, block_at)
        if shift == 0:
            return value
        value = pltpu.roll(value, LANES - shift, 1)
        if shift + size > LANES:
            after = pltpu.roll(source(name, block_at + 1), LANES - shift, 1)
            value = jnp.where(lanes < LANES - shift, value, after)
        return value

    blank = jnp.zeros((step_rows, TILE - LANES), WIDE)
    for r in range(devices):
        a, b, d = (
            taken(name, r * step * times, step * times)
            for name, times in (("a", 1), ("b", 2), ("c", 4))
        )
        tile = jnp.where(line < 10, a, jnp.where(line < 12, b, d))
        slot = (r // (ny * nx * nc), r // (nx * nc) % ny, r // nc % nx, r % nc)
        place_at = (u % STAGES,) + slot + (slice(low_row, low_row + step_rows), slice(None))
        staged[place_at] = jnp.concatenate([tile, blank], axis=1).astype(LOW)
    rs.swap(u)
    arrive(moved)

    def last(k):
        r = tiles(k, chunk)
        x1[r, :] = x1[r, :] + wide_rows(dt_recv, k, chunk)

    each(rows // chunk, last)
    grad_copy = pltpu.make_async_copy(x1, grad_ref, misc.at[1])
    grad_copy.start()
    rs.end()
    ag.end()
    grad_copy.wait()


def whole_layer(split, shape, x, dy, small, shards):
    frames, groups, valid, block = shape
    rows, width = x.shape
    nz, ny, nx, nc = split
    low, wide = LOW, WIDE
    hidden = shards[5].shape[1]
    step = shards[0].shape[0]
    shapes = [(item.shape, wide) for item in shards] + [((step, TILE), wide)]
    token, full = ((rows, width), low), ((rows, width), wide)
    gathered = [((nz, ny * nx, nc * SMALL_ROWS, LANES), low)]
    gathered += [((nz, ny * nx, nc * item.shape[0], item.shape[1]), low) for item in shards]
    joined = [((s[0], s[1] * s[2], s[3]), kind) for s, kind in gathered]
    hbm = pl.BlockSpec(memory_space=pl.ANY)
    vmem = pl.BlockSpec(memory_space=pltpu.VMEM)
    outs = [token, full] + shapes + gathered
    out_specs = [hbm, hbm] + [vmem] * len(shapes) + [hbm] * len(gathered)
    span = rows // frames
    three, big = ((rows, 3 * width), low), ((rows, hidden), low)
    cuts = ((frames * groups, block, width), low)
    scratch = [cuts, token, three, ((frames * groups, rows, LANES), low), token, token, token, full, full]
    scratch += [token, three, ((frames * HEADS, span, span), low), token, token, big, big, full]
    scratch += [((width + 16, rows), low), token, cuts, cuts, cuts, cuts, ((24, width), wide), ((24, width), wide)]
    scratch += [joined[0], ((width, TILE), wide)]
    scratch += [joined[1], joined[1], joined[6], joined[7]]
    deep = SUB * step
    scratch += [((STAGES, nz, ny, nx, nc, deep, TILE), low), ((RING, nz, ny, nx, deep, TILE), low)]
    scratch += [((RING, nz, deep, TILE // 2), low)] * 2 + [((RING, nz, deep, TILE), low)] * 2
    scratch += [((RING, nz - 1, deep, TILE), low)]
    sem = pltpu.SemaphoreType.DMA
    chunks = 1 + FIRST + THIRD + 3 + PIECES + TALL
    units = -(-(sum(item.shape[1] for item in shards[:6]) // TILE + 1) // SUB) + width // TILE
    sems = [sem((chunks, nz - 1))] * 2 + [sem((chunks, 4))] * 4 + [sem((chunks,))]
    sems += [sem((RING,))] * 2 + [sem((RING, 4))] * 2 + [sem((RING, nz - 1))] * 2
    sems += [pltpu.SemaphoreType.REGULAR((units,))]
    sems += [sem((4, 3, frames))] * 2 + [sem((4, frames)), sem((12, ny * nx)), sem((2,))]
    result = pl.pallas_call(
        functools.partial(pairs_kernel, split, shape),
        out_shape=[jax.ShapeDtypeStruct(s, kind) for s, kind in outs],
        in_specs=[hbm] * (3 + len(shards)),
        out_specs=out_specs,
        scratch_shapes=[pltpu.VMEM(s, kind) for s, kind in scratch] + sems,
        compiler_params=pltpu.CompilerParams(
            collective_id=0, has_side_effects=True, vmem_limit_bytes=63 << 20
        ),
        name="whole_layer",
    )(x, dy, small, *shards)
    return result[:10]


VECTOR_ROWS = (0, 1, 10, 2, 3, 4, 5, 12, 6, 7, 8, 14, 9)


SMALL_PLACES = {row: (row, 0) for row in range(10)} | {10: (10, 0), 12: (11, 0), 14: (12, 0)}


def pack_small(vectors):
    rows = {SMALL_PLACES[at][0]: item for at, item in zip(VECTOR_ROWS, vectors)}
    line = []
    for k in range(len(rows)):
        line.append(rows[k].reshape((1, -1)))
        line.append(jnp.zeros((1, LANES - rows[k].shape[0]), LOW))
    line.append(jnp.zeros((1, (SMALL_ROWS - len(rows)) * LANES), LOW))
    return jnp.concatenate(line, axis=1).reshape((SMALL_ROWS, LANES))


def hand_out(blocks, tile, widths):
    count = len(blocks)

    def body(*refs):
        ins, tile_ref = refs[:count], refs[count]
        outs, thin = refs[count + 1 : 2 * count + 1], refs[2 * count + 1 : -1]
        sems = refs[-1]
        copies = [pltpu.make_async_copy(a, b, sems.at[k]) for k, (a, b) in enumerate(zip(ins, outs))]
        for copy in copies:
            copy.start()
        for k, (row, width) in enumerate(widths):
            thin[k][...] = tile_ref[row : row + 1, :width]
        for copy in copies:
            copy.wait()

    hbm, vmem = pl.BlockSpec(memory_space=pl.ANY), pl.BlockSpec(memory_space=pltpu.VMEM)
    out = pl.pallas_call(
        body,
        out_shape=[jax.ShapeDtypeStruct(item.shape, WIDE) for item in blocks]
        + [jax.ShapeDtypeStruct((1, width), WIDE) for _, width in widths],
        in_specs=[vmem] * (count + 1),
        out_specs=[hbm] * count + [vmem] * len(widths),
        scratch_shapes=[pltpu.SemaphoreType.DMA((count,))],
        name="hand_out",
    )(*blocks, tile)
    return out[:count], [item.reshape(-1) for item in out[count:]]


def sum_native(terms):
    received = [
        lax.all_to_all(
            item.astype(LOW), "clip", split_axis=0, concat_axis=0, tiled=True
        ).astype(WIDE)
        for item in stack_rows(terms, lax.axis_size("clip"))
    ]
    return [
        lax.psum_scatter(item.astype(LOW), "frame", scatter_dimension=0, tiled=True).astype(WIDE)
        for item in fold_rows(received)
    ]


def on_device(
    video_tokens,
    time_gain,
    time_shift,
    time_inproj,
    time_inbias,
    time_outproj,
    time_outbias,
    time_linear,
    time_linbias,
    space_gain,
    space_shift,
    space_inproj,
    space_inbias,
    space_outproj,
    space_outbias,
    feed_gain,
    feed_shift,
    expand_weight,
    expand_bias,
    reduce_weight,
    reduce_bias,
    cotangent,
):
    split = inner_split(time_gain.shape[0])
    params = [
        time_gain,
        time_shift,
        time_inproj,
        time_inbias,
        time_outproj,
        time_outbias,
        time_linear,
        time_linbias,
        space_gain,
        space_shift,
        space_inproj,
        space_inbias,
        space_outproj,
        space_outbias,
        feed_gain,
        feed_shift,
        expand_weight,
        expand_bias,
        reduce_weight,
        reduce_bias,
    ]
    frames, places, width = video_tokens.shape[1:]
    groups = lax.axis_size("frame")
    valid = places // groups
    block = -(-valid // TILE_ROWS) * TILE_ROWS
    rows = frames * groups * block

    def padded(tokens):
        cut = tokens.reshape((frames, groups, valid, width))
        return jnp.pad(cut, ((0, 0), (0, 0), (0, block - valid), (0, 0)))

    def to_places(tokens):
        return lax.all_to_all(
            tokens.reshape((frames, groups, block, width)),
            "frame",
            split_axis=1,
            concat_axis=0,
            tiled=True,
        ).reshape((rows, width))

    def to_frames(tokens):
        return lax.all_to_all(
            tokens.reshape((frames * groups, 1, block, width)),
            "frame",
            split_axis=0,
            concat_axis=1,
            tiled=True,
        ).reshape((rows, width))

    def trimmed(tokens):
        cut = tokens.reshape((frames, groups, block, width))[:, :, :valid]
        return cut.reshape((1, frames, places, width))

    def weight(item):
        return item.reshape((4, -1, item.shape[1]))

    if split is not None:
        small = pack_small([item for item in params if item.ndim == 1])
        layer_out, input_grad, *sums = whole_layer(
            split,
            (frames, groups, valid, block),
            padded(video_tokens).reshape((rows, width)),
            padded(cotangent).reshape((rows, width)),
            small,
            [item for item in params if item.ndim == 2],
        )
        widths = [
            (SMALL_PLACES[at][0], item.shape[0])
            for at, item in zip(VECTOR_ROWS, [item for item in params if item.ndim == 1])
        ]
        wide, thin = hand_out(sums[:7], sums[7], widths)
        wide, thin = iter(wide), iter(thin)
        summed = [next(wide) if item.ndim == 2 else next(thin) for item in params]
        return (trimmed(layer_out), trimmed(input_grad)) + tuple(summed)

    full = [lax.all_gather(item, ("clip", "frame"), axis=0, tiled=True) for item in params]
    thin = [item for item in full if item.ndim == 1]
    t_in, t_out, t_lin, s_in, s_out, w_up, w_down = [weight(item) for item in full if item.ndim == 2]
    pieces = sorted(zip(VECTOR_ROWS, thin), key=lambda pair: pair[0])
    vec = jnp.concatenate([item.reshape((-1, width)) for _, item in pieces], axis=0)
    vec = jnp.pad(vec, ((0, 24 - vec.shape[0]), (0, 0))).astype(WIDE)
    tokens, d_out = padded(video_tokens), padded(cotangent)
    own = tokens.reshape((rows, width))
    placed = to_places(tokens)
    b_t, a_t, z_t, p_t, o_t, u_t = time_forward(block, placed, vec, t_in, t_out, t_lin)
    layer_out, d_x1, d_b, g_s_in, g_s_out, g_up, g_down, sums_s = space_layer(
        (frames, valid, block),
        own,
        to_frames(b_t),
        d_out.reshape((rows, width)),
        vec,
        s_in,
        s_out,
        w_up,
        w_down,
    )
    d_t, g_t_in, g_t_out, g_t_lin, sums_t = time_backward(
        block, to_places(d_b), placed, a_t, z_t, p_t, o_t, u_t, vec, t_in, t_out, t_lin
    )
    input_grad = d_x1 + to_frames(d_t).astype(WIDE)
    sums = sums_s + sums_t
    wide = iter(
        [item.reshape((-1, width if item is g_down else item.shape[2])) for item in
         (g_t_in, g_t_out, g_t_lin, g_s_in, g_s_out, g_up, g_down)]
    )
    rows_of = iter(VECTOR_ROWS)
    terms = []
    for item in params:
        if item.ndim == 2:
            terms.append(next(wide))
        else:
            at = next(rows_of)
            count = item.shape[0] * lax.axis_size(("clip", "frame")) // width
            terms.append(sums[at : at + count].reshape(-1))
    summed = sum_native(terms)
    return (trimmed(layer_out), trimmed(input_grad)) + tuple(summed)


def solution(mesh):
    return jax.shard_map(
        on_device,
        mesh=mesh,
        in_specs=(
            P("clip", "frame", None, None),
            P(("clip", "frame")),
            P(("clip", "frame")),
            P(("clip", "frame"), None),
            P(("clip", "frame")),
            P(("clip", "frame"), None),
            P(("clip", "frame")),
            P(("clip", "frame"), None),
            P(("clip", "frame")),
            P(("clip", "frame")),
            P(("clip", "frame")),
            P(("clip", "frame"), None),
            P(("clip", "frame")),
            P(("clip", "frame"), None),
            P(("clip", "frame")),
            P(("clip", "frame")),
            P(("clip", "frame")),
            P(("clip", "frame"), None),
            P(("clip", "frame")),
            P(("clip", "frame"), None),
            P(("clip", "frame")),
            P("clip", "frame", None, None),
        ),
        out_specs=(
            P("clip", "frame", None, None),
            P("clip", "frame", None, None),
            P(("clip", "frame")),
            P(("clip", "frame")),
            P(("clip", "frame"), None),
            P(("clip", "frame")),
            P(("clip", "frame"), None),
            P(("clip", "frame")),
            P(("clip", "frame"), None),
            P(("clip", "frame")),
            P(("clip", "frame")),
            P(("clip", "frame")),
            P(("clip", "frame"), None),
            P(("clip", "frame")),
            P(("clip", "frame"), None),
            P(("clip", "frame")),
            P(("clip", "frame")),
            P(("clip", "frame")),
            P(("clip", "frame"), None),
            P(("clip", "frame")),
            P(("clip", "frame"), None),
            P(("clip", "frame")),
        ),
        check_vma=False,
    )
```

```python
import functools

import jax
import jax.numpy as jnp
from jax import lax
from jax.experimental import pallas as pl
from jax.experimental.pallas import tpu as pltpu
from jax.sharding import PartitionSpec as P

MESH = pl.DeviceIdType.MESH
TILE_ROWS = 8
LOW = jnp.bfloat16
WIDE = jnp.float32
HEADS = 12
norm_eps = 1e-06
LANES = 128
TILE = 256
T_GAIN, T_SHIFT, T_OUTB, T_LINB, S_GAIN, S_SHIFT, S_OUTB, F_GAIN, F_SHIFT, R_BIAS, T_INB, S_INB, E_BIAS = 0, 1, 2, 3, 4, 5, 6, 7, 8, 9, 10, 12, 14


def dot(a, b):
    return lax.dot_general(a, b, (((1,), (0,)), ((), ())), preferred_element_type=WIDE)


def dot_nt(a, b):
    return lax.dot_general(a, b, (((1,), (1,)), ((), ())), preferred_element_type=WIDE)


def each(count, act, start=0, pump=None, every=1):
    def step(k, carry):
        act(k)
        return carry

    stride = count - start if pump is None else every
    for at in range(start, count, stride):
        lax.fori_loop(at, min(at + stride, count), step, 0)
        if pump is not None:
            pump()


def tiles(k, size=TILE):
    return pl.ds(pl.multiple_of(k * size, size), size)


def columns(w_ref, cut):
    block = w_ref[:, :, cut]
    return block.reshape((block.shape[0] * block.shape[1], block.shape[2]))


def wide_rows(ref, k, size):
    if len(ref.shape) == 2:
        return ref[tiles(k, size), :].astype(WIDE)
    per = size // ref.shape[1]
    block = ref[pl.ds(k * per, per), :, :].astype(WIDE)
    return block.reshape((size, ref.shape[2]))


def put_rows(ref, k, size, value):
    if len(ref.shape) == 2:
        ref[tiles(k, size), :] = value.astype(ref.dtype)
    else:
        per = size // ref.shape[1]
        ref[pl.ds(k * per, per), :, :] = value.reshape((per,) + ref.shape[1:]).astype(ref.dtype)


def normal(x):
    center = x - jnp.mean(x, axis=-1, keepdims=True)
    inverse = lax.rsqrt(jnp.mean(center * center, axis=-1, keepdims=True) + norm_eps)
    return center * inverse, inverse


def norm_stage(x_ref, vec, gain_row, a_ref, block, pump=None):
    gain, shift = vec[gain_row : gain_row + 1, :], vec[gain_row + 1 : gain_row + 2, :]

    def act(k):
        unit, _ = normal(wide_rows(x_ref, k, block))
        a_ref[tiles(k, block), :] = (unit * gain + shift).astype(LOW)

    each(a_ref.shape[0] // block, act, 0, pump, 2)


def norm_back_stage(x_ref, vec, gain_row, da_ref, sums, block, store):
    gain = vec[gain_row : gain_row + 1, :]
    width = da_ref.shape[1]

    def step(k, carry):
        unit, inverse = normal(wide_rows(x_ref, k, block))
        da = da_ref[tiles(k, block), :]
        e = da * gain
        dv = inverse * (
            e
            - jnp.mean(e, axis=-1, keepdims=True)
            - unit * jnp.mean(e * unit, axis=-1, keepdims=True)
        )
        store(k, dv)
        grad_gain, grad_shift = carry
        fold = lambda v: jnp.sum(v.reshape(block // 8, 8, width), axis=0)
        return grad_gain + fold(da * unit), grad_shift + fold(da)

    zero = jnp.zeros((8, width), WIDE)
    grad_gain, grad_shift = lax.fori_loop(0, da_ref.shape[0] // block, step, (zero, zero))
    sums[gain_row : gain_row + 1, :] = jnp.sum(grad_gain, axis=0, keepdims=True)
    sums[gain_row + 1 : gain_row + 2, :] = jnp.sum(grad_shift, axis=0, keepdims=True)


def inproj_stage(a_ref, w_ref, vec, bias_row, z_ref, pump=None):
    width = a_ref.shape[1]
    for part in range(3):

        def act(k, part=part):
            inner = tiles(k)
            cut = pl.ds(pl.multiple_of(part * width + k * TILE, TILE), TILE)
            total = dot(a_ref[...], columns(w_ref, cut))
            if part != 1:
                row = bias_row + part // 2
                total = total + vec[row : row + 1, inner]
            z_ref[:, cut] = total.astype(LOW)

        each(width // TILE, act, 0, pump, 3)


def project_stage(a_ref, w_ref, vec, bias_row, store, pump=None):
    def act(k):
        cut = tiles(k)
        store(cut, dot(a_ref[...], columns(w_ref, cut)) + vec[bias_row : bias_row + 1, cut])

    each(w_ref.shape[2] // TILE, act, 0, pump, 3)


def back_stage(dz_ref, w_ref, acc_ref, pump=None):
    width = acc_ref.shape[1]
    parts = w_ref.shape[2] // width
    acc_ref[...] = dot_nt(dz_ref[:, :width], columns(w_ref, pl.ds(0, width)))

    def act(k):
        cut = tiles(k + 1, width)
        acc_ref[...] = acc_ref[...] + dot_nt(dz_ref[:, cut], columns(w_ref, cut))

    if parts > 1:
        each(parts - 1, act, 0, pump)


def turn_stage(a_ref, at_ref, pump=None):
    width = a_ref.shape[1]

    def act(k):
        at_ref[tiles(k), :] = a_ref[:, tiles(k)].T

    each(width // TILE, act, 0, pump, 3)
    at_ref[width:, :] = jnp.ones((at_ref.shape[0] - width, at_ref.shape[1]), LOW)


def weight_stage(at_ref, dz_ref, g_ref, bias):
    depth, rows, _ = g_ref.shape
    full = depth * rows

    def act(k):
        cut = tiles(k)
        total = dot(at_ref[...], dz_ref[:, cut])
        g_ref[:, :, cut] = total[:full].astype(LOW).reshape((depth, rows, TILE))
        bias(k, total[full : full + 1])

    each(g_ref.shape[2] // TILE, act)


def bias_rows(sums, table, width):
    def act(k, total):
        per = width // TILE
        for part, row in enumerate(table):
            if row is None:
                continue

            @pl.when((k >= part * per) & (k < (part + 1) * per))
            def _():
                sums[row : row + 1, tiles(k - part * per)] = total

    return act


def low_head(rows):
    lane = lax.broadcasted_iota(jnp.int32, (rows, LANES), 1)
    return lane < LANES // 2


def space_attend(z_ref, p_ref, o_ref, frames, rows, valid, block, start=0, stop=None, pump=None):
    width = o_ref.shape[1]
    pairs = width // LANES
    scale = (LANES // 2) ** -0.5

    def act(step):
        f, pair = step // pairs, step % pairs
        span = tiles(f, rows)
        q = z_ref[span, pl.ds(pl.multiple_of(pair * LANES, LANES), LANES)]
        k = z_ref[span, pl.ds(pl.multiple_of(width + pair * LANES, LANES), LANES)]
        v = z_ref[span, pl.ds(pl.multiple_of(2 * width + pair * LANES, LANES), LANES)]
        first = low_head(rows)
        vt = v.T
        keep = lax.broadcasted_iota(jnp.int32, (rows, rows), 0) % block < valid
        outs = []
        for side in range(2):
            mine = first if side == 0 else ~first
            scores = dot_nt(k, jnp.where(mine, q, jnp.zeros_like(q))) * scale
            scores = jnp.where(keep, scores, -1e30)
            e = jnp.exp(scores - jnp.max(scores, axis=0, keepdims=True))
            p = (e * (1.0 / jnp.sum(e, axis=0, keepdims=True))).astype(LOW)
            p_ref[2 * step + side] = p
            outs.append(dot(vt, p))
        top = lax.broadcasted_iota(jnp.int32, (LANES, rows), 0) < LANES // 2
        o = jnp.where(top, outs[0], outs[1]).T
        o_ref[span, pl.ds(pl.multiple_of(pair * LANES, LANES), LANES)] = o.astype(LOW)

    each(frames * pairs if stop is None else stop, act, start, pump, 2)


def space_attend_back(z_ref, p_ref, do_ref, dz_ref, frames, rows, start=0, stop=None, pump=None):
    width = do_ref.shape[1]
    pairs = width // LANES
    scale = (LANES // 2) ** -0.5

    def act(step):
        f, pair = step // pairs, step % pairs
        span = tiles(f, rows)
        cut_q = pl.ds(pl.multiple_of(pair * LANES, LANES), LANES)
        cut_k = pl.ds(pl.multiple_of(width + pair * LANES, LANES), LANES)
        cut_v = pl.ds(pl.multiple_of(2 * width + pair * LANES, LANES), LANES)
        q, k, v, do = z_ref[span, cut_q], z_ref[span, cut_k], z_ref[span, cut_v], do_ref[span, cut_q]
        kt = k.T
        first = low_head(rows)
        dk = dv = None
        turned = []
        for side in range(2):
            mine = first if side == 0 else ~first
            q_side = jnp.where(mine, q, jnp.zeros_like(q))
            do_side = jnp.where(mine, do, jnp.zeros_like(do))
            p_low = p_ref[2 * step + side]
            p = p_low.astype(WIDE)
            dp = dot_nt(v, do_side)
            inner = jnp.sum(dp * p, axis=0, keepdims=True)
            ds = (p * (dp - inner)).astype(LOW)
            dv_side, dk_side = dot(p_low, do_side), dot(ds, q_side)
            dv = dv_side if dv is None else dv + dv_side
            dk = dk_side if dk is None else dk + dk_side
            turned.append(dot(kt, ds))
        top = lax.broadcasted_iota(jnp.int32, (LANES, rows), 0) < LANES // 2
        dq = jnp.where(top, turned[0], turned[1]).T
        dz_ref[span, cut_q] = (dq * scale).astype(LOW)
        dz_ref[span, cut_k] = (dk * scale).astype(LOW)
        dz_ref[span, cut_v] = dv.astype(LOW)

    each(frames * pairs if stop is None else stop, act, start, pump, 2)


def head_sum(width):
    row = lax.broadcasted_iota(jnp.int32, (width, LANES), 0) // (width // HEADS)
    col = lax.broadcasted_iota(jnp.int32, (width, LANES), 1)
    return (row == col).astype(WIDE).astype(LOW)


def head_spread(width):
    row = lax.broadcasted_iota(jnp.int32, (LANES, width), 0)
    col = lax.broadcasted_iota(jnp.int32, (LANES, width), 1) // (width // HEADS)
    return (row == col).astype(WIDE).astype(LOW)


def by_head(product, pick):
    high = product.astype(LOW)
    rest = (product - high.astype(WIDE)).astype(LOW)
    return dot(high, pick) + dot(rest, pick)


def time_attend(z_ref, p_ref, o_ref, frames, block, start=0, stop=None, pump=None):
    width = o_ref.shape[1]
    scale = (width // HEADS) ** -0.5
    pick, spread = head_sum(width), head_spread(width)
    spans = [slice(k * block, (k + 1) * block) for k in range(frames)]

    def act(pair):
        rows = tiles(pair, 2 * block)
        q = z_ref[rows, :width].astype(WIDE)
        scores = [[], []]
        for span in spans:
            k = z_ref[span, width : 2 * width].astype(WIDE)
            for half in range(2):
                scores[half].append(by_head(q[spans[half]] * k, pick) * scale)
        probs = []
        for half in range(2):
            top = functools.reduce(jnp.maximum, scores[half])
            e = [jnp.exp(s - top) for s in scores[half]]
            inverse = 1.0 / functools.reduce(jnp.add, e)
            probs.append([item * inverse for item in e])
        out = [jnp.zeros((block, width), WIDE)] * 2
        for k, span in enumerate(spans):
            v = z_ref[span, 2 * width :].astype(WIDE)
            for half in range(2):
                p = probs[half][k]
                p = p.astype(LOW)
                p_ref[2 * pair + half, span, :] = p
                out[half] = out[half] + dot(p, spread) * v
        o_ref[rows, :] = jnp.concatenate(out, axis=0).astype(LOW)

    each(frames // 2 if stop is None else stop, act, start, pump)


def time_attend_back(z_ref, p_ref, do_ref, dz_ref, dk_ref, dv_ref, frames, block, pump=None):
    width = do_ref.shape[1]
    scale = (width // HEADS) ** -0.5
    pick, spread = head_sum(width), head_spread(width)
    spans = [slice(k * block, (k + 1) * block) for k in range(frames)]
    dk_ref[...] = jnp.zeros_like(dk_ref)
    dv_ref[...] = jnp.zeros_like(dv_ref)

    def act(pair):
        rows = tiles(pair, 2 * block)
        do = do_ref[rows, :].astype(WIDE)
        q = z_ref[rows, :width].astype(WIDE)
        dps = [[], []]
        inner = [jnp.zeros((block, LANES), WIDE)] * 2
        for span in spans:
            v = z_ref[span, 2 * width :].astype(WIDE)
            for half in range(2):
                dp = by_head(do[spans[half]] * v, pick)
                inner[half] = inner[half] + dp * p_ref[2 * pair + half, span, :].astype(WIDE)
                dps[half].append(dp)
        dq = [jnp.zeros((block, width), WIDE)] * 2
        for at, span in enumerate(spans):
            k = z_ref[span, width : 2 * width].astype(WIDE)
            dk, dv = dk_ref[span, :], dv_ref[span, :]
            for half in range(2):
                p = p_ref[2 * pair + half, span, :]
                ds = dot((p.astype(WIDE) * (dps[half][at] - inner[half])).astype(LOW), spread)
                dq[half] = dq[half] + ds * k
                dk = dk + ds * q[spans[half]]
                dv = dv + dot(p, spread) * do[spans[half]]
            dk_ref[span, :] = dk
            dv_ref[span, :] = dv
        dz_ref[rows, :width] = (jnp.concatenate(dq, axis=0) * scale).astype(LOW)

    each(frames // 2, act, 0, pump)

    def out(pair):
        rows = tiles(pair, 2 * block)
        dz_ref[rows, width : 2 * width] = (dk_ref[rows, :] * scale).astype(LOW)
        dz_ref[rows, 2 * width :] = dv_ref[rows, :].astype(LOW)

    each(frames // 2, out)


def expand_stage(a_ref, w_ref, vec, g_ref, slope_ref, start=0, stop=None, pump=None):
    width = a_ref.shape[1]
    per = width // TILE

    def act(k):
        cut = tiles(k)
        h = dot(a_ref[...], columns(w_ref, cut))
        inner = tiles(k % per)
        bias = vec[pl.ds(E_BIAS + k // per, 1), inner]
        h = h + bias
        cdf = 0.5 * (1.0 + lax.erf(h * (0.5 ** 0.5)))
        g_ref[:, cut] = (h * cdf).astype(LOW)
        slope_ref[:, cut] = (cdf + h * (jnp.exp(-0.5 * h * h) * 0.3989422804014327)).astype(LOW)

    each(w_ref.shape[2] // TILE if stop is None else stop, act, start, pump, 2)


def reduce_stage(g_ref, w_ref, vec, x_ref, out_store, pump=None):
    depth, rows, width = w_ref.shape

    def act(k):
        cut = tiles(k)
        total = x_ref[:, cut] + vec[R_BIAS : R_BIAS + 1, cut]
        for z in range(depth):
            total = total + dot(g_ref[:, z * rows : (z + 1) * rows], w_ref[z, :, cut])
        out_store(cut, total)

    each(width // TILE, act, 0, pump, 3)


def reduce_back_stage(dm_ref, w_ref, slope_ref, dh_ref, pump=None):
    depth, rows, _ = w_ref.shape
    per = rows // TILE

    def act(k):
        cut = tiles(k)
        block = w_ref[k // per, tiles(k % per), :]
        dh_ref[:, cut] = (dot_nt(dm_ref[...], block) * slope_ref[:, cut].astype(WIDE)).astype(LOW)

    each(depth * per, act, 0, pump, 4)


def reduce_grad_stage(g_ref, gt_ref, dm_ref, out_ref, sums):
    depth, rows, width = out_ref.shape

    def act(k):
        z, part = k // (rows // TILE), k % (rows // TILE)
        turned = g_ref[:, tiles(k)].T
        gt_ref[...] = turned
        out_ref[z, tiles(part), :] = dot(gt_ref[...], dm_ref[...]).astype(LOW)

    each(depth * rows // TILE, act)
    ones = jnp.ones((16, dm_ref.shape[0]), LOW)
    sums[R_BIAS : R_BIAS + 1, :] = dot(ones, dm_ref[...])[:1]


def vmem_call(body, outs, ins, scratch, name):
    return pl.pallas_call(
        body,
        out_shape=[jax.ShapeDtypeStruct(shape, kind) for shape, kind in outs],
        in_specs=[pl.BlockSpec(memory_space=pltpu.VMEM)] * len(ins),
        out_specs=[pl.BlockSpec(memory_space=pltpu.VMEM)] * len(outs),
        scratch_shapes=[pltpu.VMEM(shape, kind) for shape, kind in scratch],
        compiler_params=pltpu.CompilerParams(vmem_limit_bytes=60 << 20),
        name=name,
    )(*ins)


def time_forward(block, x, vec, w_in, w_out, w_lin):
    rows, width = x.shape
    frames = rows // block

    def body(x_ref, vec_ref, w_in, w_out, w_lin, b_ref, a_ref, z_ref, p_ref, o_ref, u_ref):
        def store(ref):
            def act(cut, total):
                ref[:, cut] = total.astype(LOW)

            return act

        norm_stage(x_ref, vec_ref, T_GAIN, a_ref, 2 * block)
        inproj_stage(a_ref, w_in, vec_ref, T_INB, z_ref)
        time_attend(z_ref, p_ref, o_ref, frames, block)
        project_stage(o_ref, w_out, vec_ref, T_OUTB, store(u_ref))
        project_stage(u_ref, w_lin, vec_ref, T_LINB, store(b_ref))

    token = ((rows, width), LOW)
    outs = [token, token, ((rows, 3 * width), LOW), ((frames, rows, LANES), LOW), token, token]
    return vmem_call(body, outs, (x, vec, w_in, w_out, w_lin), [], "time_forward")


def space_layer(shape, x, b, dy, vec, w_in, w_out, w_up, w_down):
    frames, valid, block = shape
    rows, width = x.shape
    span = rows // frames
    hidden = w_up.shape[2]
    heads_all = frames * HEADS

    def body(x_ref, b_ref, dy_ref, vec_ref, w_in, w_out, w_up, w_down, out_ref, dx1_ref, db_ref,
             g_in, g_out, g_up, g_down, sums, x1, x2, a_s, z_s, p_s, o_s, a_m, act_g, slope, dh, acc, at, gt, low):
        sums[...] = jnp.zeros_like(sums)

        def first(k):
            r = tiles(k, 2 * block)
            x1[r, :] = x_ref[r, :].astype(WIDE) + b_ref[r, :].astype(WIDE)

        each(rows // (2 * block), first)
        norm_stage(x1, vec_ref, S_GAIN, a_s, 2 * block)
        inproj_stage(a_s, w_in, vec_ref, S_INB, z_s)
        space_attend(z_s, p_s, o_s, frames, span, valid, block)

        def add_x1(cut, total):
            x2[:, cut] = x1[:, cut] + total

        project_stage(o_s, w_out, vec_ref, S_OUTB, add_x1)
        norm_stage(x2, vec_ref, F_GAIN, a_m, 2 * block)
        expand_stage(a_m, w_up, vec_ref, act_g, slope)

        def put_out(cut, total):
            out_ref[:, cut] = total.astype(LOW)

        reduce_stage(act_g, w_down, vec_ref, x2, put_out)
        reduce_grad_stage(act_g, gt, dy_ref, g_down, sums)
        reduce_back_stage(dy_ref, w_down, slope, dh)
        turn_stage(a_m, at)
        weight_stage(at, dh, g_up, bias_rows(sums, [E_BIAS + k for k in range(hidden // width)], width))
        back_stage(dh, w_up, acc)

        def put_x2(k, dv):
            r = tiles(k, 2 * block)
            total = dy_ref[r, :].astype(WIDE) + dv
            dx1_ref[r, :] = total
            low[r, :] = total.astype(LOW)

        norm_back_stage(x2, vec_ref, F_GAIN, acc, sums, 2 * block, put_x2)
        turn_stage(o_s, at)
        weight_stage(at, low, g_out, bias_rows(sums, [S_OUTB], width))
        back_stage(low, w_out, acc)
        low[...] = acc[...].astype(LOW)
        dz = dh.at[:, : 3 * width]
        space_attend_back(z_s, p_s, low, dz, frames, span)
        turn_stage(a_s, at)
        weight_stage(at, dz, g_in, bias_rows(sums, [S_INB, None, S_INB + 1], width))
        back_stage(dz, w_in, acc)

        def put_x1(k, dv):
            r = tiles(k, 2 * block)
            total = dx1_ref[r, :] + dv
            dx1_ref[r, :] = total
            db_ref[r, :] = total.astype(LOW)

        norm_back_stage(x1, vec_ref, S_GAIN, acc, sums, 2 * block, put_x1)

    token, full = ((rows, width), LOW), ((rows, width), WIDE)
    outs = [token, full, token] + [(w.shape, LOW) for w in (w_in, w_out, w_up, w_down)] + [(vec.shape, WIDE)]
    scratch = [full, full, token, ((rows, 3 * width), LOW), ((heads_all, span, span), LOW), token, token]
    scratch += [((rows, hidden), LOW)] * 3 + [full, ((width + 16, rows), LOW), ((TILE, rows), LOW), token]
    return vmem_call(body, outs, (x, b, dy, vec, w_in, w_out, w_up, w_down), scratch, "space_layer")


def time_backward(block, db, x, a, z, p, o, u, vec, w_in, w_out, w_lin):
    rows, width = x.shape
    frames = rows // block

    def body(db_ref, x_ref, a_ref, z_ref, p_ref, o_ref, u_ref, vec_ref, w_in, w_out, w_lin,
             dt_ref, g_in, g_out, g_lin, sums, low, dz, dk, dv, acc, at):
        sums[...] = jnp.zeros_like(sums)
        turn_stage(u_ref, at)
        weight_stage(at, db_ref, g_lin, bias_rows(sums, [T_LINB], width))
        back_stage(db_ref, w_lin, acc)
        low[...] = acc[...].astype(LOW)
        turn_stage(o_ref, at)
        weight_stage(at, low, g_out, bias_rows(sums, [T_OUTB], width))
        back_stage(low, w_out, acc)
        low[...] = acc[...].astype(LOW)
        time_attend_back(z_ref, p_ref, low, dz, dk, dv, frames, block)
        turn_stage(a_ref, at)
        weight_stage(at, dz, g_in, bias_rows(sums, [T_INB, None, T_INB + 1], width))
        back_stage(dz, w_in, acc)

        def put(k, dv):
            put_rows(dt_ref, k, 2 * block, dv)

        norm_back_stage(x_ref, vec_ref, T_GAIN, acc, sums, 2 * block, put)

    token, full = ((rows, width), LOW), ((rows, width), WIDE)
    outs = [token] + [(w.shape, LOW) for w in (w_in, w_out, w_lin)] + [(vec.shape, WIDE)]
    scratch = [token, ((rows, 3 * width), LOW), full, full, full, ((width + 16, rows), LOW)]
    return vmem_call(body, outs, (db, x, a, z, p, o, u, vec, w_in, w_out, w_lin), scratch, "time_backward")


def stack_rows(terms, groups):
    return tuple(
        (item.reshape((groups, item.shape[0] // groups) + item.shape[1:]) for item in terms)
    )


def fold_rows(received):
    return tuple((jnp.sum(item, axis=0) for item in received))


def remote(source, target, send, recv, device):
    return pltpu.make_async_remote_copy(
        src_ref=source,
        dst_ref=target,
        send_sem=send,
        recv_sem=recv,
        device_id=device,
        device_id_type=MESH,
    )


def place(split):
    nz, ny, nx, nc = split
    clip, frame = lax.axis_index("clip"), lax.axis_index("frame")
    z, y, x, c = clip // ny, clip % ny, frame // nc, frame % nc

    def mesh_at(z, y, x, c):
        return (z * ny + y, x * nc + c)

    row = [mesh_at((z + step) % nz, y, x, c) for step in range(1, nz)]
    beside = (mesh_at(z, y, 1 - x, c), mesh_at(z, 1 - y, x, c), mesh_at(z, y, x, 1 - c))
    return (z, y, x, c), row, beside


def greet(devices):
    barrier = pltpu.get_barrier_semaphore()
    for device in devices:
        pl.semaphore_signal(barrier, inc=1, device_id=device, device_id_type=MESH)
    pl.semaphore_wait(barrier, len(devices))


def inner_split(rows):
    clips, frames = lax.axis_size("clip"), lax.axis_size("frame")
    if frames == 4 and clips % 2 == 0 and clips > 2 and rows % TILE_ROWS == 0:
        return (clips // 2, 2, 2, 2)
    return None


SMALL_ROWS = 16
RING = 6
AHEAD = 2
PIECES = 2
FIRST = 3
TALL = 4
LATE = 2
LATE_RELAY = 1
LATE_SEND = 7
LATE_STEP = 2
OVER_Y = ()
THIRD = 1
TWO = 1
THREE = 1
TB = 2
SB = 1
GB = 0
RB = 1
RD = 1
TN = 1
BK = 1
GT = 1
BL = 1
STAGES = 3
SUB = 4


class Move:
    def __init__(self, make):
        self.make = make
        make().start()

    def wait(self):
        self.make().wait()

    def wait_recv(self):
        self.make().wait_recv()

    def wait_send(self):
        self.make().wait_send()


class Gather:
    def __init__(self, split, where, row, beside, chunks, sems, ahead):
        self.split, self.where, self.row, self.beside = split, where, row, beside
        self.chunks, self.sems = chunks, sems
        self.started, self.first, self.second, self.third, self.core = [], {}, {}, {}, {}
        self.along = {}
        plain = [i for i, item in enumerate(chunks) if item[7] != 2]
        late = [i for i, item in enumerate(chunks) if item[7] == 2]
        self.here, count = set(), len(plain)
        self.events, self.ends = [], set()

        def then(call, i):
            self.events.append(lambda: call(i))

        for i in plain[:ahead]:
            then(self.spread, i)
        for i in late:
            then(self.sideways, i)
        for t in range(count + 3):
            if t < count:
                then(self.sideways, plain[t])
            if t + ahead < count:
                then(self.spread, plain[t + ahead])
            if 0 <= t - 2 < count:
                then(self.finish, plain[t - 2])
            if 0 <= t - 3 < count:
                then(self.receive, plain[t - 3])
            if 0 <= t - 1 < count:
                then(self.relay_x, plain[t - 1])
                then(self.relay_y, plain[t - 1])
            for k, i in enumerate(late):
                if t == LATE_RELAY:
                    then(self.relay_x, i)
                    then(self.relay_y, i)
                if t == LATE_SEND + LATE_STEP * k:
                    then(self.lengthwise, i)
                if t == count + 1:
                    then(self.finish, i)
                if t == count + 2:
                    then(self.receive, i)
            self.ends.add(len(self.events))
        self.next = 0

    def pump(self, times=1):
        for _ in range(times):
            if self.next < len(self.events):
                self.next += 1
                self.events[self.next - 1]()

    def need(self, i):
        while i not in self.here or self.next not in self.ends:
            self.pump()

    def launch(self, make):
        move = Move(make)
        self.started.append(move)
        return move

    def block(self, i, y, x, c, half=None):
        _, full, per, low, count, start, width, way = self.chunks[i]
        first = c * per + low
        if half is not None and width % (2 * LANES) == 0:
            start, width = start + half * (width // 2), width // 2
        elif half is not None:
            first, count = first + half * (count // 2), count // 2
        rows = pl.ds(pl.multiple_of(first, TILE_ROWS), count)
        places = self.where[0] if way == 2 else slice(None)
        return full.at[places, y * self.split[2] + x, rows, pl.ds(start, width)]

    def own(self, i):
        z, y, x, c = self.where
        _, full, per, low, count, start, width, _ = self.chunks[i]
        rows = pl.ds(pl.multiple_of(c * per + low, TILE_ROWS), count)
        return full.at[z, y * self.split[2] + x, rows, pl.ds(start, width)]

    def core_part(self, i, place):
        c = self.where[3]
        _, full, per, low, count, start, width, _ = self.chunks[i]
        rows = pl.ds(pl.multiple_of(c * per + low, TILE_ROWS), count)
        return full.at[place, :, rows, pl.ds(start, width)]

    def mine(self, i):
        shard, _, _, low, count, start, width, _ = self.chunks[i]
        return shard.at[pl.ds(low, count), pl.ds(start, width)]

    def keep(self, i):
        return Move(lambda: pltpu.make_async_copy(self.mine(i), self.own(i), self.sems[6].at[i]))

    def to_row(self, i, source, target):
        send, recv = self.sems[0], self.sems[1]
        return [
            self.launch(
                lambda k=k, device=device: remote(source(), target(), send.at[i, k], recv.at[i, k], device)
            )
            for k, device in enumerate(self.row)
        ]

    def spread(self, i):
        self.first[i] = self.to_row(i, lambda: self.mine(i), lambda: self.own(i))
        self.first[i].append(self.keep(i))

    def side(self, i, k, block, device):
        send, recv = self.sems[2], self.sems[3]
        return self.launch(lambda: remote(block(), block(), send.at[i, k], recv.at[i, k], device))

    def to_twin(self, i, k, block):
        send, recv, twin = self.sems[4], self.sems[5], self.beside[2]
        return self.launch(lambda: remote(block(), block(), send.at[i, k], recv.at[i, k], twin))

    def sideways(self, i):
        _, y, x, c = self.where
        if self.chunks[i][7] == 2:
            self.first[i] = [self.keep(i)]
        for copy in self.first[i][:-1]:
            copy.wait_recv()
        self.first[i][-1].wait()
        block = lambda: self.block(i, y, x, c)
        self.second[i] = [self.side(i, k, block, self.beside[k]) for k in range(2)]
        self.core[i] = [] if self.chunks[i][7] == 2 else [self.to_twin(i, 0, block)]

    def relay_x(self, i):
        _, y, x, c = self.where
        way = self.chunks[i][7]
        self.second[i][0].wait_recv()
        part = None if way == 1 else 0
        self.third[i] = [self.side(i, 2, lambda: self.block(i, y, 1 - x, c, part), self.beside[1])]
        if way != 2:
            self.core[i].append(self.to_twin(i, 1, lambda: self.block(i, y, 1 - x, c)))

    def relay_y(self, i):
        _, y, x, c = self.where
        way = self.chunks[i][7]
        self.second[i][1].wait_recv()
        if way != 1:
            block = lambda: self.block(i, 1 - y, x, c, 1)
            self.third[i].append(self.side(i, 3, block, self.beside[0]))
        if way != 2:
            self.core[i].append(self.to_twin(i, 2, lambda: self.block(i, 1 - y, x, c)))

    def lengthwise(self, i):
        for copy in self.third[i]:
            copy.wait_recv()
        part = lambda: self.core_part(i, self.where[0])
        self.along[i] = self.to_row(i, part, part)

    def finish(self, i):
        _, y, x, c = self.where
        if self.chunks[i][7] == 2:
            for copy in self.along[i]:
                copy.wait_recv()
            self.core[i].append(self.to_twin(i, 3, lambda: self.core_part(i, slice(None))))
            return
        for copy in self.third[i]:
            copy.wait_recv()
        self.core[i].append(self.to_twin(i, 3, lambda: self.block(i, 1 - y, 1 - x, c)))

    def receive(self, i):
        for copy in self.core[i]:
            copy.wait_recv()
        self.here.add(i)

    def end(self):
        for i in range(len(self.chunks)):
            self.need(i)
        for copy in self.started:
            copy.wait_send()


class Totals:
    def __init__(self, split, where, row, beside, count, bufs, sems, put):
        self.split, self.where, self.row, self.beside, self.count = split, where, row, beside, count
        self.staged, self.held, self.low, self.high, self.from_x, self.from_y, self.from_row = bufs
        self.sems, self.put = sems, put
        self.core, self.diagonal, self.aside, self.last = {}, {}, {}, {}
        self.folded = self.crossing = self.crossed = self.joined = self.done = self.swapped = 0
        self.round = []

    def room(self, u):
        while self.folded < u - STAGES + 1:
            self.pump()
        if u >= STAGES:
            self.core[u - STAGES].wait_send()

    def each_row(self, act):
        each(self.split[0], act)

    def swap(self, u):
        c = self.where[3]
        if u >= RING:
            while self.done < u - RING + 1:
                self.pump()
            pl.semaphore_wait(self.sems[6].at[u - RING], len(self.row) + len(self.beside))
        self.core[u] = Move(
            lambda: remote(
                self.staged.at[u % STAGES, :, :, :, 1 - c],
                self.held.at[u % RING],
                self.sems[0].at[u % RING],
                self.sems[1].at[u % RING],
                self.beside[2],
            )
        )
        self.swapped = u + 1

    def side(self, u, k, block, target, device):
        send, recv = self.sems[2], self.sems[3]
        return Move(lambda: remote(block(), target.at[u % RING], send.at[u % RING, k], recv.at[u % RING, k], device))

    def part(self, u, yy, xx, half=None):
        cols = slice(None) if half is None else pl.ds(half * (TILE // 2), TILE // 2)
        return self.held.at[u % RING, :, yy, xx, :, cols]

    def fold_core(self):
        u = self.folded
        _, y, x, c = self.where
        s, q, held = u % RING, u % STAGES, self.held
        self.core[u].wait_recv()

        def fold(yy, xx):
            def act(k):
                held[s, k, yy, xx] = held[s, k, yy, xx] + self.staged[q, k, yy, xx, c]

            self.each_row(act)

        fold(1 - y, 1 - x)
        self.diagonal[u] = [
            self.side(u, 0, lambda: self.part(u, 1 - y, 1 - x, 0), self.low, self.beside[0]),
            self.side(u, 1, lambda: self.part(u, 1 - y, 1 - x, 1), self.high, self.beside[1]),
        ]
        fold(1 - y, x)
        fold(y, 1 - x)
        fold(y, x)
        self.folded = u + 1

    def fold_low(self):
        u = self.crossing
        _, y, x, _ = self.where
        s, held, half = u % RING, self.held, TILE // 2
        self.diagonal[u][0].wait_recv()

        def act_low(k):
            held[s, k, 1 - y, x, :, :half] = held[s, k, 1 - y, x, :, :half] + self.low[s, k]

        self.each_row(act_low)
        self.aside[u] = [self.side(u, 2, lambda: self.part(u, 1 - y, x), self.from_y, self.beside[1])]
        self.crossing = u + 1

    def fold_high(self):
        u = self.crossed
        _, y, x, _ = self.where
        s, held, half = u % RING, self.held, TILE // 2
        self.diagonal[u][1].wait_recv()

        def act_high(k):
            held[s, k, y, 1 - x, :, half:] = held[s, k, y, 1 - x, :, half:] + self.high[s, k]

        self.each_row(act_high)
        self.aside[u].append(
            self.side(u, 3, lambda: self.part(u, y, 1 - x), self.from_x, self.beside[0])
        )
        self.crossed = u + 1

    def fold_side(self):
        u = self.joined
        z, y, x, _ = self.where
        s, held, depth = u % RING, self.held, self.split[0]
        for copy in self.aside[u]:
            copy.wait_recv()

        def act(k):
            total = held[s, k, y, x].astype(WIDE) + self.from_x[s, k].astype(WIDE)
            held[s, k, y, x] = (total + self.from_y[s, k].astype(WIDE)).astype(LOW)

        self.each_row(act)
        self.last[u] = [
            Move(
                lambda k=k, device=device: remote(
                    held.at[s, (z + k + 1) % depth, y, x],
                    self.from_row.at[s, k],
                    self.sems[4].at[u % RING, k],
                    self.sems[5].at[u % RING, k],
                    device,
                )
            )
            for k, device in enumerate(self.row)
        ]
        self.joined = u + 1

    def fold_row(self):
        u = self.done
        z, y, x, _ = self.where
        s = u % RING
        for copy in self.last[u]:
            copy.wait_recv()
        total = self.held[s, z, y, x].astype(WIDE)
        for k in range(self.split[0] - 1):
            total = total + self.from_row[s, k].astype(WIDE)
        self.put(u, total)
        for copy in self.diagonal[u] + self.aside[u] + self.last[u]:
            copy.wait_send()
        if u + RING < self.count:
            for device in self.row + list(self.beside):
                pl.semaphore_signal(self.sems[6].at[u], inc=1, device_id=device, device_id_type=MESH)
        self.done = u + 1

    def pump(self, times=1):
        for _ in range(times):
            if not self.round:
                if self.folded < self.swapped:
                    self.round.append(self.fold_core)
                if self.crossed < self.folded:
                    self.round += [self.fold_low, self.fold_high]
                if self.joined < self.crossed:
                    self.round.append(self.fold_side)
                if self.done < self.joined:
                    self.round.append(self.fold_row)
            if self.round:
                self.round.pop(0)()

    def end(self):
        while self.done < self.count:
            self.pump()
        for u in range(max(self.count - STAGES, 0), self.count):
            self.core[u].wait_send()


def pairs_kernel(split, shape, *refs):
    frames, groups, valid, block = shape
    it = iter(refs)
    take = lambda n: [next(it) for _ in range(n)]
    (x_in, dy_in, small_in), shards = take(3), take(7)
    out_ref, grad_ref = take(2)
    g_t_in, g_t_out, g_t_lin, g_s_in, g_s_out, g_up, g_down, g_small = take(8)
    small_all, full = next(it), take(7)
    xt, a_t, z_t, p_t, o_t, u_t, dy, x1, x2, a_s, z_s, p_s, o_s, a_m, act_g, slope, acc, at, low = take(19)
    b_recv, db_recv, dt_recv, sent, vec, sums, small_v, tile_v = take(8)
    w_a, w_b, w_up, w_down = take(4)
    bufs = take(7)
    ag_sems, rs_sems = take(7), take(7)
    ex_send, ex_recv, ex_own, load_sem, misc = take(5)

    where, row, beside = place(split)
    z, y, x, c = where
    nz, ny, nx, nc = split
    corner = (z * ny + y, (1 - x) * nc + (1 - c))
    greet(row + list(beside) + [corner])
    rows, width = x1.shape
    span = rows // frames
    pair = 2 * block
    chunk = pair
    mine = x * nc + c
    peers = [(beside[0], (1 - x) * nc + c), (beside[2], x * nc + (1 - c)), (corner, (1 - x) * nc + (1 - c))]
    waiting = []

    def cut(ref, index):
        if len(ref.shape) == 3:
            return ref.at[index]
        return ref.at[pl.ds(pl.multiple_of(index * block, TILE_ROWS), block)]

    def exchange(e, source, target, to_places):
        copies = []
        for f in range(frames):
            for k, (device, index) in enumerate(peers):
                src = f * groups + index if to_places else index * frames + f
                dst = mine * frames + f if to_places else f * groups + mine
                copies.append(
                    Move(
                        lambda src=src, dst=dst, k=k, f=f, device=device: remote(
                            cut(source, src), cut(target, dst), ex_send.at[e, k, f], ex_recv.at[e, k, f], device
                        )
                    )
                )
            src = f * groups + mine if to_places else mine * frames + f
            dst = mine * frames + f if to_places else f * groups + mine
            copies.append(
                Move(
                    lambda src=src, dst=dst, f=f: pltpu.make_async_copy(
                        cut(source, src), cut(target, dst), ex_own.at[e, f]
                    )
                )
            )
        return copies

    def arrive(copies):
        for copy in copies:
            copy.wait()

    moved = exchange(0, x_in, xt, True)
    dims = [s.shape for s in shards]
    chunks, ready = [(small_in, small_all, SMALL_ROWS, 0, SMALL_ROWS, 0, LANES, 0)], {}
    for k, (deep, wide) in enumerate(dims):
        tall = TALL if deep > dims[0][0] else 1
        cuts = PIECES if wide > 3 * width else FIRST if k == 0 else THIRD if k == 3 else 1
        for part in range(tall * cuts):
            count, cols = deep // tall, wide // cuts
            top, left = (part * count, 0) if tall > 1 else (0, part * cols)
            way = 2 if tall > 1 and part >= tall - LATE else 1 if k in OVER_Y else 0
            chunks.append((shards[k], full[k], deep, top, count, left, cols, way))
            ready[k, part] = len(chunks) - 1
    ag = Gather(split, where, row, beside, chunks, ag_sems, AHEAD)
    ag.pump(AHEAD)
    loads = {}

    class Load:
        def __init__(self, pairs):
            index = len(loads)
            self.copies = [
                Move(lambda a=a, b=b, k=k: pltpu.make_async_copy(a, b, load_sem.at[index, k]))
                for k, (a, b) in enumerate(pairs)
            ]

        def wait(self):
            for copy in self.copies:
                copy.wait()

    def load(key, source, target):
        if len(source.shape) == 2:
            pairs = [(source, target)]
        else:
            per = source.shape[2]
            pairs = [
                (source.at[:, k], target.at[:, pl.ds(k * per, per)]) for k in range(source.shape[1])
            ]
        loads[key] = Load(pairs)

    def fetch(key, k, target):
        for (which, _), i in ready.items():
            if which == k:
                ag.need(i)
        load(key, full[k], target)

    load("x", x_in, low)
    load("dy", dy_in, dy)
    sums[...] = jnp.zeros_like(sums)
    wb = [w_b.at[:, :, pl.ds(k * width, width)] for k in range(3)]
    wa = w_a
    ag.need(0)
    load("small", small_all, small_v)
    loads["small"].wait()
    devices = nz * ny * nx * nc
    per_row = devices * SMALL_ROWS // (nz * SMALL_ROWS)

    parts, step = {}, width // devices
    lanes = lax.broadcasted_iota(jnp.int32, (SMALL_ROWS, LANES), 1)

    def add(key, value):
        parts[key] = parts[key] + value if key in parts else value

    def put_at(name, tile, column, size):
        block_at, shift = column // LANES, column % LANES
        moved = pltpu.roll(tile, shift, 1) if shift else tile
        if shift + size <= LANES:
            add((name, block_at), moved)
        else:
            add((name, block_at), jnp.where(lanes >= shift, moved, 0.0))
            add((name, block_at + 1), jnp.where(lanes < shift, moved, 0.0))

    for r in range(devices):
        k, s = r // per_row, r % per_row
        tile = small_v[k, s * SMALL_ROWS : (s + 1) * SMALL_ROWS, :].astype(WIDE)
        for name, times in (("a", 1), ("b", 2), ("c", 4)):
            put_at(name, tile, r * step * times, step * times)
    per_line = width // LANES
    for k in range(per_line):
        vec[0:10, k * LANES : (k + 1) * LANES] = parts["a", k][0:10]
    for name, tile_row, top_line in (("b", 10, T_INB), ("b", 11, S_INB), ("c", 12, E_BIAS)):
        for k in range(per_line * (2 if name == "b" else 4)):
            to_line, col = top_line + k // per_line, k % per_line * LANES
            vec[to_line : to_line + 1, col : col + LANES] = parts[name, k][tile_row : tile_row + 1]

    arrive(moved)
    norm_stage(xt, vec, T_GAIN, a_t, chunk)
    fetch("t_in", 0, wa)
    two, three = (lambda: ag.pump(TWO)), (lambda: ag.pump(THREE))
    loads["t_in"].wait()
    inproj_stage(a_t, wa, vec, T_INB, z_t)
    all_frames = frames * groups
    fetch("t_out", 1, wb[0])
    time_attend(z_t, p_t, o_t, all_frames, block, 0, all_frames // 4)
    fetch("t_lin", 2, wb[1])
    time_attend(z_t, p_t, o_t, all_frames, block, all_frames // 4, all_frames // 2)

    def store(ref):
        def act(cols, total):
            if len(ref.shape) == 3:
                ref[:, :, cols] = total.reshape(ref.shape[:2] + (-1,)).astype(LOW)
            else:
                ref[:, cols] = total.astype(LOW)

        return act

    loads["t_out"].wait()
    project_stage(o_t, wb[0], vec, T_OUTB, store(u_t))
    loads["t_lin"].wait()
    project_stage(u_t, wb[1], vec, T_LINB, store(sent))
    moved = exchange(1, sent, b_recv, False)
    fetch("s_in", 3, wa)
    loads["x"].wait()
    arrive(moved)

    def first(k):
        r = tiles(k, chunk)
        x1[r, :] = low[r, :].astype(WIDE) + wide_rows(b_recv, k, chunk)

    each(rows // chunk, first)
    norm_stage(x1, vec, S_GAIN, a_s, chunk)
    loads["s_in"].wait()
    inproj_stage(a_s, wa, vec, S_INB, z_s)
    fetch("s_out", 4, wb[2])
    heads = width // LANES * frames
    space_attend(z_s, p_s, o_s, frames, span, valid, block, 0, heads // 2)
    ag.need(ready[5, 0])
    space_attend(z_s, p_s, o_s, frames, span, valid, block, heads // 2, heads)

    def add_x1(cut, total):
        x2[:, cut] = x1[:, cut] + total

    loads["s_out"].wait()
    project_stage(o_s, wb[2], vec, S_OUTB, add_x1)
    norm_stage(x2, vec, F_GAIN, a_m, chunk)
    for part in range(PIECES):
        half = w_up.shape[2] // PIECES
        cols = pl.ds(part * half, half)
        ag.need(min(ready[5, part] + 1, ready[6, 0]))
        load(f"up{part}", full[5].at[:, :, :, cols], w_up.at[:, :, cols])
        loads[f"up{part}"].wait()
        per = half // TILE
        expand_stage(a_m, w_up, vec, act_g, slope, part * per, (part + 1) * per)
    loads["dy"].wait()

    per = width // TILE
    plan = {}
    order = [(g_up, 4 * per), (g_s_out, per), (g_s_in, 3 * per), (g_t_lin, per), (g_t_out, per), (g_t_in, 3 * per), (g_small, 1)]
    units, sub = per - 1, SUB
    homes = {}
    for out, count in order:
        for k in range(count):
            if sub == SUB:
                units, sub = units + 1, 0
                plan[units] = []
            plan[units].append((out, k))
            homes[id(out), k] = (units, sub)
            sub += 1
    count = units + 1
    step_rows = g_up.shape[0]

    def put(u, total):
        if u < per:
            g_down[:, u * TILE : (u + 1) * TILE] = total
            return
        for b, (out, k) in enumerate(plan[u]):
            out[:, k * TILE : (k + 1) * TILE] = total[b * step_rows : (b + 1) * step_rows]

    rs = Totals(split, where, row, beside, count, bufs, rs_sems, put)
    staged = bufs[0]

    def down(k):
        at[:width, :] = act_g[:, tiles(k, width)].T
        for u in range(per):
            total = dot(at[:width, :], dy[:, u * TILE : (u + 1) * TILE])
            staged[u, k] = total.reshape((ny, nx, nc, -1, TILE)).astype(LOW)

    each(nz, down)
    ones = jnp.ones((16, rows), LOW)
    sums[R_BIAS : R_BIAS + 1, :] = dot(ones, dy[...])[:1]
    for u in range(per):
        rs.swap(u)
    fetch("down", 6, w_down)
    turns = lambda times: (lambda: rs.pump(times))

    def grads(out, dz_ref, table):
        count = out.shape[1] // TILE
        act_bias = bias_rows(sums, table, width)
        k = 0
        while k < count:
            u, b0 = homes[id(out), k]
            n = min(SUB - b0, count - k)
            if b0 == 0:
                rs.room(u)

            def act(i, k=k, u=u, b0=b0, n=n):
                t = k + i
                total = dot(at[...], dz_ref[:, tiles(t)])
                act_bias(t, total[width : width + 1])
                tile_v[...] = total[:width]
                for b in range(n):

                    @pl.when(i == b)
                    def _():
                        low_row = (b0 + b) * step_rows
                        staged[u % STAGES, :, :, :, :, low_row : low_row + step_rows, :] = (
                            tile_v[...].reshape((nz, ny, nx, nc, step_rows, TILE)).astype(LOW)
                        )

            each(n, act, 0, turns(GT), 4)
            k += n
            if b0 + n == SUB:
                rs.swap(u)
                rs.pump(GB)

    loads["down"].wait()
    reduce_back_stage(dy, w_down, slope, slope, turns(RB))

    hidden = act_g.shape[1]
    reduce_stage(act_g, w_down, vec, x2, store(low), turns(RD))
    out_copy = pltpu.make_async_copy(low, out_ref, misc.at[0])
    out_copy.start()
    turn_stage(a_m, at, turns(TN))
    grads(g_up, slope, [E_BIAS + k for k in range(hidden // width)])
    back_stage(slope, w_up, acc, turns(BK))
    out_copy.wait()

    def put_x2(k, dv):
        r = tiles(k, chunk)
        total = dy[r, :].astype(WIDE) + dv
        x2[r, :] = total
        low[r, :] = total.astype(LOW)

    norm_back_stage(x2, vec, F_GAIN, acc, sums, chunk, put_x2)
    load("t_in again", full[0], w_up.at[:, :, pl.ds(0, 3 * width)])
    turn_stage(o_s, at, turns(TN))
    grads(g_s_out, low, [S_OUTB])
    back_stage(low, wb[2], acc)
    rs.pump(BL)
    low[...] = acc[...].astype(LOW)
    dz = slope.at[:, pl.ds(0, 3 * width)]
    space_attend_back(z_s, p_s, low, dz, frames, span, pump=lambda: rs.pump(SB))
    back_stage(dz, wa, acc, turns(BK))

    def put_x1(k, dv):
        r = tiles(k, chunk)
        total = x2[r, :] + dv
        x1[r, :] = total
        put_rows(sent, k, chunk, total)

    norm_back_stage(x1, vec, S_GAIN, acc, sums, chunk, put_x1)
    moved = exchange(2, sent, db_recv, True)
    turn_stage(a_s, at, turns(TN))
    grads(g_s_in, dz, [S_INB, None, S_INB + 1])
    turn_stage(u_t, at, turns(TN))
    arrive(moved)

    def flat(k):
        low[tiles(k, chunk), :] = wide_rows(db_recv, k, chunk).astype(LOW)

    each(rows // chunk, flat)
    grads(g_t_lin, low, [T_LINB])
    back_stage(low, wb[1], acc)
    rs.pump(BL)
    low[...] = acc[...].astype(LOW)
    turn_stage(o_t, at, turns(TN))
    grads(g_t_out, low, [T_OUTB])
    back_stage(low, wb[0], acc)
    rs.pump(BL)
    low[...] = acc[...].astype(LOW)
    time_attend_back(z_t, p_t, low, dz, x2, acc, all_frames, block, lambda: rs.pump(TB))
    loads["t_in again"].wait()
    back_stage(dz, w_up.at[:, :, pl.ds(0, 3 * width)], acc, turns(BK))

    def put_t(k, dv):
        put_rows(sent, k, chunk, dv)

    norm_back_stage(xt, vec, T_GAIN, acc, sums, chunk, put_t)
    moved = exchange(3, sent, dt_recv, False)
    turn_stage(a_t, at, turns(TN))
    grads(g_t_in, dz, [T_INB, None, T_INB + 1])

    u, b0 = homes[id(g_small), 0]
    if b0 == 0:
        rs.room(u)
    low_row = b0 * step_rows
    line = lax.broadcasted_iota(jnp.int32, (step_rows, LANES), 0)
    lanes = lax.broadcasted_iota(jnp.int32, (step_rows, LANES), 1)
    blocks = {}

    def source(name, k):
        if (name, k) not in blocks:
            row, cols = k // per_line, pl.ds(k % per_line * LANES, LANES)
            if name == "a":
                rest = jnp.zeros((step_rows - SMALL_ROWS, LANES), WIDE)
                value = jnp.concatenate([sums[0:SMALL_ROWS, cols], rest], axis=0)
            elif name == "b":
                first, second = sums[T_INB + row : T_INB + row + 1, cols], sums[S_INB + row : S_INB + row + 1, cols]
                value = jnp.where(line == 10, first, second)
            else:
                value = sums[E_BIAS + row : E_BIAS + row + 1, cols] + jnp.zeros((step_rows, LANES), WIDE)
            blocks[name, k] = value
        return blocks[name, k]

    def taken(name, column, size):
        block_at, shift = column // LANES, column % LANES
        value = source(name, block_at)
        if shift == 0:
            return value
        value = pltpu.roll(value, LANES - shift, 1)
        if shift + size > LANES:
            after = pltpu.roll(source(name, block_at + 1), LANES - shift, 1)
            value = jnp.where(lanes < LANES - shift, value, after)
        return value

    blank = jnp.zeros((step_rows, TILE - LANES), WIDE)
    for r in range(devices):
        a, b, d = (
            taken(name, r * step * times, step * times)
            for name, times in (("a", 1), ("b", 2), ("c", 4))
        )
        tile = jnp.where(line < 10, a, jnp.where(line < 12, b, d))
        slot = (r // (ny * nx * nc), r // (nx * nc) % ny, r // nc % nx, r % nc)
        place_at = (u % STAGES,) + slot + (slice(low_row, low_row + step_rows), slice(None))
        staged[place_at] = jnp.concatenate([tile, blank], axis=1).astype(LOW)
    rs.swap(u)
    arrive(moved)

    def last(k):
        r = tiles(k, chunk)
        x1[r, :] = x1[r, :] + wide_rows(dt_recv, k, chunk)

    each(rows // chunk, last)
    grad_copy = pltpu.make_async_copy(x1, grad_ref, misc.at[1])
    grad_copy.start()
    rs.end()
    ag.end()
    grad_copy.wait()


def whole_layer(split, shape, x, dy, small, shards):
    frames, groups, valid, block = shape
    rows, width = x.shape
    nz, ny, nx, nc = split
    low, wide = LOW, WIDE
    hidden = shards[5].shape[1]
    step = shards[0].shape[0]
    shapes = [(item.shape, wide) for item in shards] + [((step, TILE), wide)]
    token, full = ((rows, width), low), ((rows, width), wide)
    gathered = [((nz, ny * nx, nc * SMALL_ROWS, LANES), low)]
    gathered += [((nz, ny * nx, nc * item.shape[0], item.shape[1]), low) for item in shards]
    joined = [((s[0], s[1] * s[2], s[3]), kind) for s, kind in gathered]
    hbm = pl.BlockSpec(memory_space=pl.ANY)
    vmem = pl.BlockSpec(memory_space=pltpu.VMEM)
    outs = [token, full] + shapes + gathered
    out_specs = [hbm, hbm] + [vmem] * len(shapes) + [hbm] * len(gathered)
    span = rows // frames
    three, big = ((rows, 3 * width), low), ((rows, hidden), low)
    cuts = ((frames * groups, block, width), low)
    scratch = [cuts, token, three, ((frames * groups, rows, LANES), low), token, token, token, full, full]
    scratch += [token, three, ((frames * HEADS, span, span), low), token, token, big, big, full]
    scratch += [((width + 16, rows), low), token, cuts, cuts, cuts, cuts, ((24, width), wide), ((24, width), wide)]
    scratch += [joined[0], ((width, TILE), wide)]
    scratch += [joined[1], joined[1], joined[6], joined[7]]
    deep = SUB * step
    scratch += [((STAGES, nz, ny, nx, nc, deep, TILE), low), ((RING, nz, ny, nx, deep, TILE), low)]
    scratch += [((RING, nz, deep, TILE // 2), low)] * 2 + [((RING, nz, deep, TILE), low)] * 2
    scratch += [((RING, nz - 1, deep, TILE), low)]
    sem = pltpu.SemaphoreType.DMA
    chunks = 1 + FIRST + THIRD + 3 + PIECES + TALL
    units = -(-(sum(item.shape[1] for item in shards[:6]) // TILE + 1) // SUB) + width // TILE
    sems = [sem((chunks, nz - 1))] * 2 + [sem((chunks, 4))] * 4 + [sem((chunks,))]
    sems += [sem((RING,))] * 2 + [sem((RING, 4))] * 2 + [sem((RING, nz - 1))] * 2
    sems += [pltpu.SemaphoreType.REGULAR((units,))]
    sems += [sem((4, 3, frames))] * 2 + [sem((4, frames)), sem((12, ny * nx)), sem((2,))]
    result = pl.pallas_call(
        functools.partial(pairs_kernel, split, shape),
        out_shape=[jax.ShapeDtypeStruct(s, kind) for s, kind in outs],
        in_specs=[hbm] * (3 + len(shards)),
        out_specs=out_specs,
        scratch_shapes=[pltpu.VMEM(s, kind) for s, kind in scratch] + sems,
        compiler_params=pltpu.CompilerParams(
            collective_id=0, has_side_effects=True, vmem_limit_bytes=63 << 20
        ),
        name="whole_layer",
    )(x, dy, small, *shards)
    return result[:10]


VECTOR_ROWS = (0, 1, 10, 2, 3, 4, 5, 12, 6, 7, 8, 14, 9)


SMALL_PLACES = {row: (row, 0) for row in range(10)} | {10: (10, 0), 12: (11, 0), 14: (12, 0)}


def pack_small(vectors):
    rows = {SMALL_PLACES[at][0]: item for at, item in zip(VECTOR_ROWS, vectors)}
    line = []
    for k in range(len(rows)):
        line.append(rows[k].reshape((1, -1)))
        line.append(jnp.zeros((1, LANES - rows[k].shape[0]), LOW))
    line.append(jnp.zeros((1, (SMALL_ROWS - len(rows)) * LANES), LOW))
    return jnp.concatenate(line, axis=1).reshape((SMALL_ROWS, LANES))


def hand_out(blocks, tile, widths):
    count = len(blocks)

    def body(*refs):
        ins, tile_ref = refs[:count], refs[count]
        outs, thin = refs[count + 1 : 2 * count + 1], refs[2 * count + 1 : -1]
        sems = refs[-1]
        copies = [pltpu.make_async_copy(a, b, sems.at[k]) for k, (a, b) in enumerate(zip(ins, outs))]
        for copy in copies:
            copy.start()
        for k, (row, width) in enumerate(widths):
            thin[k][...] = tile_ref[row : row + 1, :width]
        for copy in copies:
            copy.wait()

    hbm, vmem = pl.BlockSpec(memory_space=pl.ANY), pl.BlockSpec(memory_space=pltpu.VMEM)
    out = pl.pallas_call(
        body,
        out_shape=[jax.ShapeDtypeStruct(item.shape, WIDE) for item in blocks]
        + [jax.ShapeDtypeStruct((1, width), WIDE) for _, width in widths],
        in_specs=[vmem] * (count + 1),
        out_specs=[hbm] * count + [vmem] * len(widths),
        scratch_shapes=[pltpu.SemaphoreType.DMA((count,))],
        name="hand_out",
    )(*blocks, tile)
    return out[:count], [item.reshape(-1) for item in out[count:]]


def sum_native(terms):
    received = [
        lax.all_to_all(
            item.astype(LOW), "clip", split_axis=0, concat_axis=0, tiled=True
        ).astype(WIDE)
        for item in stack_rows(terms, lax.axis_size("clip"))
    ]
    return [
        lax.psum_scatter(item.astype(LOW), "frame", scatter_dimension=0, tiled=True).astype(WIDE)
        for item in fold_rows(received)
    ]


def on_device(
    video_tokens,
    time_gain,
    time_shift,
    time_inproj,
    time_inbias,
    time_outproj,
    time_outbias,
    time_linear,
    time_linbias,
    space_gain,
    space_shift,
    space_inproj,
    space_inbias,
    space_outproj,
    space_outbias,
    feed_gain,
    feed_shift,
    expand_weight,
    expand_bias,
    reduce_weight,
    reduce_bias,
    cotangent,
):
    split = inner_split(time_gain.shape[0])
    params = [
        time_gain,
        time_shift,
        time_inproj,
        time_inbias,
        time_outproj,
        time_outbias,
        time_linear,
        time_linbias,
        space_gain,
        space_shift,
        space_inproj,
        space_inbias,
        space_outproj,
        space_outbias,
        feed_gain,
        feed_shift,
        expand_weight,
        expand_bias,
        reduce_weight,
        reduce_bias,
    ]
    frames, places, width = video_tokens.shape[1:]
    groups = lax.axis_size("frame")
    valid = places // groups
    block = -(-valid // TILE_ROWS) * TILE_ROWS
    rows = frames * groups * block

    def padded(tokens):
        cut = tokens.reshape((frames, groups, valid, width))
        return jnp.pad(cut, ((0, 0), (0, 0), (0, block - valid), (0, 0)))

    def to_places(tokens):
        return lax.all_to_all(
            tokens.reshape((frames, groups, block, width)),
            "frame",
            split_axis=1,
            concat_axis=0,
            tiled=True,
        ).reshape((rows, width))

    def to_frames(tokens):
        return lax.all_to_all(
            tokens.reshape((frames * groups, 1, block, width)),
            "frame",
            split_axis=0,
            concat_axis=1,
            tiled=True,
        ).reshape((rows, width))

    def trimmed(tokens):
        cut = tokens.reshape((frames, groups, block, width))[:, :, :valid]
        return cut.reshape((1, frames, places, width))

    def weight(item):
        return item.reshape((4, -1, item.shape[1]))

    if split is not None:
        small = pack_small([item for item in params if item.ndim == 1])
        layer_out, input_grad, *sums = whole_layer(
            split,
            (frames, groups, valid, block),
            padded(video_tokens).reshape((rows, width)),
            padded(cotangent).reshape((rows, width)),
            small,
            [item for item in params if item.ndim == 2],
        )
        widths = [
            (SMALL_PLACES[at][0], item.shape[0])
            for at, item in zip(VECTOR_ROWS, [item for item in params if item.ndim == 1])
        ]
        wide, thin = hand_out(sums[:7], sums[7], widths)
        wide, thin = iter(wide), iter(thin)
        summed = [next(wide) if item.ndim == 2 else next(thin) for item in params]
        return (trimmed(layer_out), trimmed(input_grad)) + tuple(summed)

    full = [lax.all_gather(item, ("clip", "frame"), axis=0, tiled=True) for item in params]
    thin = [item for item in full if item.ndim == 1]
    t_in, t_out, t_lin, s_in, s_out, w_up, w_down = [weight(item) for item in full if item.ndim == 2]
    pieces = sorted(zip(VECTOR_ROWS, thin), key=lambda pair: pair[0])
    vec = jnp.concatenate([item.reshape((-1, width)) for _, item in pieces], axis=0)
    vec = jnp.pad(vec, ((0, 24 - vec.shape[0]), (0, 0))).astype(WIDE)
    tokens, d_out = padded(video_tokens), padded(cotangent)
    own = tokens.reshape((rows, width))
    placed = to_places(tokens)
    b_t, a_t, z_t, p_t, o_t, u_t = time_forward(block, placed, vec, t_in, t_out, t_lin)
    layer_out, d_x1, d_b, g_s_in, g_s_out, g_up, g_down, sums_s = space_layer(
        (frames, valid, block),
        own,
        to_frames(b_t),
        d_out.reshape((rows, width)),
        vec,
        s_in,
        s_out,
        w_up,
        w_down,
    )
    d_t, g_t_in, g_t_out, g_t_lin, sums_t = time_backward(
        block, to_places(d_b), placed, a_t, z_t, p_t, o_t, u_t, vec, t_in, t_out, t_lin
    )
    input_grad = d_x1 + to_frames(d_t).astype(WIDE)
    sums = sums_s + sums_t
    wide = iter(
        [item.reshape((-1, width if item is g_down else item.shape[2])) for item in
         (g_t_in, g_t_out, g_t_lin, g_s_in, g_s_out, g_up, g_down)]
    )
    rows_of = iter(VECTOR_ROWS)
    terms = []
    for item in params:
        if item.ndim == 2:
            terms.append(next(wide))
        else:
            at = next(rows_of)
            count = item.shape[0] * lax.axis_size(("clip", "frame")) // width
            terms.append(sums[at : at + count].reshape(-1))
    summed = sum_native(terms)
    return (trimmed(layer_out), trimmed(input_grad)) + tuple(summed)


def solution(mesh):
    return jax.shard_map(
        on_device,
        mesh=mesh,
        in_specs=(
            P("clip", "frame", None, None),
            P(("clip", "frame")),
            P(("clip", "frame")),
            P(("clip", "frame"), None),
            P(("clip", "frame")),
            P(("clip", "frame"), None),
            P(("clip", "frame")),
            P(("clip", "frame"), None),
            P(("clip", "frame")),
            P(("clip", "frame")),
            P(("clip", "frame")),
            P(("clip", "frame"), None),
            P(("clip", "frame")),
            P(("clip", "frame"), None),
            P(("clip", "frame")),
            P(("clip", "frame")),
            P(("clip", "frame")),
            P(("clip", "frame"), None),
            P(("clip", "frame")),
            P(("clip", "frame"), None),
            P(("clip", "frame")),
            P("clip", "frame", None, None),
        ),
        out_specs=(
            P("clip", "frame", None, None),
            P("clip", "frame", None, None),
            P(("clip", "frame")),
            P(("clip", "frame")),
            P(("clip", "frame"), None),
            P(("clip", "frame")),
            P(("clip", "frame"), None),
            P(("clip", "frame")),
            P(("clip", "frame"), None),
            P(("clip", "frame")),
            P(("clip", "frame")),
            P(("clip", "frame")),
            P(("clip", "frame"), None),
            P(("clip", "frame")),
            P(("clip", "frame"), None),
            P(("clip", "frame")),
            P(("clip", "frame")),
            P(("clip", "frame")),
            P(("clip", "frame"), None),
            P(("clip", "frame")),
            P(("clip", "frame"), None),
            P(("clip", "frame")),
        ),
        check_vma=False,
    )
```
